32 devices in a mesh: ctx: 4 (over x, core), fsdp: 8 (over z, y).
Axes of the slice: x: 2, y: 2, z: 4, core: 2. Of those that a mesh axis runs over, the one named last changes fastest.
Arguments:
- tokens_in: bfloat16 [8, 1024, 1600], P('fsdp', 'ctx'), may hold values from -6 to 6
- group_order: int32 [8], replicated, may hold values from 0 to 7, each once
- out_grad: bfloat16 [8, 1024, 1600], P('fsdp', 'ctx'), may hold values from -6 to 6
- w_qkv: bfloat16 [1600, 4800], P('fsdp'), may hold values from -0.15625 to 0.15625
- w_attn_out: bfloat16 [1600, 1600], P('fsdp'), may hold values from -0.625 to 0.625
- b_query: bfloat16 [1600], P('fsdp'), may hold values from -3 to 3
- b_value: bfloat16 [1600], P('fsdp'), may hold values from -3 to 3
- b_attn_out: bfloat16 [1600], P('fsdp'), may hold values from -3 to 3
- w_fc: bfloat16 [1600, 6400], P('fsdp'), may hold values from -0.15625 to 0.15625
- w_proj: bfloat16 [6400, 1600], P('fsdp'), may hold values from -0.078125 to 0.078125
- b_fc: bfloat16 [6400], P('fsdp'), may hold values from -3 to 3
- b_proj: bfloat16 [1600], P('fsdp'), may hold values from -3 to 3
- ln1_gain: bfloat16 [1600], P('fsdp'), may hold values from 0.5 to 1.5
- ln1_bias: bfloat16 [1600], P('fsdp'), may hold values from -2 to 2
- ln2_gain: bfloat16 [1600], P('fsdp'), may hold values from 0.5 to 1.5
- ln2_bias: bfloat16 [1600], P('fsdp'), may hold values from -2 to 2
Outputs:
- tokens_out: bfloat16 [8, 1024, 1600], P('fsdp', 'ctx')
- grad_tokens: float32 [8, 1024, 1600], P('fsdp', 'ctx')
- grad_w_qkv: float32 [1600, 4800], P('fsdp')
- grad_w_attn_out: float32 [1600, 1600], P('fsdp')
- grad_b_query: float32 [1600], P('fsdp')
- grad_b_value: float32 [1600], P('fsdp')
- grad_b_attn_out: float32 [1600], P('fsdp')
- grad_w_fc: float32 [1600, 6400], P('fsdp')
- grad_w_proj: float32 [6400, 1600], P('fsdp')
- grad_b_fc: float32 [6400], P('fsdp')
- grad_b_proj: float32 [1600], P('fsdp')
- grad_ln1_gain: float32 [1600], P('fsdp')
- grad_ln1_bias: float32 [1600], P('fsdp')
- grad_ln2_gain: float32 [1600], P('fsdp')
- grad_ln2_bias: float32 [1600], P('fsdp')
The draws below stay inside these ranges and needn't reach their ends.
Inputs may be any that keep to these rules, and one draw needn't show every extreme that they name: group_order is a permutation: each of the 8 groups of a sequence is stored at exactly one slot.
All inputs are finite; a program needn't handle non-finite values.
Results may differ from the reference program's by a relative error of at most 0.02.
Values may be sent and summed in bfloat16 or wider, within the bound.
No kernel may reach another device: no remote copies, remote signals or barrier semaphores. Data moves between devices by JAX's collectives and lax.ppermute only.
A program may use at most 384 MiB of HBM per device.

```python
from functools import partial
import jax
import jax.numpy as jnp
from jax import lax

D = 1600
H = 25
HD = 64
FF = 6400
GROUP = 128
LEN = 1024
SEQS = 8
N_CTX = 4


def raised(values, own_key, source, target, parts, factor):
    owner, partner = [(jnp.arange(values.shape[position]) // (values.shape[position] // parts)).reshape([-1 if axis == position else 1 for axis in range(values.ndim)]) for position in (source, target)]
    chosen = jax.random.permutation(own_key, parts)[partner]
    strong = (owner == chosen) | (owner == (partner + parts // 2) % parts)
    return jnp.where(strong, factor * values, values)


def block_scale(key, dims, cuts, low, largest):
    factor_of = 1.0
    for dim, blocks in cuts:
        steps = jax.random.uniform(jax.random.fold_in(jax.random.fold_in(key, 6), dim), (blocks,), jnp.float32, low / len(cuts), largest / len(cuts))
        factor_of = factor_of * jnp.repeat(jnp.exp(steps), dims[dim] // blocks).reshape((-1,) + (1,) * (len(dims) - 1 - dim))
    return factor_of


def gaussian(rng, shape, width, limit, split=(), kind=jnp.bfloat16):
    values = width * jax.random.normal(rng, shape, jnp.float32)
    if split:
        values = values * block_scale(rng, shape, split, -0.22, 0.18)
    return jnp.clip(values, -limit, limit).astype(kind)


def bell_draw_with(rng, dims, scale, reach, split, heavy, held_as=jnp.bfloat16):
    entries = scale * jax.random.normal(rng, dims, jnp.float32)
    if split:
        entries = entries * block_scale(rng, dims, split, -0.22, 0.18)
    return jnp.clip(raised(entries, jax.random.fold_in(rng, 3), *heavy), -reach, reach).astype(held_as)


def setup_inputs(seed: int = 0) -> dict:
    keys = jax.random.split(jax.random.key(seed), 17)
    tokens_in = bell_draw_with(keys[0], (SEQS, LEN, D), 1.0, 6.0, ((0, 8), (1, 4)), (0, 2, 8, 2.0))
    group_order = jax.random.permutation(keys[1], 2 * N_CTX).astype(jnp.int32)
    out_grad = gaussian(keys[2], (SEQS, LEN, D), 1.0, 6.0, ((0, 8), (1, 4)))
    w_qkv = gaussian(keys[3], (D, 3 * D), D ** -0.5, 0.15625, ((0, 8),))
    w_attn_out = gaussian(keys[4], (D, D), (D // 16) ** -0.5, 0.625, ((0, 8),))
    b_query = gaussian(keys[5], (D,), 0.5, 3.0, ((0, 8),))
    b_value = gaussian(keys[6], (D,), 0.5, 3.0, ((0, 8),))
    b_attn_out = gaussian(keys[7], (D,), 0.5, 3.0, ((0, 8),))
    w_fc = gaussian(keys[8], (D, FF), D ** -0.5, 0.15625, ((0, 8),))
    w_proj = gaussian(keys[9], (FF, D), FF ** -0.5, 0.078125, ((0, 8),))
    b_fc = gaussian(keys[10], (FF,), 0.5, 3.0, ((0, 8),))
    b_proj = gaussian(keys[11], (D,), 0.5, 3.0, ((0, 8),))
    ln1_gain = jnp.clip(1.0 + 0.1 * jax.random.normal(keys[12], (D,), jnp.float32), 0.5, 1.5).astype(jnp.bfloat16)
    ln1_bias = gaussian(keys[13], (D,), 0.3, 2.0, ((0, 8),))
    ln2_gain = jnp.clip(1.0 + 0.1 * jax.random.normal(keys[14], (D,), jnp.float32), 0.5, 1.5).astype(jnp.bfloat16)
    ln2_bias = gaussian(keys[15], (D,), 0.3, 2.0, ((0, 8),))
    return dict(tokens_in=tokens_in, group_order=group_order, out_grad=out_grad, w_qkv=w_qkv, w_attn_out=w_attn_out, b_query=b_query, b_value=b_value, b_attn_out=b_attn_out, w_fc=w_fc, w_proj=w_proj, b_fc=b_fc, b_proj=b_proj, ln1_gain=ln1_gain, ln1_bias=ln1_bias, ln2_gain=ln2_gain, ln2_bias=ln2_bias)


@jax.custom_vjp
def low(v):
    return lax.optimization_barrier(v.astype(jnp.bfloat16)).astype(jnp.float32)

@jax.custom_vjp
def low_back(v):
    return v

def low_keep(v):
    return (low(v), None)

def low_pass(kept, grad):
    return (grad,)

def back_keep(v):
    return (v, None)

def back_low(kept, grad):
    return (low(grad),)
low.defvjp(low_keep, low_pass)
low_back.defvjp(back_keep, back_low)
norm_eps = 1e-05
exact_mode = lax.Precision.HIGHEST

def matmul(left_op, right_op):
    return jnp.dot(left_op, right_op, precision=exact_mode)

def layer_norm(values, norm_gain, norm_shift):
    centre = values - lax.optimization_barrier(jnp.mean(values, axis=-1, keepdims=True))
    spread = lax.optimization_barrier(jnp.mean(centre * centre, axis=-1, keepdims=True))
    return centre * lax.rsqrt(spread + norm_eps) * norm_gain + norm_shift

def gelu_tanh(values):
    return 0.5 * values * (1.0 + jnp.tanh(0.7978845608028654 * (values + 0.044715 * values * values * values)))

def head_attend(head_parts, positions):
    queries, keys_all, values_all = head_parts
    scores = low_back(matmul(queries, keys_all.T) * HD ** (-0.5))
    allowed = positions[:, None] >= positions[None, :]
    scores = jnp.where(allowed, scores, -1e+30)
    probs_full = jax.nn.softmax(scores, axis=-1)
    return matmul(low(probs_full), values_all)

def to_heads(matrix):
    return matrix.reshape(LEN, H, HD).transpose(1, 0, 2)

def block_layer(tokens, w_qkv, w_attn_out, b_query, b_value, b_attn_out, w_fc, w_proj, b_fc, b_proj, ln1_gain, ln1_bias, ln2_gain, ln2_bias, positions):
    normed = low(layer_norm(tokens, ln1_gain, ln1_bias))
    mixed_all = matmul(normed, w_qkv)
    queries = low_back(low(mixed_all[:, :D] + b_query))
    keys_all = low_back(low(mixed_all[:, D:2 * D]))
    values_all = low_back(low(mixed_all[:, 2 * D:] + b_value))
    attend_fn = jax.checkpoint(partial(head_attend, positions=positions))
    per_head = lax.map(attend_fn, (to_heads(queries), to_heads(keys_all), to_heads(values_all)))
    attended = low_back(low(per_head.transpose(1, 0, 2).reshape(LEN, D)))
    branch = low_back(matmul(attended, w_attn_out) + b_attn_out)
    middle = tokens + branch
    normed_two = low(layer_norm(middle, ln2_gain, ln2_bias))
    before = low_back(matmul(normed_two, w_fc) + b_fc)
    activated = low(gelu_tanh(before))
    branch_two = low_back(matmul(activated, w_proj) + b_proj)
    return middle + branch_two

def reference(tokens_in, group_order, out_grad, w_qkv, w_attn_out, b_query, b_value, b_attn_out, w_fc, w_proj, b_fc, b_proj, ln1_gain, ln1_bias, ln2_gain, ln2_bias):
    places = jnp.arange(LEN, dtype=jnp.int32)
    positions = (group_order[places // GROUP] * GROUP + places % GROUP).astype(jnp.int32)
    params = tuple((weight.astype(jnp.float32) for weight in (w_qkv, w_attn_out, b_query, b_value, b_attn_out, w_fc, w_proj, b_fc, b_proj, ln1_gain, ln1_bias, ln2_gain, ln2_bias)))

    def forward(tokens, *weights):
        return block_layer(tokens, *weights, positions)

    def per_sequence(totals, seq_pair):
        seq_tokens, seq_grad = seq_pair
        result, pullback = jax.vjp(forward, seq_tokens.astype(jnp.float32), *params)
        gradients = pullback(seq_grad.astype(jnp.float32))
        totals = tuple((running + addend for running, addend in zip(totals, gradients[1:])))
        return (totals, (result.astype(jnp.bfloat16), gradients[0]))
    zero_totals = tuple((jnp.zeros(weight.shape, jnp.float32) for weight in params))
    totals, (outputs, input_grads) = lax.scan(per_sequence, zero_totals, (tokens_in, out_grad))
    return (outputs, input_grads, totals[0], totals[1], totals[2], totals[3], totals[4], totals[5], totals[6], totals[7], totals[8], totals[9], totals[10], totals[11], totals[12])
```

```python
import jax
import jax.numpy as jnp
import numpy as np
from jax import lax
from jax.experimental import pallas as pl
from jax.experimental.pallas import tpu as pltpu
from jax.sharding import PartitionSpec as P

H = 25
HD = 64
GROUP = 128
QB = 256
PAIR = 2 * HD
SLOTS = 7
norm_eps = 1e-05
masked_low = -1e30
f32 = jnp.float32
bf16 = jnp.bfloat16


def outer_sum(left_op, right_op):
    return lax.dot_general(
        left_op, right_op, (((0,), (0,)), ((), ())), preferred_element_type=f32
    )


def back_product(left_op, right_op):
    return lax.dot_general(
        left_op, right_op, (((1,), (1,)), ((), ())), preferred_element_type=f32
    )


def product(left_op, right_op):
    return jnp.dot(left_op, right_op, preferred_element_type=f32)


def added(*terms):
    total = terms[0].astype(f32)
    for term in terms[1:]:
        total = total + term.astype(f32)
    return total


def ctx_swap(block, bit):
    return lax.ppermute(block, "ctx", [(i, i ^ bit) for i in range(lax.axis_size("ctx"))])


def gather_ctx(block):
    near = ctx_swap(block, 1)
    far = ctx_swap(block, 2)
    return [block, near, far, ctx_swap(far, 1)]


def scatter_ctx(parts):
    got = ctx_swap(jnp.stack([parts[1], parts[3]]), 1)
    onward = added(parts[2], got[1]).astype(bf16)
    return added(parts[0], got[0], ctx_swap(onward, 2))


def plane_of(count):
    return count // 2, 2


def gather_shards(block):
    count = lax.axis_size("fsdp")
    if count != 8:
        return lax.all_gather(block, "fsdp", axis=0, tiled=False)
    rows, cols = plane_of(count)
    me = lax.axis_index("fsdp")
    row, col = me // cols, me % cols

    def side(value, keep):
        pairs = [(r * 2 + c, r * 2 + 1 - c) for r in range(rows) if keep(r) for c in (0, 1)]
        return lax.ppermute(value, "fsdp", pairs)

    up, down = [block], [block]
    side_up, side_down = [side(block, lambda r: True)], [None]
    for s in range(1, rows):
        up.append(
            lax.ppermute(
                up[-1],
                "fsdp",
                [(r * 2 + c, r * 2 + 2 + c) for r in range(s - 1, rows - 1) for c in (0, 1)],
            )
        )
        down.append(
            lax.ppermute(
                down[-1],
                "fsdp",
                [(r * 2 + 2 + c, r * 2 + c) for r in range(rows - s) for c in (0, 1)],
            )
        )
        side_up.append(side(up[s], lambda r: r >= s))
        side_down.append(side(down[s], lambda r: r < rows - s))
    whole = jnp.zeros((rows, cols) + block.shape, block.dtype)

    def put(whole, value, r, c):
        return lax.dynamic_update_slice(whole, value[None, None], (r, c, 0, 0))

    whole = put(whole, block, row, col)
    whole = put(whole, side_up[0], row, 1 - col)
    for s in range(1, rows):
        whole = put(whole, jnp.where(row >= s, up[s], down[rows - s]), (row - s) % rows, col)
        whole = put(
            whole, jnp.where(row >= s, side_up[s], side_down[rows - s]), (row - s) % rows, 1 - col
        )
    return whole.reshape((count,) + block.shape)


def scatter_shards(blocks):
    count = lax.axis_size("fsdp")
    if count != 8:
        return lax.psum_scatter(blocks, "fsdp", scatter_dimension=0, tiled=False).astype(f32)
    rows, cols = plane_of(count)
    me = lax.axis_index("fsdp")
    row, col = me // cols, me % cols
    grid = blocks.reshape((rows, cols) + blocks.shape[1:])

    def pick(r, c):
        return lax.dynamic_slice(grid, (r, c, 0, 0), (1, 1) + blocks.shape[1:])[0, 0]

    order = [sorted(range(rows), key=lambda t: (-abs(t - r), -t)) for r in range(rows)]
    table = jnp.asarray(np.array(order, np.int32))
    sums = []
    for k in range(rows):
        target = lax.dynamic_index_in_dim(
            lax.dynamic_index_in_dim(table, row, 0, False), k, 0, False
        )
        got = lax.ppermute(pick(target, 1 - col), "fsdp", [(i, i ^ 1) for i in range(count)])
        sums.append(added(got, pick(target, col)))

    def chosen(offset):
        value = None
        for r in range(rows):
            if 0 <= r + offset < rows:
                found = sums[order[r].index(r + offset)]
                value = found if value is None else jnp.where(row == r, found, value)
        return value

    up = down = None
    for s in range(1, rows):
        d = rows - s
        send_up = chosen(d) if up is None else added(chosen(d), up)
        send_down = chosen(-d) if down is None else added(chosen(-d), down)
        up = lax.ppermute(
            send_up.astype(bf16),
            "fsdp",
            [(r * 2 + c, r * 2 + 2 + c) for r in range(s) for c in (0, 1)],
        )
        down = lax.ppermute(
            send_down.astype(bf16),
            "fsdp",
            [(r * 2 + c, r * 2 - 2 + c) for r in range(d, rows) for c in (0, 1)],
        )
    return added(sums[-1], up, down)


def gather_small(vector):
    count = lax.axis_size("fsdp")
    me = lax.axis_index("fsdp")
    held = vector[None]
    bit = 1
    while bit < count:
        got = lax.ppermute(held, "fsdp", [(i, i ^ bit) for i in range(count)])
        low = (me & bit) == 0
        held = jnp.concatenate([jnp.where(low, held, got), jnp.where(low, got, held)], axis=0)
        bit *= 2
    return held


def reduce_small(table):
    count = lax.axis_size("fsdp")
    me = lax.axis_index("fsdp")
    held = table
    bit = count // 2
    while bit:
        halves = held.reshape(2, bit, -1)
        high = (me & bit) != 0
        keep = jnp.where(high, halves[1], halves[0])
        give = jnp.where(high, halves[0], halves[1])
        held = keep + lax.ppermute(give, "fsdp", [(i, i ^ bit) for i in range(count)])
        bit //= 2
    held = held[0]
    held = held + ctx_swap(held, 1)
    return held + ctx_swap(held, 2)


def norm_stats(values):
    centre = values - jnp.mean(values, axis=-1, keepdims=True)
    scale = lax.rsqrt(jnp.mean(centre * centre, axis=-1, keepdims=True) + norm_eps)
    return centre * scale, scale


def norm_back(grad, unit, scale, gain):
    inner = grad * gain
    back = scale * (
        inner
        - jnp.mean(inner, axis=-1, keepdims=True)
        - unit * jnp.mean(inner * unit, axis=-1, keepdims=True)
    )
    return back, jnp.sum(grad * unit, axis=0), jnp.sum(grad, axis=0)


def across(left_op, right_op, left_dim, right_dim):
    return lax.dot_general(
        left_op, right_op, (((left_dim,), (right_dim,)), ((), ())), preferred_element_type=f32
    )


def head_columns(which, last):
    if last:
        return [slice(t * HD, (t + 1) * HD) for t in range(3)]
    return [slice(t * PAIR + which * HD, t * PAIR + (which + 1) * HD) for t in range(3)]


def diagonal_kept():
    shape = (QB, QB)
    return lax.broadcasted_iota(jnp.int32, shape, 0) <= lax.broadcasted_iota(jnp.int32, shape, 1)


def attend_head(which, last, qkv_ref, out_ref, mass_ref):
    at_q, at_k, at_v = head_columns(which, last)
    length = qkv_ref.shape[0]
    queries = qkv_ref[:, at_q] * bf16(HD**-0.5)
    keys = qkv_ref[:, at_k]
    values_t = qkv_ref[:, at_v].T
    kept = diagonal_kept()
    for i in range(length // QB):
        rows = slice(i * QB, (i + 1) * QB)
        mine = queries[rows]
        diag = jnp.where(kept, across(keys[rows], mine, 1, 1), masked_low)
        peak = jnp.max(diag, axis=0, keepdims=True)
        if i:
            rest = across(keys[: i * QB], mine, 1, 1)
            peak = jnp.maximum(peak, jnp.max(rest, axis=0, keepdims=True))
        diag = jnp.exp(diag - peak)
        mass = jnp.sum(diag, axis=0, keepdims=True)
        out = across(values_t[:, rows], diag.astype(bf16), 1, 0)
        if i:
            rest = jnp.exp(rest - peak)
            mass = mass + jnp.sum(rest, axis=0, keepdims=True)
            out = out + across(values_t[:, : i * QB], rest.astype(bf16), 1, 0)
        out = out / mass
        out_ref[rows, which * HD : (which + 1) * HD] = out.T.astype(bf16)
        mass_ref[0, which : which + 1, rows] = peak + jnp.log(mass)


def attend_kernel(qkv_ref, out_ref, mass_ref):
    pair = pl.program_id(0)
    final = pl.num_programs(0) - 1

    @pl.when(pair < final)
    def _():
        for which in range(2):
            attend_head(which, False, qkv_ref, out_ref, mass_ref)

    @pl.when(pair == final)
    def _():
        out_ref[...] = jnp.zeros_like(out_ref)
        mass_ref[...] = jnp.zeros_like(mass_ref)
        attend_head(0, True, qkv_ref, out_ref, mass_ref)


def attend_back_head(which, last, qkv_ref, grad_ref, mass_ref, out_ref, key_acc, value_acc):
    at_q, at_k, at_v = head_columns(which, last)
    length = qkv_ref.shape[0]
    queries = qkv_ref[:, at_q] * bf16(HD**-0.5)
    keys = qkv_ref[:, at_k]
    keys_t = keys.T
    values = qkv_ref[:, at_v]
    grads = grad_ref[:, which * HD : (which + 1) * HD]
    kept = diagonal_kept()
    for i in range(length // QB):
        rows = slice(i * QB, (i + 1) * QB)
        mine = queries[rows]
        grad = grads[rows]
        mass = mass_ref[0, which : which + 1, rows]
        spans = [(rows, True)] + ([(slice(0, i * QB), False)] if i else [])
        probs, both, delta = [], [], None
        for span, diagonal in spans:
            scores = across(keys[span], mine, 1, 1)
            if diagonal:
                scores = jnp.where(kept, scores, masked_low)
            prob = jnp.exp(scores - mass)
            prod = prob * across(values[span], grad, 1, 1)
            part = jnp.sum(prod, axis=0, keepdims=True)
            delta = part if delta is None else delta + part
            probs.append(prob)
            both.append(prod)
        query_t = None
        for (span, diagonal), prob, prod in zip(spans, probs, both):
            grad_scores = (prod - prob * delta).astype(bf16)
            part = across(keys_t[:, span], grad_scores, 1, 0)
            query_t = part if query_t is None else query_t + part
            key_part = across(grad_scores, mine, 1, 0)
            value_part = across(prob.astype(bf16), grad, 1, 0)
            if diagonal:
                key_acc[span, :] = key_part
                value_acc[span, :] = value_part
            else:
                key_acc[span, :] += key_part
                value_acc[span, :] += value_part
        out_ref[rows, at_q] = (query_t * HD**-0.5).T.astype(bf16)
    out_ref[:, at_k] = key_acc[...].astype(bf16)
    out_ref[:, at_v] = value_acc[...].astype(bf16)


def attend_back_kernel(qkv_ref, grad_ref, mass_ref, out_ref, key_acc, value_acc):
    pair = pl.program_id(0)
    final = pl.num_programs(0) - 1
    refs = (qkv_ref, grad_ref, mass_ref, out_ref, key_acc, value_acc)

    @pl.when(pair < final)
    def _():
        for which in range(2):
            attend_back_head(which, False, *refs)

    @pl.when(pair == final)
    def _():
        out_ref[...] = jnp.zeros_like(out_ref)
        attend_back_head(0, True, *refs)


def attend(qkv):
    length = qkv.shape[0]
    pairs = (SLOTS + 1) // 2
    area = SLOTS * length * (length + QB) // 2
    return pl.pallas_call(
        attend_kernel,
        grid=(pairs,),
        in_specs=[pl.BlockSpec((length, 3 * PAIR), lambda p: (0, p))],
        out_specs=[
            pl.BlockSpec((length, PAIR), lambda p: (0, p)),
            pl.BlockSpec((1, 8, length), lambda p: (p, 0, 0)),
        ],
        out_shape=[
            jax.ShapeDtypeStruct((length, pairs * PAIR), bf16),
            jax.ShapeDtypeStruct((pairs, 8, length), f32),
        ],
        compiler_params=pltpu.CompilerParams(vmem_limit_bytes=40 << 20),
        cost_estimate=pl.CostEstimate(
            flops=4 * area * HD * 4, transcendentals=area, bytes_accessed=8 << 20
        ),
        name="attend",
    )(qkv)


def attend_back(qkv, grad, mass):
    length = qkv.shape[0]
    pairs = (SLOTS + 1) // 2
    area = SLOTS * length * (length + QB) // 2
    return pl.pallas_call(
        attend_back_kernel,
        grid=(pairs,),
        in_specs=[
            pl.BlockSpec((length, 3 * PAIR), lambda p: (0, p)),
            pl.BlockSpec((length, PAIR), lambda p: (0, p)),
            pl.BlockSpec((1, 8, length), lambda p: (p, 0, 0)),
        ],
        out_specs=pl.BlockSpec((length, 3 * PAIR), lambda p: (0, p)),
        out_shape=jax.ShapeDtypeStruct((length, pairs * 3 * PAIR), bf16),
        scratch_shapes=[pltpu.VMEM((length, HD), f32), pltpu.VMEM((length, HD), f32)],
        compiler_params=pltpu.CompilerParams(vmem_limit_bytes=40 << 20),
        cost_estimate=pl.CostEstimate(
            flops=10 * area * HD * 4, transcendentals=area, bytes_accessed=12 << 20
        ),
        name="attend_back",
    )(qkv, grad, mass)


def head_slice(matrix, rank, part_count):
    rows = matrix.shape[0]
    width = matrix.shape[1] // part_count
    span = SLOTS * HD
    parts = [
        jnp.pad(matrix[:, t * width : (t + 1) * width], ((0, 0), (0, 4 * span - width)))
        for t in range(part_count)
    ]
    return [lax.dynamic_slice(part, (0, rank * span), (rows, span)) for part in parts]


def to_pairs(parts):
    pieces = []
    for p in range(SLOTS // 2):
        pieces += [part[:, p * PAIR : (p + 1) * PAIR] for part in parts]
    pieces += [part[:, (SLOTS - 1) * HD :] for part in parts]
    return jnp.concatenate(pieces, axis=1)


def from_pairs(matrix):
    whole = SLOTS // 2
    parts = []
    for t in range(3):
        pieces = [
            matrix[:, (3 * p + t) * PAIR : (3 * p + t + 1) * PAIR] for p in range(whole)
        ]
        start = 3 * whole * PAIR + t * HD
        pieces.append(matrix[:, start : start + HD])
        parts.append(jnp.concatenate(pieces, axis=1))
    return parts


def per_device(
    tokens_in,
    group_order,
    out_grad,
    w_qkv,
    w_attn_out,
    b_query,
    b_value,
    b_attn_out,
    w_fc,
    w_proj,
    b_fc,
    b_proj,
    ln1_gain,
    ln1_bias,
    ln2_gain,
    ln2_bias,
):
    ctx = lax.axis_size("ctx")
    shards = lax.axis_size("fsdp")
    rank = lax.axis_index("ctx")
    tokens = tokens_in[0].astype(f32)
    count, width = tokens.shape
    length = count * ctx
    span = SLOTS * HD
    padded = (SLOTS + 1) // 2 * 3 * PAIR
    shard_rows = w_qkv.shape[0]
    unit_rows = w_proj.shape[0] // ctx
    quarter = width // ctx
    peers = [rank ^ k for k in range(ctx)]

    def groups_of(owner):
        return [
            lax.dynamic_index_in_dim(group_order, owner * 2 + j, 0, False) for j in range(2)
        ]

    def sorted_rows(blocks):
        whole = jnp.zeros((length // GROUP, GROUP, blocks[0].shape[1]), blocks[0].dtype)
        for k, block in enumerate(blocks):
            for j, slot in enumerate(groups_of(peers[k])):
                piece = block[j * GROUP : (j + 1) * GROUP][None]
                whole = lax.dynamic_update_slice(whole, piece, (slot, 0, 0))
        return whole.reshape(length, -1)

    def rows_of(matrix, owner):
        return jnp.concatenate(
            [
                lax.dynamic_slice(matrix, (slot * GROUP, 0), (GROUP, matrix.shape[1]))
                for slot in groups_of(owner)
            ],
            axis=0,
        )

    small = gather_small(
        jnp.concatenate(
            [b_query, b_value, b_attn_out, b_proj, ln1_gain, ln1_bias, ln2_gain, ln2_bias, b_fc]
        )
    ).astype(f32)
    vectors = [
        small[:, t * shard_rows : (t + 1) * shard_rows].reshape(-1) for t in range(8)
    ]
    bias_q, bias_v, bias_o, bias_p, gain_one, shift_one, gain_two, shift_two = vectors
    bias_fc = lax.dynamic_index_in_dim(
        small[:, 8 * shard_rows :].reshape(shards, ctx, unit_rows), rank, 1, False
    ).reshape(-1)

    qkv_block = to_pairs(head_slice(w_qkv, rank, 3))
    out_block = lax.dynamic_slice(w_attn_out, (0, rank * quarter), (shard_rows, quarter))
    fc_block = jnp.concatenate(
        [
            lax.dynamic_slice(
                w_fc, (0, (i * ctx + rank) * unit_rows), (shard_rows, unit_rows)
            )
            for i in range(shards)
        ],
        axis=1,
    )
    proj_block = lax.dynamic_slice(w_proj, (rank * unit_rows, 0), (unit_rows, width))

    qkv_weights = gather_shards(qkv_block).reshape(width, 3 * span)
    qkv_weights = jnp.pad(qkv_weights, ((0, 0), (0, padded - 3 * span)))
    out_quarters = gather_ctx(gather_shards(out_block).reshape(width, quarter))
    out_weights = jnp.zeros((ctx, width, quarter), bf16)
    for k in range(ctx):
        out_weights = lax.dynamic_update_slice(out_weights, out_quarters[k][None], (peers[k], 0, 0))
    out_weights = jnp.concatenate([out_weights[k] for k in range(ctx)], axis=1)
    fc_weights = gather_shards(fc_block).reshape(width, shards * unit_rows)
    proj_weights = gather_shards(proj_block).reshape(shards * unit_rows, width)

    unit_one, scale_one = norm_stats(tokens)
    normed_one = (unit_one * gain_one + shift_one).astype(bf16)
    normed_all = sorted_rows(gather_ctx(normed_one))
    none = jnp.zeros((1, span), f32)

    def my_bias(vector):
        return lax.dynamic_slice(
            jnp.pad(vector, (0, ctx * span - width)), (rank * span,), (span,)
        )[None]

    bias_mixed = jnp.pad(
        to_pairs([my_bias(bias_q), none, my_bias(bias_v)]), ((0, 0), (0, padded - 3 * span))
    )
    mixed = (product(normed_all, qkv_weights) + bias_mixed).astype(bf16)
    attended_mine, mass = attend(mixed)
    attended_mine = attended_mine[:, :span]
    attended = jnp.zeros((count, ctx * span), bf16)
    for k in range(ctx):
        got = rows_of(attended_mine, peers[k])
        if k:
            got = ctx_swap(got, k)
        attended = lax.dynamic_update_slice(attended, got, (0, peers[k] * span))
    attended = attended[:, :width]
    middle = tokens + product(attended, out_weights) + bias_o

    unit_two, scale_two = norm_stats(middle)
    normed_two = (unit_two * gain_two + shift_two).astype(bf16)
    normed_two_all = jnp.concatenate(gather_ctx(normed_two), axis=0)
    grad_low = out_grad[0]
    grad_all = jnp.concatenate(gather_ctx(grad_low), axis=0)
    before = product(normed_two_all, fc_weights) + bias_fc
    inner = jnp.tanh(0.7978845608028654 * (before + 0.044715 * before * before * before))
    activated = (0.5 * before * (1.0 + inner)).astype(bf16)
    slope = 0.5 * (1.0 + inner) + 0.5 * before * (1.0 - inner * inner) * (
        0.7978845608028654 * (1.0 + 3 * 0.044715 * before * before)
    )
    branch_two = product(activated, proj_weights).astype(bf16)
    branch_two = scatter_ctx([branch_two[k * count : (k + 1) * count] for k in range(ctx)])
    tokens_out = (middle + branch_two + bias_p).astype(bf16)[None]

    grad_proj = outer_sum(activated, grad_all).astype(bf16)
    shard_proj = scatter_shards(grad_proj.reshape(shards, unit_rows, width))
    before_low = (back_product(grad_all, proj_weights) * slope).astype(bf16)
    grad_fc = outer_sum(normed_two_all, before_low).astype(bf16)
    shard_fc = scatter_shards(grad_fc.reshape(shards, shard_rows, shards * unit_rows))
    grad_two = back_product(before_low, fc_weights).astype(bf16)
    grad_two = scatter_ctx([grad_two[k * count : (k + 1) * count] for k in range(ctx)])
    grad_out = grad_low.astype(f32)
    grad_norm, grad_gain_two, grad_shift_two = norm_back(grad_two, unit_two, scale_two, gain_two)
    grad_middle = grad_out + grad_norm
    middle_low = grad_middle.astype(bf16)

    grad_attended = back_product(middle_low, out_weights).astype(bf16)
    grad_attended = jnp.pad(grad_attended, ((0, 0), (0, ctx * span - width)))
    grad_blocks = []
    for k in range(ctx):
        got = lax.dynamic_slice(grad_attended, (0, peers[k] * span), (count, span))
        grad_blocks.append(ctx_swap(got, k) if k else got)
    grad_heads = jnp.pad(sorted_rows(grad_blocks), ((0, 0), (0, padded // 3 - span)))
    grad_attn_out = outer_sum(attended, middle_low).astype(bf16)
    grad_attn_out = scatter_ctx(
        [
            lax.dynamic_slice(grad_attn_out, (0, peers[k] * quarter), (width, quarter))
            for k in range(ctx)
        ]
    ).astype(bf16)
    shard_attn_out = scatter_shards(grad_attn_out.reshape(shards, shard_rows, quarter))
    grad_mixed = attend_back(mixed, grad_heads, mass)
    grad_qkv = outer_sum(normed_all, grad_mixed)[:, : 3 * span].astype(bf16)
    shard_qkv = scatter_shards(grad_qkv.reshape(shards, shard_rows, 3 * span))
    grad_one = back_product(grad_mixed, qkv_weights).astype(bf16)
    grad_one = scatter_ctx([rows_of(grad_one, peers[k]) for k in range(ctx)])
    grad_norm, grad_gain_one, grad_shift_one = norm_back(grad_one, unit_one, scale_one, gain_one)
    grad_tokens = (grad_middle + grad_norm)[None]

    bias_sums = from_pairs(jnp.sum(grad_mixed.astype(f32), axis=0, keepdims=True))

    def all_heads(vector):
        whole = jnp.zeros((ctx * span,), f32)
        return lax.dynamic_update_slice(whole, vector.reshape(-1), (rank * span,))[:width]

    grad_bias_fc = lax.dynamic_update_slice(
        jnp.zeros((shards, ctx, unit_rows), f32),
        jnp.sum(before_low.astype(f32), axis=0).reshape(shards, 1, unit_rows),
        (0, rank, 0),
    )
    small_grads = [
        all_heads(bias_sums[0]),
        all_heads(bias_sums[2]),
        jnp.sum(middle_low.astype(f32), axis=0),
        jnp.sum(grad_out, axis=0),
        grad_gain_one,
        grad_shift_one,
        grad_gain_two,
        grad_shift_two,
        grad_bias_fc,
    ]
    summed = reduce_small(
        jnp.concatenate([value.reshape(shards, -1) for value in small_grads], axis=1)
    )
    shares = [summed[t * shard_rows : (t + 1) * shard_rows] for t in range(8)]
    share_fc = summed[8 * shard_rows :]

    def all_ranks(share):
        whole = jnp.zeros((ctx,) + share.shape, bf16)
        for k, block in enumerate(gather_ctx(share.astype(bf16))):
            whole = lax.dynamic_update_slice(whole, block[None], (peers[k], 0, 0))
        return whole

    whole_proj = all_ranks(shard_proj).reshape(ctx * unit_rows, width).astype(f32)
    whole_fc = all_ranks(shard_fc)
    whole_fc = jnp.concatenate(
        [
            whole_fc[r][:, i * unit_rows : (i + 1) * unit_rows]
            for i in range(shards)
            for r in range(ctx)
        ],
        axis=1,
    ).astype(f32)
    whole_attn_out = all_ranks(shard_attn_out)
    whole_attn_out = jnp.concatenate([whole_attn_out[r] for r in range(ctx)], axis=1).astype(f32)
    whole_qkv = all_ranks(shard_qkv)
    columns = [from_pairs(whole_qkv[r]) for r in range(ctx)]
    whole_qkv = jnp.concatenate(
        [
            jnp.concatenate([columns[r][t] for r in range(ctx)], axis=1)[:, :width]
            for t in range(3)
        ],
        axis=1,
    ).astype(f32)

    return (
        tokens_out,
        grad_tokens,
        whole_qkv,
        whole_attn_out,
        shares[0],
        shares[1],
        shares[2],
        whole_fc,
        whole_proj,
        share_fc,
        shares[3],
        shares[4],
        shares[5],
        shares[6],
        shares[7],
    )


def solution(mesh):
    placed = (
        P("fsdp", "ctx", None),
        P(),
        P("fsdp", "ctx", None),
        P("fsdp", None),
        P("fsdp", None),
        P("fsdp"),
        P("fsdp"),
        P("fsdp"),
        P("fsdp", None),
        P("fsdp", None),
        P("fsdp"),
        P("fsdp"),
        P("fsdp"),
        P("fsdp"),
        P("fsdp"),
        P("fsdp"),
    )
    return jax.shard_map(
        per_device,
        mesh=mesh,
        in_specs=placed,
        out_specs=(
            P("fsdp", "ctx", None),
            P("fsdp", "ctx", None),
            P("fsdp", None),
            P("fsdp", None),
            P("fsdp"),
            P("fsdp"),
            P("fsdp"),
            P("fsdp", None),
            P("fsdp", None),
            P("fsdp"),
            P("fsdp"),
            P("fsdp"),
            P("fsdp"),
            P("fsdp"),
            P("fsdp"),
        ),
        check_vma=False,
    )
```

```python
import functools

import jax
import jax.numpy as jnp
import numpy as np
from jax import lax
from jax.experimental import pallas as pl
from jax.experimental.layout import Layout, with_layout_constraint
from jax.experimental.pallas import tpu as pltpu
from jax.sharding import PartitionSpec as P

H = 25
HD = 64
GROUP = 128
QB = 256
PAIR = 2 * HD
RANKS = 4
BASE = H // RANKS
SLOTS = H - (RANKS - 1) * BASE
norm_eps = 1e-05
masked_low = -1e30
f32 = jnp.float32
bf16 = jnp.bfloat16


def outer_sum(left_op, right_op):
    return lax.dot_general(
        left_op, right_op, (((0,), (0,)), ((), ())), preferred_element_type=f32
    )


def back_product(left_op, right_op):
    return lax.dot_general(
        left_op, right_op, (((1,), (1,)), ((), ())), preferred_element_type=f32
    )


def product(left_op, right_op):
    return jnp.dot(left_op, right_op, preferred_element_type=f32)


def added(*terms):
    total = terms[0].astype(f32)
    for term in terms[1:]:
        total = total + term.astype(f32)
    return total


def row_major(matrix):
    return with_layout_constraint(matrix, Layout(major_to_minor=tuple(range(matrix.ndim))))


def after(value, *others):
    return lax.optimization_barrier((value,) + others)[0]


PEERS = (0, 2, 1, 3)


def ctx_swap(block, bit):
    pairs = [(i, i ^ bit) for i in range(lax.axis_size("ctx"))]
    return row_major(lax.ppermute(row_major(block), "ctx", pairs))


def gather_ctx(block):
    far = ctx_swap(block, 2)
    near = ctx_swap(block, 1)
    return [block, far, near, ctx_swap(far, 1)]


def scatter_near(matrix):
    half = matrix.shape[0] // 2
    quarter = half // 2
    got = ctx_swap(matrix[half:], 1)
    onward = added(matrix[quarter:half], got[quarter:]).astype(bf16)
    return added(matrix[:quarter], got[:quarter]), onward


def scatter_far(kept, onward):
    return added(kept, ctx_swap(onward, 2))


def exchange_near(matrix):
    half = matrix.shape[0] // 2
    quarter = half // 2
    got = ctx_swap(matrix[half:], 1)
    return matrix[:quarter], got[:quarter], jnp.concatenate([matrix[quarter:half], got[quarter:]])


def exchange_far(mine, near, onward):
    quarter = mine.shape[0]
    got = ctx_swap(onward, 2)
    return [mine, got[:quarter], near, got[quarter:]]


RING = (0, 2, 4, 6, 7, 5, 3, 1)
HALF = len(RING) // 2


def ring_hop(value, step):
    count = len(RING)
    pairs = [(RING[q], RING[(q + step) % count]) for q in range(count)]
    return row_major(lax.ppermute(row_major(value), "fsdp", pairs))


def ring_owners():
    place = jnp.asarray(np.argsort(np.array(RING)).astype(np.int32))
    mine = lax.dynamic_index_in_dim(place, lax.axis_index("fsdp"), 0, False)
    offsets = np.array([0, -1, 1, -2, 2, -3, 3, 4], np.int32)
    return jnp.take(jnp.asarray(np.array(RING, np.int32)), (mine + offsets) % len(RING))


def on_ring():
    return lax.axis_size("fsdp") == len(RING)


def upper_part(rows):
    return rows // 16 * 8


class Gather:
    def __init__(self, block):
        self.block = block
        self.cut = upper_part(block.shape[0])
        self.pieces = [block]
        self.forth = self.back = block

    def hop(self, *gate):
        if not on_ring():
            return
        k = (len(self.pieces) + 1) // 2
        forth, back = self.forth, self.back
        if k == HALF:
            forth, back = forth[: self.cut], back[self.cut :]
        if gate:
            forth, back = after(forth, *gate), after(back, *gate)
        self.forth, self.back = ring_hop(forth, 1), ring_hop(back, -1)
        self.pieces += [self.forth, self.back]

    def arrived(self):
        return (self.forth, self.back) if on_ring() else ()

    def result(self, owners, columns, rows):
        if not on_ring():
            whole = lax.all_gather(self.block, "fsdp", axis=0, tiled=False)
            return [whole[:, top : top + n, c : c + w] for c, w, top, n in columns]
        return collect(self.pieces, owners, self.cut, columns)


def collect_kernel(cut, columns, owners, *refs):
    pieces = refs[: 2 * HALF + 1]
    outs = refs[2 * HALF + 1 : 2 * HALF + 1 + len(columns)]
    sems = refs[-1]
    copies = []
    for out, (start, width, top, rows) in zip(outs, columns):
        for j, piece in enumerate(pieces):
            first = cut if j == 2 * HALF else 0
            low = max(top, first)
            high = min(top + rows, first + piece.shape[0])
            if low < high:
                copies.append(
                    pltpu.make_async_copy(
                        piece.at[pl.ds(low - first, high - low), pl.ds(start, width)],
                        out.at[owners[min(j, 2 * HALF - 1)], pl.ds(low - top, high - low)],
                        sems.at[len(copies)],
                    )
                )
    for copy in copies:
        copy.start()
    for copy in copies:
        copy.wait()


def collect(pieces, owners, cut, columns):
    shapes = [(len(RING), rows, width) for _, width, _, rows in columns]
    return pl.pallas_call(
        functools.partial(collect_kernel, cut, columns),
        grid_spec=pltpu.PrefetchScalarGridSpec(
            num_scalar_prefetch=1,
            grid=(1,),
            in_specs=[pl.BlockSpec(memory_space=pl.ANY)] * len(pieces),
            out_specs=[pl.BlockSpec(shape, lambda i, t: (0, 0, 0)) for shape in shapes],
            scratch_shapes=[pltpu.SemaphoreType.DMA((len(pieces) * len(columns),))],
        ),
        out_shape=[jax.ShapeDtypeStruct(shape, pieces[0].dtype) for shape in shapes],
        compiler_params=pltpu.CompilerParams(vmem_limit_bytes=40 << 20),
        cost_estimate=pl.CostEstimate(flops=0, transcendentals=0, bytes_accessed=12 << 20),
        name="collect",
    )(owners, *pieces)


class Scatter:
    def __init__(self, blocks, owners):
        self.blocks, self.owners = blocks, owners
        self.cut = upper_part(blocks.shape[1])
        self.next = HALF
        self.forth = self.back = None

    def part(self, offset):
        where = {0: 0, 4: 7}.get(offset, 2 * abs(offset) - (offset < 0))
        return lax.dynamic_index_in_dim(self.blocks, self.owners[where], 0, False)

    def hop(self, *gate):
        if not on_ring():
            return
        k, cut = self.next, self.cut
        if k == HALF:
            far = self.part(HALF)
            ahead, behind = far[:cut], far[cut:]
        else:
            ahead, behind = self.part(k), self.part(-k)
            forth, back = self.forth, self.back
            if gate:
                forth, back = after(forth, *gate), after(back, *gate)
            if k == HALF - 1:
                ahead = jnp.concatenate([added(ahead[:cut], forth).astype(bf16), ahead[cut:]])
                behind = jnp.concatenate([behind[:cut], added(behind[cut:], back).astype(bf16)])
            else:
                ahead = added(ahead, forth).astype(bf16)
                behind = added(behind, back).astype(bf16)
        self.next -= 1
        self.forth, self.back = ring_hop(ahead, 1), ring_hop(behind, -1)

    def result(self):
        if not on_ring():
            return lax.psum_scatter(
                self.blocks, "fsdp", scatter_dimension=0, tiled=False
            ).astype(f32)
        return added(self.part(0), self.forth, self.back)


def reduce_small(table):
    count = lax.axis_size("fsdp")
    me = lax.axis_index("fsdp")
    held = table
    bit = count // 2
    while bit:
        halves = held.reshape(2, bit, -1)
        high = (me & bit) != 0
        keep = jnp.where(high, halves[1], halves[0])
        give = jnp.where(high, halves[0], halves[1])
        held = keep + lax.ppermute(give, "fsdp", [(i, i ^ bit) for i in range(count)])
        bit //= 2
    held = held[0]
    held = held + ctx_swap(held, 1)
    return held + ctx_swap(held, 2)


def norm_stats(values):
    centre = values - jnp.mean(values, axis=-1, keepdims=True)
    scale = lax.rsqrt(jnp.mean(centre * centre, axis=-1, keepdims=True) + norm_eps)
    return centre * scale, scale


def norm_back(grad, unit, scale, gain):
    inner = grad * gain
    back = scale * (
        inner
        - jnp.mean(inner, axis=-1, keepdims=True)
        - unit * jnp.mean(inner * unit, axis=-1, keepdims=True)
    )
    return back, jnp.sum(grad * unit, axis=0), jnp.sum(grad, axis=0)


def across(left_op, right_op, left_dim, right_dim):
    return lax.dot_general(
        left_op, right_op, (((left_dim,), (right_dim,)), ((), ())), preferred_element_type=f32
    )


def diagonal_kept():
    shape = (QB, QB)
    return lax.broadcasted_iota(jnp.int32, shape, 0) <= lax.broadcasted_iota(jnp.int32, shape, 1)


def sorted_tile(table, ref, columns):
    groups = ref.shape[0] // GROUP
    return jnp.concatenate(
        [ref[pl.ds(pl.multiple_of(table[g], GROUP), GROUP), columns] for g in range(groups)],
        axis=0,
    )


def put_sorted(table, ref, columns, first, value):
    for j in range(value.shape[0] // GROUP):
        start = pl.multiple_of(table[first + j], GROUP)
        ref[pl.ds(start, GROUP), columns] = value[j * GROUP : (j + 1) * GROUP]


def split_heads(tiles, last):
    if last:
        return [(tiles[0][:, :HD], tiles[0][:, HD:], tiles[1][:, :HD])]
    return [tuple(t[:, w * HD : (w + 1) * HD] for t in tiles) for w in range(2)]


def pair_columns(pair, last):
    if last:
        start = SLOTS // 2 * 3 * PAIR
        return [slice(start, start + PAIR), slice(start + PAIR, start + 2 * PAIR)]
    return [pl.ds(pl.multiple_of(pair * 3 * PAIR + t * PAIR, PAIR), PAIR) for t in range(3)]


def attend_pair(pair, last, table, qkv_ref, out_ref, mass_ref):
    tiles = [sorted_tile(table, qkv_ref, c) for c in pair_columns(pair, last)]
    heads = split_heads(tiles, last)
    length = qkv_ref.shape[0]
    kept = diagonal_kept()
    ready = [(q * bf16(HD**-0.5), k, v.T) for q, k, v in heads]
    for i in range(length // QB):
        rows = slice(i * QB, (i + 1) * QB)
        outs = []
        for w, (queries, keys, values_t) in enumerate(ready):
            mine = queries[rows]
            diag = jnp.where(kept, across(keys[rows], mine, 1, 1), masked_low)
            peak = jnp.max(diag, axis=0, keepdims=True)
            if i:
                rest = across(keys[: i * QB], mine, 1, 1)
                peak = jnp.maximum(peak, jnp.max(rest, axis=0, keepdims=True))
            diag = jnp.exp(diag - peak)
            mass = jnp.sum(diag, axis=0, keepdims=True)
            out = across(values_t[:, rows], diag.astype(bf16), 1, 0)
            if i:
                rest = jnp.exp(rest - peak)
                mass = mass + jnp.sum(rest, axis=0, keepdims=True)
                out = out + across(values_t[:, : i * QB], rest.astype(bf16), 1, 0)
            outs.append(out / mass)
            mass_ref[0, w : w + 1, rows] = peak + jnp.log(mass)
        if last:
            outs.append(jnp.zeros_like(outs[0]))
        tile = jnp.concatenate(outs, axis=0).T.astype(bf16)
        put_sorted(table, out_ref, slice(None), 2 * i, tile)


def attend_kernel(table, qkv_ref, out_ref, mass_ref):
    pair = pl.program_id(0)
    final = pl.num_programs(0) - 1

    @pl.when(pair < final)
    def _():
        attend_pair(pair, False, table, qkv_ref, out_ref, mass_ref)

    @pl.when(pair == final)
    def _():
        mass_ref[...] = jnp.zeros_like(mass_ref)

        @pl.when(table[table.shape[0] - 1] == 0)
        def _():
            out_ref[...] = jnp.zeros_like(out_ref)

        @pl.when(table[table.shape[0] - 1] != 0)
        def _():
            attend_pair(pair, True, table, qkv_ref, out_ref, mass_ref)


def attend_back_pair(pair, last, table, qkv_ref, grad_ref, mass_ref, out_ref, acc):
    places = pair_columns(pair, last)
    heads = split_heads([sorted_tile(table, qkv_ref, c) for c in places], last)
    grads = sorted_tile(table, grad_ref, slice(None))
    length = qkv_ref.shape[0]
    kept = diagonal_kept()
    ready = [
        (q * bf16(HD**-0.5), k, k.T, v, grads[:, w * HD : (w + 1) * HD])
        for w, (q, k, v) in enumerate(heads)
    ]
    for i in range(length // QB):
        rows = slice(i * QB, (i + 1) * QB)
        query_tiles = []
        for w, (queries, keys, keys_t, values, grads_w) in enumerate(ready):
            mine = queries[rows]
            grad = grads_w[rows]
            mass = mass_ref[0, w : w + 1, rows]
            spans = [(rows, True)] + ([(slice(0, i * QB), False)] if i else [])
            probs, both, delta = [], [], None
            for span, diagonal in spans:
                scores = across(keys[span], mine, 1, 1)
                if diagonal:
                    scores = jnp.where(kept, scores, masked_low)
                prob = jnp.exp(scores - mass)
                prod = prob * across(values[span], grad, 1, 1)
                part = jnp.sum(prod, axis=0, keepdims=True)
                delta = part if delta is None else delta + part
                probs.append(prob)
                both.append(prod)
            query_t = None
            for (span, diagonal), prob, prod in zip(spans, probs, both):
                grad_scores = (prod - prob * delta).astype(bf16)
                part = across(keys_t[:, span], grad_scores, 1, 0)
                query_t = part if query_t is None else query_t + part
                key_part = across(grad_scores, mine, 1, 0)
                value_part = across(prob.astype(bf16), grad, 1, 0)
                if diagonal:
                    acc[2 * w, span, :] = key_part
                    acc[2 * w + 1, span, :] = value_part
                else:
                    acc[2 * w, span, :] += key_part
                    acc[2 * w + 1, span, :] += value_part
            query_tiles.append(query_t * HD**-0.5)
        if last:
            query_tiles.append(jnp.zeros_like(query_tiles[0]))
        tile = jnp.concatenate(query_tiles, axis=0).T
        if last:
            tile = jnp.concatenate([tile[:, :HD], jnp.zeros_like(tile[:, HD:])], axis=1)
        put_sorted(table, out_ref, places[0], 2 * i, tile.astype(bf16))
    if last:
        old = sorted_tile(table, out_ref, places[0])
        tile = jnp.concatenate([old[:, :HD], acc[0].astype(bf16)], axis=1)
        put_sorted(table, out_ref, places[0], 0, tile)
        tile = jnp.concatenate([acc[1].astype(bf16), jnp.zeros((length, HD), bf16)], axis=1)
        put_sorted(table, out_ref, places[1], 0, tile)
    else:
        for t in range(2):
            tile = jnp.concatenate([acc[t].astype(bf16), acc[2 + t].astype(bf16)], axis=1)
            put_sorted(table, out_ref, places[1 + t], 0, tile)


def attend_back_kernel(table, qkv_ref, grad_ref, mass_ref, out_ref, acc):
    pair = pl.program_id(0)
    final = pl.num_programs(0) - 1
    refs = (table, qkv_ref, grad_ref, mass_ref, out_ref, acc)

    @pl.when(pair < final)
    def _():
        attend_back_pair(pair, False, *refs)

    @pl.when(pair == final)
    def _():
        @pl.when(table[table.shape[0] - 1] == 0)
        def _():
            for columns in pair_columns(pair, True):
                out_ref[:, columns] = jnp.zeros((out_ref.shape[0], PAIR), bf16)

        @pl.when(table[table.shape[0] - 1] != 0)
        def _():
            attend_back_pair(pair, True, *refs)


def attend(table, qkv):
    length, columns = qkv.shape
    pairs = (SLOTS + 1) // 2
    area = SLOTS * length * (length + QB) // 2
    return pl.pallas_call(
        attend_kernel,
        grid_spec=pltpu.PrefetchScalarGridSpec(
            num_scalar_prefetch=1,
            grid=(pairs,),
            in_specs=[pl.BlockSpec((length, columns), lambda p, t: (0, 0))],
            out_specs=[
                pl.BlockSpec((length, PAIR), lambda p, t: (0, p)),
                pl.BlockSpec((1, 8, length), lambda p, t: (p, 0, 0)),
            ],
        ),
        out_shape=[
            jax.ShapeDtypeStruct((length, pairs * PAIR), bf16),
            jax.ShapeDtypeStruct((pairs, 8, length), f32),
        ],
        compiler_params=pltpu.CompilerParams(vmem_limit_bytes=40 << 20),
        cost_estimate=pl.CostEstimate(
            flops=4 * area * HD * 4, transcendentals=area, bytes_accessed=8 << 20
        ),
        name="attend",
    )(table, qkv)


def attend_back(table, qkv, grad, mass):
    length, columns = qkv.shape
    pairs = (SLOTS + 1) // 2
    area = SLOTS * length * (length + QB) // 2
    return pl.pallas_call(
        attend_back_kernel,
        grid_spec=pltpu.PrefetchScalarGridSpec(
            num_scalar_prefetch=1,
            grid=(pairs,),
            in_specs=[
                pl.BlockSpec((length, columns), lambda p, t: (0, 0)),
                pl.BlockSpec((length, PAIR), lambda p, t: (0, p)),
                pl.BlockSpec((1, 8, length), lambda p, t: (p, 0, 0)),
            ],
            out_specs=pl.BlockSpec((length, columns), lambda p, t: (0, 0)),
            scratch_shapes=[pltpu.VMEM((4, length, HD), f32)],
        ),
        out_shape=jax.ShapeDtypeStruct((length, columns), bf16),
        compiler_params=pltpu.CompilerParams(vmem_limit_bytes=40 << 20),
        cost_estimate=pl.CostEstimate(
            flops=10 * area * HD * 4, transcendentals=area, bytes_accessed=12 << 20
        ),
        name="attend_back",
    )(table, qkv, grad, mass)


def head_slice(matrix, rank, part_count):
    width = matrix.shape[1] // part_count
    return [
        lax.dynamic_slice(
            matrix, (0, t * width + rank * BASE * HD), (matrix.shape[0], SLOTS * HD)
        )
        for t in range(part_count)
    ]


def to_pairs(parts):
    pieces = []
    for p in range(SLOTS // 2):
        pieces += [part[:, p * PAIR : (p + 1) * PAIR] for part in parts]
    pieces += [part[:, (SLOTS - 1) * HD :] for part in parts]
    pieces.append(jnp.zeros((parts[0].shape[0], HD), parts[0].dtype))
    return jnp.concatenate(pieces, axis=1)


def from_pairs(matrix, part, last):
    pieces = [
        matrix[:, (3 * p + part) * PAIR : (3 * p + part + 1) * PAIR] for p in range(SLOTS // 2)
    ]
    if last:
        start = 3 * (SLOTS // 2) * PAIR + part * HD
        pieces.append(matrix[:, start : start + HD])
    return pieces


def per_device(
    tokens_in,
    group_order,
    out_grad,
    w_qkv,
    w_attn_out,
    b_query,
    b_value,
    b_attn_out,
    w_fc,
    w_proj,
    b_fc,
    b_proj,
    ln1_gain,
    ln1_bias,
    ln2_gain,
    ln2_bias,
):
    ctx = lax.axis_size("ctx")
    shards = lax.axis_size("fsdp")
    rank = lax.axis_index("ctx")
    tokens = tokens_in[0].astype(f32)
    count, width = tokens.shape
    span = SLOTS * HD
    step = BASE * HD
    mixed_width = (3 * span + PAIR - 1) // PAIR * PAIR
    attn_width = mixed_width + span
    shard_rows = w_qkv.shape[0]
    unit_rows = w_proj.shape[0] // ctx
    peers = [rank ^ bit for bit in PEERS]
    owners = ring_owners() if on_ring() else None

    def by_rank(blocks):
        whole = jnp.zeros((ctx,) + blocks[0].shape, blocks[0].dtype)
        for peer, block in zip(peers, blocks):
            whole = lax.dynamic_update_slice(whole, block[None], (peer,) + (0,) * block.ndim)
        return row_major(whole)

    def columns_of(blocks):
        return jnp.concatenate(
            [blocks[r][:, :step] for r in range(ctx - 1)] + [blocks[ctx - 1]], axis=1
        )

    def windows(matrix):
        return jnp.concatenate(
            [
                row_major(lax.dynamic_slice(matrix, (0, peer * step), (matrix.shape[0], span)))
                for peer in peers
            ]
        )

    slots = jnp.argsort(group_order).astype(jnp.int32)
    place = jnp.take(jnp.asarray(np.argsort(np.array(PEERS)).astype(np.int32)), (slots // 2) ^ rank)
    slot_rows = (place * 2 + slots % 2) * GROUP
    table = jnp.concatenate([slot_rows, (rank == ctx - 1).astype(jnp.int32)[None]])

    vectors = jnp.concatenate(
        [b_query, b_value, b_attn_out, b_proj, ln1_gain, ln1_bias, ln2_gain, ln2_bias, b_fc]
    )
    vector_rows = (vectors.shape[0] + attn_width * 8 - 1) // (attn_width * 8) * 8
    vector_block = jnp.pad(vectors, (0, vector_rows * attn_width - vectors.shape[0]))
    attn_block = jnp.concatenate(
        [
            to_pairs(head_slice(w_qkv, rank, 3)),
            lax.dynamic_slice(w_attn_out, (0, rank * step), (shard_rows, span)),
        ],
        axis=1,
    )
    attn_block = jnp.concatenate([attn_block, vector_block.reshape(vector_rows, attn_width)])
    fc_block = jnp.concatenate(
        [
            lax.dynamic_slice(
                w_fc, (0, (i * ctx + rank) * unit_rows), (shard_rows, unit_rows)
            )
            for i in range(shards)
        ],
        axis=1,
    )
    proj_block = lax.dynamic_slice(w_proj, (rank * unit_rows, 0), (unit_rows, width))
    attn_gather = Gather(attn_block)
    attn_gather.hop()
    tokens_all = row_major(jnp.concatenate(gather_ctx(tokens_in[0])))
    attn_gather.hop()
    attn_gather.hop()
    fc_gather = Gather(after(fc_block, *attn_gather.arrived()))
    proj_gather = Gather(after(proj_block, *attn_gather.arrived()))
    attn_gather.hop()
    grad_all = row_major(
        jnp.concatenate(gather_ctx(after(out_grad[0], *attn_gather.arrived())))
    )
    for _ in range(HALF):
        fc_gather.hop()
        proj_gather.hop()

    qkv_weights, out_columns, small = attn_gather.result(
        owners,
        (
            (0, mixed_width, 0, shard_rows),
            (mixed_width, span, 0, shard_rows),
            (0, attn_width, shard_rows, vector_rows),
        ),
        None,
    )
    qkv_weights = qkv_weights.reshape(width, mixed_width)
    small = small.reshape(shards, -1).astype(f32)
    bias_q, bias_v, bias_o, bias_p, gain_one, shift_one, gain_two, shift_two = [
        small[:, t * shard_rows : (t + 1) * shard_rows].reshape(-1) for t in range(8)
    ]
    units = ctx * unit_rows
    bias_fc = lax.dynamic_index_in_dim(
        small[:, 8 * shard_rows : 8 * shard_rows + units].reshape(shards, ctx, unit_rows),
        rank,
        1,
        False,
    ).reshape(-1)

    normed_all = row_major(
        (norm_stats(tokens_all.astype(f32))[0] * gain_one + shift_one).astype(bf16)
    )

    def my_bias(vector):
        return lax.dynamic_slice(vector, (rank * step,), (span,))[None]

    bias_mixed = to_pairs([my_bias(bias_q), jnp.zeros((1, span), f32), my_bias(bias_v)])
    mixed = row_major((product(normed_all, qkv_weights) + bias_mixed).astype(bf16))
    attended_mine, mass = attend(table, mixed)
    out_windows = by_rank(gather_ctx(out_columns.reshape(width, span)))
    out_weights = row_major(columns_of(out_windows))
    attended = exchange_far(*exchange_near(row_major(attended_mine[:, :span])))
    attended = row_major(columns_of(by_rank(attended)))
    middle = tokens + product(attended, out_weights) + bias_o

    unit_two, scale_two = norm_stats(middle)
    normed_two = row_major((unit_two * gain_two + shift_two).astype(bf16))
    normed_two_all = row_major(jnp.concatenate(gather_ctx(normed_two)))
    (fc_weights,) = fc_gather.result(owners, ((0, shards * unit_rows, 0, shard_rows),), None)
    (proj_weights,) = proj_gather.result(owners, ((0, width, 0, unit_rows),), None)
    fc_weights = fc_weights.reshape(width, -1)
    proj_weights = proj_weights.reshape(-1, width)
    before = product(normed_two_all, fc_weights) + bias_fc
    inner = jnp.tanh(0.7978845608028654 * (before + 0.044715 * before * before * before))
    activated = row_major((0.5 * before * (1.0 + inner)).astype(bf16))
    slope = 0.5 * (1.0 + inner) + 0.5 * before * (1.0 - inner * inner) * (
        0.7978845608028654 * (1.0 + 3 * 0.044715 * before * before)
    )

    grad_proj = row_major(outer_sum(activated, grad_all).astype(bf16))
    proj_scatter = Scatter(grad_proj.reshape(shards, unit_rows, width), owners)
    proj_scatter.hop()
    before_low = row_major(
        (back_product(after(grad_all, grad_proj), proj_weights) * slope).astype(bf16)
    )
    grad_two = row_major(back_product(before_low, fc_weights).astype(bf16))
    proj_scatter.hop()
    kept_two, onward_two = scatter_near(grad_two)
    grad_fc = row_major(outer_sum(normed_two_all, after(before_low, grad_two)).astype(bf16))
    fc_scatter = Scatter(grad_fc.reshape(shards, shard_rows, shards * unit_rows), owners)
    fc_scatter.hop()
    proj_scatter.hop(onward_two)
    fc_scatter.hop(onward_two)
    grad_two = scatter_far(kept_two, onward_two)
    grad_out = out_grad[0].astype(f32)
    grad_norm, grad_gain_two, grad_shift_two = norm_back(grad_two, unit_two, scale_two, gain_two)
    grad_middle = grad_out + grad_norm
    middle_low = row_major(grad_middle.astype(bf16))
    proj_scatter.hop(middle_low)
    fc_scatter.hop(middle_low)

    grad_attended = row_major(back_product(middle_low, out_weights).astype(bf16))
    heads_near = exchange_near(windows(grad_attended))
    grad_heads = jnp.concatenate(exchange_far(*heads_near))
    grad_heads = jnp.pad(grad_heads, ((0, 0), (0, PAIR - span % PAIR)))
    grad_mixed = attend_back(table, mixed, grad_heads, mass)
    fc_scatter.hop(grad_heads)
    grad_qkv = row_major(outer_sum(normed_all, grad_mixed).astype(bf16))
    qkv_scatter = Scatter(grad_qkv.reshape(shards, shard_rows, mixed_width), owners)
    qkv_scatter.hop()
    grad_one = row_major(
        back_product(after(grad_mixed, grad_qkv), qkv_weights).astype(bf16)
    )
    kept_one, onward_one = scatter_near(grad_one)
    qkv_scatter.hop()
    grad_attn_out = row_major(
        outer_sum(attended, after(middle_low, onward_one)).astype(bf16)
    )
    kept_out, onward_out = scatter_near(windows(grad_attn_out))
    qkv_scatter.hop()
    grad_one = scatter_far(kept_one, onward_one)
    grad_attn_out = row_major(scatter_far(kept_out, onward_out).astype(bf16))
    out_scatter = Scatter(grad_attn_out.reshape(shards, shard_rows, span), owners)
    out_scatter.hop()
    qkv_scatter.hop()
    out_scatter.hop()
    out_scatter.hop()
    out_scatter.hop()

    unit_one, scale_one = norm_stats(tokens)
    grad_norm, grad_gain_one, grad_shift_one = norm_back(grad_one, unit_one, scale_one, gain_one)
    grad_tokens = (grad_middle + grad_norm)[None]

    branch_two = row_major(product(activated, after(proj_weights, grad_qkv)).astype(bf16))
    branch_two = scatter_far(*scatter_near(branch_two))
    tokens_out = (middle + branch_two + bias_p).astype(bf16)[None]

    bias_sums = jnp.sum(grad_mixed.astype(f32), axis=0, keepdims=True)

    def all_heads(part):
        mine = jnp.concatenate(from_pairs(bias_sums, part, True), axis=1)
        return lax.dynamic_update_slice(jnp.zeros((1, width), f32), mine, (0, rank * step))

    grad_bias_fc = lax.dynamic_update_slice(
        jnp.zeros((shards, ctx, unit_rows), f32),
        jnp.sum(before_low.astype(f32), axis=0).reshape(shards, 1, unit_rows),
        (0, rank, 0),
    )
    small_grads = [
        all_heads(0),
        all_heads(2),
        jnp.sum(middle_low.astype(f32), axis=0),
        jnp.sum(grad_out, axis=0),
        grad_gain_one,
        grad_shift_one,
        grad_gain_two,
        grad_shift_two,
        grad_bias_fc,
    ]
    summed = reduce_small(
        jnp.concatenate([value.reshape(shards, -1) for value in small_grads], axis=1)
    )
    shares = [summed[t * shard_rows : (t + 1) * shard_rows] for t in range(8)]
    share_fc = summed[8 * shard_rows :]

    shard_ff = jnp.stack([fc_scatter.result(), proj_scatter.result()]).astype(bf16)
    whole_ff = gather_ctx(after(shard_ff, grad_qkv))
    whole_proj = by_rank([g[1] for g in whole_ff]).reshape(ctx * unit_rows, width).astype(f32)
    whole_fc = by_rank([g[0] for g in whole_ff])
    whole_fc = jnp.concatenate(
        [
            whole_fc[r][:, i * unit_rows : (i + 1) * unit_rows]
            for i in range(shards)
            for r in range(ctx)
        ],
        axis=1,
    ).astype(f32)
    shard_attn = jnp.concatenate([qkv_scatter.result(), out_scatter.result()], axis=1)
    whole_attn = by_rank(gather_ctx(shard_attn.astype(bf16)))
    whole_attn_out = columns_of(whole_attn[:, :, mixed_width:]).astype(f32)
    whole_qkv = jnp.concatenate(
        [
            piece
            for t in range(3)
            for r in range(ctx)
            for piece in from_pairs(whole_attn[r], t, r == ctx - 1)
        ],
        axis=1,
    ).astype(f32)

    return (
        tokens_out,
        grad_tokens,
        whole_qkv,
        whole_attn_out,
        shares[0],
        shares[1],
        shares[2],
        whole_fc,
        whole_proj,
        share_fc,
        shares[3],
        shares[4],
        shares[5],
        shares[6],
        shares[7],
    )


def solution(mesh):
    placed = (
        P("fsdp", "ctx", None),
        P(),
        P("fsdp", "ctx", None),
        P("fsdp", None),
        P("fsdp", None),
        P("fsdp"),
        P("fsdp"),
        P("fsdp"),
        P("fsdp", None),
        P("fsdp", None),
        P("fsdp"),
        P("fsdp"),
        P("fsdp"),
        P("fsdp"),
        P("fsdp"),
        P("fsdp"),
    )
    return jax.shard_map(
        per_device,
        mesh=mesh,
        in_specs=placed,
        out_specs=(
            P("fsdp", "ctx", None),
            P("fsdp", "ctx", None),
            P("fsdp", None),
            P("fsdp", None),
            P("fsdp"),
            P("fsdp"),
            P("fsdp"),
            P("fsdp", None),
            P("fsdp", None),
            P("fsdp"),
            P("fsdp"),
            P("fsdp"),
            P("fsdp"),
            P("fsdp"),
            P("fsdp"),
        ),
        check_vma=False,
    )
```

```python
import functools

import jax
import jax.numpy as jnp
import numpy as np
from jax import lax
from jax.experimental import pallas as pl
from jax.experimental.layout import Layout, with_layout_constraint
from jax.experimental.pallas import tpu as pltpu
from jax.sharding import PartitionSpec as P

H = 25
HD = 64
GROUP = 128
QB = 256
PAIR = 2 * HD
RANKS = 4
BASE = H // RANKS
SLOTS = H - (RANKS - 1) * BASE
norm_eps = 1e-05
masked_low = -1e30
LIGHT = pl.CostEstimate(flops=1 << 20, transcendentals=0, bytes_accessed=1 << 16)
VMEM_LIMIT = 56 << 20
f32 = jnp.float32
bf16 = jnp.bfloat16


def outer_sum(left_op, right_op):
    return lax.dot_general(
        left_op, right_op, (((0,), (0,)), ((), ())), preferred_element_type=f32
    )


def back_product(left_op, right_op):
    return lax.dot_general(
        left_op, right_op, (((1,), (1,)), ((), ())), preferred_element_type=f32
    )


def product(left_op, right_op):
    return jnp.dot(left_op, right_op, preferred_element_type=f32)


def added(*terms):
    total = terms[0].astype(f32)
    for term in terms[1:]:
        total = total + term.astype(f32)
    return total


def row_major(matrix):
    return with_layout_constraint(matrix, Layout(major_to_minor=tuple(range(matrix.ndim))))


def after(value, *others):
    return lax.optimization_barrier((value,) + others)[0]


PEERS = (0, 2, 1, 3)


def tiled(block):
    if block.ndim != 2 or block.shape[0] % 8:
        return block
    return block.reshape(-1, 8, block.shape[1])


def ctx_swap(block, bit):
    pairs = [(i, i ^ bit) for i in range(lax.axis_size("ctx"))]
    got = row_major(lax.ppermute(row_major(tiled(block)), "ctx", pairs))
    return got.reshape(block.shape)


def gather_ctx(block):
    far = ctx_swap(block, 2)
    near = ctx_swap(block, 1)
    return [block, far, near, ctx_swap(far, 1)]


def halves(matrix):
    half = matrix.shape[0] // 2
    return matrix[:half], matrix[half:]


def pair_add_kernel(keep, got, kept, onward):
    rows = kept.shape[0]
    kept[...] = added(keep[:rows], got[:rows])
    onward[...] = added(keep[rows:], got[rows:]).astype(bf16)


def scatter_near(keep, give, *gates):
    rows, columns = keep.shape
    half = (rows // 2, columns)
    return call(
        pair_add_kernel,
        "pair_add",
        1,
        (keep, ctx_swap(give, 1)),
        [whole(keep.shape)] * 2,
        [(half, f32), (half, bf16)],
        [whole(half)] * 2,
        gates=gates,
    )


def exchange_near(keep, give):
    quarter = keep.shape[0] // 2
    got = ctx_swap(give, 1)
    return keep[:quarter], got[:quarter], jnp.concatenate([keep[quarter:], got[quarter:]])


def exchange_far(mine, near, onward):
    quarter = mine.shape[0]
    got = ctx_swap(onward, 2)
    return [mine, got[:quarter], near, got[quarter:]]


RING = (0, 2, 4, 6, 7, 5, 3, 1)
HALF = len(RING) // 2


def ring_hop(value, step):
    count = len(RING)
    pairs = [(RING[q], RING[(q + step) % count]) for q in range(count)]
    return row_major(lax.ppermute(row_major(value), "fsdp", pairs))


def ring_owners():
    place = jnp.asarray(np.argsort(np.array(RING)).astype(np.int32))
    mine = lax.dynamic_index_in_dim(place, lax.axis_index("fsdp"), 0, False)
    offsets = np.array([0, -1, 1, -2, 2, -3, 3, 4], np.int32)
    return jnp.take(jnp.asarray(np.array(RING, np.int32)), (mine + offsets) % len(RING))


def on_ring():
    return lax.axis_size("fsdp") == len(RING)


def upper_part(rows):
    return rows // 16 * 8


class Gather:
    def __init__(self, block):
        self.block = block
        self.cut = upper_part(block.shape[0])
        self.pieces = [block]
        self.forth = self.back = block

    def hop(self, *gate):
        if not on_ring():
            return
        k = (len(self.pieces) + 1) // 2
        forth, back = self.forth, self.back
        if k == HALF:
            forth, back = forth[: self.cut], back[self.cut :]
        if gate:
            forth, back = after(forth, *gate), after(back, *gate)
        self.forth, self.back = ring_hop(forth, 1), ring_hop(back, -1)
        self.pieces += [self.forth, self.back]

    def arrived(self):
        return (self.forth, self.back) if on_ring() else ()

    def result(self, owners, columns, gates=()):
        if not on_ring():
            whole = lax.all_gather(self.block, "fsdp", axis=0, tiled=False)
            return [whole[:, top : top + n, c : c + w] for c, w, top, n in columns]
        return collect(self.pieces, owners, self.cut, columns, gates)


def collect_kernel(cut, columns, owners, *refs):
    pieces = refs[: 2 * HALF + 1]
    outs = refs[2 * HALF + 1 : 2 * HALF + 1 + len(columns)]
    sems = refs[-1]
    copies = []
    for out, (start, width, top, rows) in zip(outs, columns):
        for j, piece in enumerate(pieces):
            first = cut if j == 2 * HALF else 0
            low = max(top, first)
            high = min(top + rows, first + piece.shape[0])
            if low < high:
                copies.append(
                    pltpu.make_async_copy(
                        piece.at[pl.ds(low - first, high - low), pl.ds(start, width)],
                        out.at[owners[min(j, 2 * HALF - 1)], pl.ds(low - top, high - low)],
                        sems.at[len(copies)],
                    )
                )
    for copy in copies:
        copy.start()
    for copy in copies:
        copy.wait()


def collect(pieces, owners, cut, columns, gates):
    shapes = [(len(RING), rows, width) for _, width, _, rows in columns]
    return call(
        functools.partial(collect_kernel, cut, columns),
        "collect",
        1,
        pieces,
        [pl.BlockSpec(memory_space=pl.ANY)] * len(pieces),
        [(shape, pieces[0].dtype) for shape in shapes],
        [whole(shape) for shape in shapes],
        [pltpu.SemaphoreType.DMA((len(pieces) * len(columns),))],
        owners,
        gates,
    )


PLACE = {0: 0, -1: 1, 1: 2, -2: 3, 2: 4, -3: 5, 3: 6, 4: 7}


def ring_part_kernel(distance, cut, owners, *refs):
    if distance == HALF:
        far, ahead, behind = refs
        ahead[...] = far[:cut]
        behind[...] = far[cut:]
    elif distance == 0:
        own, forth, back, out = refs
        out[...] = added(own[...], forth[...], back[...]).astype(bf16)
    else:
        mine_ahead, mine_behind, forth, back, ahead, behind = refs
        if distance == HALF - 1:
            ahead[:cut] = added(mine_ahead[:cut], forth[...]).astype(bf16)
            ahead[cut:] = mine_ahead[cut:]
            behind[:cut] = mine_behind[:cut]
            behind[cut:] = added(mine_behind[cut:], back[...]).astype(bf16)
        else:
            ahead[...] = added(mine_ahead[...], forth[...]).astype(bf16)
            behind[...] = added(mine_behind[...], back[...]).astype(bf16)


def ring_part(blocks, owners, distance, cut, moved, gates=()):
    rows, columns = blocks.shape[1:]
    distances = (distance,) if distance in (0, HALF) else (distance, -distance)
    if distance == HALF:
        shapes = [(cut, columns), (rows - cut, columns)]
    else:
        shapes = [(rows, columns)] * len(distances)
    places = [PLACE[d] for d in distances]
    return call(
        functools.partial(ring_part_kernel, distance, cut),
        "ring_part",
        1,
        (*[blocks] * len(places), *moved),
        [
            pl.BlockSpec((None, rows, columns), lambda i, t, p=p: (t[p], 0, 0)) for p in places
        ]
        + [whole(value.shape) for value in moved],
        [(shape, bf16) for shape in shapes],
        [whole(shape) for shape in shapes],
        table=owners,
        gates=gates,
    )


class Scatter:
    def __init__(self, blocks, owners):
        self.blocks, self.owners = blocks, owners
        self.cut = upper_part(blocks.shape[1])
        self.next = HALF
        self.moved = self.given = ()

    def hop(self, *gate):
        if not on_ring():
            return
        self.given = ring_part(
            self.blocks, self.owners, self.next, self.cut, self.moved, gate
        )
        self.moved = [ring_hop(self.given[0], 1), ring_hop(self.given[1], -1)]
        self.next -= 1

    def result(self, *gate):
        if not on_ring():
            return lax.psum_scatter(self.blocks, "fsdp", scatter_dimension=0, tiled=False)
        return ring_part(self.blocks, self.owners, 0, self.cut, self.moved, gate)[0]


def reduce_small(table):
    count = lax.axis_size("fsdp")
    me = lax.axis_index("fsdp")
    held = table
    bit = count // 2
    while bit:
        halves = held.reshape(2, bit, -1)
        high = (me & bit) != 0
        keep = jnp.where(high, halves[1], halves[0])
        give = jnp.where(high, halves[0], halves[1])
        held = keep + lax.ppermute(give, "fsdp", [(i, i ^ bit) for i in range(count)])
        bit //= 2
    held = held[0]
    held = held + ctx_swap(held, 1)
    return held + ctx_swap(held, 2)


def norm_stats(values):
    centre = values - jnp.mean(values, axis=-1, keepdims=True)
    scale = lax.rsqrt(jnp.mean(centre * centre, axis=-1, keepdims=True) + norm_eps)
    return centre * scale, scale


def norm_back(grad, unit, scale, gain):
    inner = grad * gain
    back = scale * (
        inner
        - jnp.mean(inner, axis=-1, keepdims=True)
        - unit * jnp.mean(inner * unit, axis=-1, keepdims=True)
    )
    return back, jnp.sum(grad * unit, axis=0), jnp.sum(grad, axis=0)


def across(left_op, right_op, left_dim, right_dim):
    return lax.dot_general(
        left_op, right_op, (((left_dim,), (right_dim,)), ((), ())), preferred_element_type=f32
    )


def diagonal_kept():
    shape = (QB, QB)
    return lax.broadcasted_iota(jnp.int32, shape, 0) <= lax.broadcasted_iota(jnp.int32, shape, 1)


def sorted_tile(table, ref, columns):
    groups = ref.shape[0] // GROUP
    return jnp.concatenate(
        [ref[pl.ds(pl.multiple_of(table[g], GROUP), GROUP), columns] for g in range(groups)],
        axis=0,
    )


def put_sorted(table, ref, columns, first, value):
    for j in range(value.shape[0] // GROUP):
        start = pl.multiple_of(table[first + j], GROUP)
        ref[pl.ds(start, GROUP), columns] = value[j * GROUP : (j + 1) * GROUP]


def split_heads(tiles, last):
    if last:
        return [(tiles[0][:, :HD], tiles[0][:, HD:], tiles[1][:, :HD])]
    return [tuple(t[:, w * HD : (w + 1) * HD] for t in tiles) for w in range(2)]


def pair_columns(pair, last):
    if last:
        start = SLOTS // 2 * 3 * PAIR
        return [slice(start, start + PAIR), slice(start + PAIR, start + 2 * PAIR)]
    return [pl.ds(pl.multiple_of(pair * 3 * PAIR + t * PAIR, PAIR), PAIR) for t in range(3)]


def attend_pair(pair, last, table, qkv_ref, out_ref, mass_ref):
    tiles = [sorted_tile(table, qkv_ref, c) for c in pair_columns(pair, last)]
    heads = split_heads(tiles, last)
    length = qkv_ref.shape[0]
    kept = diagonal_kept()
    ready = [(q * bf16(HD**-0.5), k, v.T) for q, k, v in heads]
    for i in range(length // QB):
        rows = slice(i * QB, (i + 1) * QB)
        outs = []
        for w, (queries, keys, values_t) in enumerate(ready):
            mine = queries[rows]
            diag = jnp.where(kept, across(keys[rows], mine, 1, 1), masked_low)
            peak = jnp.max(diag, axis=0, keepdims=True)
            if i:
                rest = across(keys[: i * QB], mine, 1, 1)
                peak = jnp.maximum(peak, jnp.max(rest, axis=0, keepdims=True))
            diag = jnp.exp(diag - peak)
            mass = jnp.sum(diag, axis=0, keepdims=True)
            out = across(values_t[:, rows], diag.astype(bf16), 1, 0)
            if i:
                rest = jnp.exp(rest - peak)
                mass = mass + jnp.sum(rest, axis=0, keepdims=True)
                out = out + across(values_t[:, : i * QB], rest.astype(bf16), 1, 0)
            outs.append(out / mass)
            mass_ref[0, w : w + 1, rows] = peak + jnp.log(mass)
        if last:
            outs.append(jnp.zeros_like(outs[0]))
        tile = jnp.concatenate(outs, axis=0).T.astype(bf16)
        put_sorted(table, out_ref, slice(None), 2 * i, tile)


def attend_kernel(table, qkv_ref, out_ref, mass_ref):
    pair = pl.program_id(0)
    final = pl.num_programs(0) - 1

    @pl.when(pair < final)
    def _():
        attend_pair(pair, False, table, qkv_ref, out_ref, mass_ref)

    @pl.when(pair == final)
    def _():
        mass_ref[...] = jnp.zeros_like(mass_ref)

        @pl.when(table[table.shape[0] - 1] == 0)
        def _():
            out_ref[...] = jnp.zeros_like(out_ref)

        @pl.when(table[table.shape[0] - 1] != 0)
        def _():
            attend_pair(pair, True, table, qkv_ref, out_ref, mass_ref)


def attend_back_pair(pair, last, table, qkv_ref, grad_ref, mass_ref, out_ref, acc):
    places = pair_columns(pair, last)
    heads = split_heads([sorted_tile(table, qkv_ref, c) for c in places], last)
    grads = sorted_tile(table, grad_ref, slice(None))
    length = qkv_ref.shape[0]
    kept = diagonal_kept()
    ready = [
        (q * bf16(HD**-0.5), k, k.T, v, grads[:, w * HD : (w + 1) * HD])
        for w, (q, k, v) in enumerate(heads)
    ]
    for i in range(length // QB):
        rows = slice(i * QB, (i + 1) * QB)
        query_tiles = []
        for w, (queries, keys, keys_t, values, grads_w) in enumerate(ready):
            mine = queries[rows]
            grad = grads_w[rows]
            mass = mass_ref[0, w : w + 1, rows]
            spans = [(rows, True)] + ([(slice(0, i * QB), False)] if i else [])
            probs, both, delta = [], [], None
            for span, diagonal in spans:
                scores = across(keys[span], mine, 1, 1)
                if diagonal:
                    scores = jnp.where(kept, scores, masked_low)
                prob = jnp.exp(scores - mass)
                prod = prob * across(values[span], grad, 1, 1)
                part = jnp.sum(prod, axis=0, keepdims=True)
                delta = part if delta is None else delta + part
                probs.append(prob)
                both.append(prod)
            query_t = None
            for (span, diagonal), prob, prod in zip(spans, probs, both):
                grad_scores = (prod - prob * delta).astype(bf16)
                part = across(keys_t[:, span], grad_scores, 1, 0)
                query_t = part if query_t is None else query_t + part
                key_part = across(grad_scores, mine, 1, 0)
                value_part = across(prob.astype(bf16), grad, 1, 0)
                if diagonal:
                    acc[2 * w, span, :] = key_part
                    acc[2 * w + 1, span, :] = value_part
                else:
                    acc[2 * w, span, :] += key_part
                    acc[2 * w + 1, span, :] += value_part
            query_tiles.append(query_t * HD**-0.5)
        if last:
            query_tiles.append(jnp.zeros_like(query_tiles[0]))
        tile = jnp.concatenate(query_tiles, axis=0).T
        if last:
            tile = jnp.concatenate([tile[:, :HD], jnp.zeros_like(tile[:, HD:])], axis=1)
        put_sorted(table, out_ref, places[0], 2 * i, tile.astype(bf16))
    if last:
        old = sorted_tile(table, out_ref, places[0])
        tile = jnp.concatenate([old[:, :HD], acc[0].astype(bf16)], axis=1)
        put_sorted(table, out_ref, places[0], 0, tile)
        tile = jnp.concatenate([acc[1].astype(bf16), jnp.zeros((length, HD), bf16)], axis=1)
        put_sorted(table, out_ref, places[1], 0, tile)
    else:
        for t in range(2):
            tile = jnp.concatenate([acc[t].astype(bf16), acc[2 + t].astype(bf16)], axis=1)
            put_sorted(table, out_ref, places[1 + t], 0, tile)


def attend_back_kernel(table, qkv_ref, grad_ref, mass_ref, out_ref, acc):
    pair = pl.program_id(0)
    final = pl.num_programs(0) - 1
    refs = (table, qkv_ref, grad_ref, mass_ref, out_ref, acc)

    @pl.when(pair < final)
    def _():
        attend_back_pair(pair, False, *refs)

    @pl.when(pair == final)
    def _():
        @pl.when(table[table.shape[0] - 1] == 0)
        def _():
            for columns in pair_columns(pair, True):
                out_ref[:, columns] = jnp.zeros((out_ref.shape[0], PAIR), bf16)

        @pl.when(table[table.shape[0] - 1] != 0)
        def _():
            attend_back_pair(pair, True, *refs)


def attend(table, qkv, gates):
    length, columns = qkv.shape
    pairs = (SLOTS + 1) // 2
    return call(
        attend_kernel,
        "attend",
        pairs,
        (qkv,),
        [whole((length, columns))],
        [((length, pairs * PAIR), bf16), ((pairs, 8, length), f32)],
        [
            pl.BlockSpec((length, PAIR), lambda p, t: (0, p)),
            pl.BlockSpec((1, 8, length), lambda p, t: (p, 0, 0)),
        ],
        table=table,
        gates=gates,
    )


def attend_back(table, qkv, grad, mass, gates):
    length, columns = qkv.shape
    pairs = (SLOTS + 1) // 2
    return call(
        attend_back_kernel,
        "attend_back",
        pairs,
        (qkv, grad, mass),
        [
            whole((length, columns)),
            pl.BlockSpec((length, PAIR), lambda p, t: (0, p)),
            pl.BlockSpec((1, 8, length), lambda p, t: (p, 0, 0)),
        ],
        [((length, columns), bf16)],
        [whole((length, columns))],
        [pltpu.VMEM((4, length, HD), f32)],
        table,
        gates,
    )[0]


def whole(shape):
    return pl.BlockSpec(shape, lambda *_: (0,) * len(shape))


def rows_spec(rows, columns):
    return pl.BlockSpec((rows, columns), lambda i, *_: (i, 0))


def call(kernel, name, grid, operands, specs, outs, out_specs, scratch=(), table=None, gates=()):
    tables = () if table is None else (table,)
    first = len(tables) + len(operands)
    count = len(gates)

    def body(*refs):
        kernel(*refs[:first], *refs[first + count :])

    return pl.pallas_call(
        body,
        grid_spec=pltpu.PrefetchScalarGridSpec(
            num_scalar_prefetch=len(tables),
            grid=(grid,),
            in_specs=list(specs) + [pl.BlockSpec(memory_space=pl.ANY)] * count,
            out_specs=out_specs,
            scratch_shapes=list(scratch),
        ),
        out_shape=[jax.ShapeDtypeStruct(shape, kind) for shape, kind in outs],
        compiler_params=pltpu.CompilerParams(vmem_limit_bytes=VMEM_LIMIT),
        cost_estimate=LIGHT,
        name=name,
    )(*tables, *operands, *gates)


def pick_block(refs, held):
    for j, ref in enumerate(refs):

        @pl.when(pl.program_id(0) == j)
        def _(ref=ref):
            held[...] = ref[...]


def norm_mixed_kernel(*refs):
    blocks, (gain, shift, weights, bias, normed, mixed, held) = refs[:4], refs[4:]
    pick_block(blocks, held)
    unit, _ = norm_stats(held[...].astype(f32))
    low = (unit * gain[...] + shift[...]).astype(bf16)
    normed[...] = low
    mixed[...] = (product(low, weights[...]) + bias[...]).astype(bf16)


def norm_mixed(blocks, gain, shift, weights, bias):
    count, width = blocks[0].shape
    mixed_width = weights.shape[1]
    length = count * len(blocks)
    return call(
        norm_mixed_kernel,
        "norm_mixed",
        len(blocks),
        (*blocks, gain[None], shift[None], weights, bias),
        [whole((count, width))] * len(blocks)
        + [whole((1, width))] * 2
        + [whole(weights.shape), whole((1, mixed_width))],
        [((length, width), bf16), ((length, mixed_width), bf16)],
        [rows_spec(count, width), rows_spec(count, mixed_width)],
        [pltpu.VMEM((count, width), bf16)],
    )


def join_kernel(table, *refs):
    pieces, out, sems, last_sem = refs[:4], refs[4], refs[5], refs[6]
    step, span = BASE * HD, SLOTS * HD
    width = out.shape[1]
    rest = span - step
    last = len(pieces) - 1

    def copies(j):
        start = pl.multiple_of(table[j] * step, PAIR)
        main = pltpu.make_async_copy(
            pieces[j].at[:, pl.ds(0, step)], out.at[:, pl.ds(start, step)], sems.at[j]
        )
        tail = pltpu.make_async_copy(
            pieces[j].at[:, pl.ds(step, rest)], out.at[:, pl.ds(width - rest, rest)], last_sem.at[0]
        )
        return main, tail

    for j in range(len(pieces)):
        main, tail = copies(j)
        main.start()

        @pl.when(table[j] == last)
        def _(tail=tail):
            tail.start()

    for j in range(len(pieces)):
        main, tail = copies(j)
        main.wait()

        @pl.when(table[j] == last)
        def _(tail=tail):
            tail.wait()


def join_windows(table, pieces, width):
    rows = pieces[0].shape[0]
    return call(
        join_kernel,
        "join_windows",
        1,
        pieces,
        [pl.BlockSpec(memory_space=pl.ANY)] * len(pieces),
        [((rows, width), pieces[0].dtype)],
        [whole((rows, width))],
        [pltpu.SemaphoreType.DMA((len(pieces),)), pltpu.SemaphoreType.DMA((1,))],
        table,
    )[0]


def attn_out_kernel(table, *refs):
    pieces, rest = refs[:4], refs[4:]
    weights, tokens, bias, gain, shift, middle, normed, attended = rest
    step, span = BASE * HD, SLOTS * HD
    width = attended.shape[1]
    for j, piece in enumerate(pieces):
        start = pl.multiple_of(table[j] * step, PAIR)
        attended[:, pl.ds(start, step)] = piece[:, :step]

        @pl.when(table[j] == len(pieces) - 1)
        def _(piece=piece):
            attended[:, width - (span - step) :] = piece[:, step:]

    value = tokens[...].astype(f32) + product(attended[...], weights[...]) + bias[...]
    middle[...] = value
    unit, _ = norm_stats(value)
    normed[...] = (unit * gain[...] + shift[...]).astype(bf16)


def attn_out(table, pieces, weights, tokens, bias, gain, shift):
    count, width = tokens.shape
    return call(
        attn_out_kernel,
        "attn_out",
        1,
        (*pieces, weights, tokens, bias[None], gain[None], shift[None]),
        [whole(piece.shape) for piece in pieces]
        + [whole(weights.shape), whole((count, width))]
        + [whole((1, width))] * 3,
        [((count, width), f32), ((count, width), bf16), ((count, width), bf16)],
        [whole((count, width))] * 3,
        table=table,
    )


def up_kernel(*refs):
    blocks, (weights, bias, activated, slope, normed, held) = refs[:4], refs[4:]
    pick_block(blocks, held)
    normed[...] = held[...]
    before = product(held[...], weights[...]) + bias[...]
    square = before * before
    inner = jnp.tanh(before * (0.7978845608028654 + 0.7978845608028654 * 0.044715 * square))
    half = 0.5 * (1.0 + inner)
    activated[...] = (before * half).astype(bf16)
    slope[...] = (
        half
        + 0.5
        * before
        * (1.0 - inner * inner)
        * (0.7978845608028654 + 3 * 0.7978845608028654 * 0.044715 * square)
    ).astype(bf16)


def feed_up(blocks, weights, bias):
    count, width = blocks[0].shape
    units = weights.shape[1]
    length = count * len(blocks)
    return call(
        up_kernel,
        "feed_up",
        len(blocks),
        (*blocks, weights, bias[None]),
        [whole((count, width))] * len(blocks) + [whole(weights.shape), whole((1, units))],
        [((length, units), bf16), ((length, units), bf16), ((length, width), bf16)],
        [rows_spec(count, units), rows_spec(count, units), rows_spec(count, width)],
        [pltpu.VMEM((count, width), bf16)],
    )


def back_kernel(*refs):
    blocks, (down, slope, low, sums, held) = refs[:4], refs[4:]
    pick_block(blocks, held)
    value = (back_product(held[...], down[...]) * slope[...].astype(f32)).astype(bf16)
    low[...] = value

    @pl.when(pl.program_id(0) == 0)
    def _():
        sums[...] = jnp.zeros_like(sums)

    sums[...] += jnp.sum(value.astype(f32), axis=0, keepdims=True)


def feed_back(blocks, down, slope, gates):
    count, width = blocks[0].shape
    units = slope.shape[1]
    length = count * len(blocks)
    return call(
        back_kernel,
        "feed_back",
        len(blocks),
        (*blocks, down, slope),
        [whole((count, width))] * len(blocks) + [whole(down.shape), rows_spec(count, units)],
        [((length, units), bf16), ((1, units), f32)],
        [rows_spec(count, units), whole((1, units))],
        [pltpu.VMEM((count, width), bf16)],
        gates=gates,
    )


def plain_back_kernel(left, right, out):
    out[...] = back_product(left[...], right[...]).astype(bf16)


def plain_back(left, right, name, gates):
    length, inner = left.shape
    width = right.shape[0]
    return call(
        plain_back_kernel,
        name,
        length // QB,
        (left, right),
        [rows_spec(QB, inner), whole(right.shape)],
        [((length, width), bf16)],
        [rows_spec(QB, width)],
        gates=gates,
    )[0]


VECTOR_ROWS = 8
FC_START = 2 * PAIR


def attn_block_kernel(place, qkv, out_weights, *refs):
    vectors, bias_fc, block = refs[:VECTOR_ROWS], refs[VECTOR_ROWS], refs[VECTOR_ROWS + 1]
    step, span = BASE * HD, SLOTS * HD
    width = out_weights.shape[1]
    rows = qkv.shape[0]
    parts = []
    for t in range(3):
        skip = t * width % PAIR
        start = pl.multiple_of(place[0] * step + (t * width - skip), PAIR)
        parts.append(qkv[:, pl.ds(start, span + skip)][:, skip:])
    for p in range(SLOTS // 2):
        for t in range(3):
            first = (3 * p + t) * PAIR
            block[:rows, first : first + PAIR] = parts[t][:, p * PAIR : (p + 1) * PAIR]
    rest = [part[:, (SLOTS - 1) * HD :] for part in parts] + [jnp.zeros((rows, HD), bf16)]
    first = 3 * (SLOTS // 2) * PAIR
    for p in range(2):
        block[:rows, first + p * PAIR : first + (p + 1) * PAIR] = jnp.concatenate(
            rest[2 * p : 2 * p + 2], axis=1
        )
    start = pl.multiple_of(place[0] * step, PAIR)
    block[:rows, first + 2 * PAIR :] = out_weights[:, pl.ds(start, span)]
    block[rows:, :] = jnp.zeros((VECTOR_ROWS, block.shape[1]), bf16)
    lines = jnp.stack([vector[...].astype(f32) for vector in vectors])
    block[rows:, : lines.shape[1]] = lines.astype(bf16)
    units = bias_fc.shape[0]
    line = jnp.broadcast_to(bias_fc[...].astype(f32)[None], (VECTOR_ROWS, units))
    block[rows:, FC_START : FC_START + units] = line.astype(bf16)


def form_attn_block(place, qkv, out_weights, vectors, bias_fc):
    rows = qkv.shape[0]
    columns = 3 * (SLOTS // 2) * PAIR + 2 * PAIR + SLOTS * HD
    vectors = [*vectors, bias_fc]
    return call(
        attn_block_kernel,
        "form_attn_block",
        1,
        (qkv, out_weights, *vectors),
        [whole(value.shape) for value in (qkv, out_weights, *vectors)],
        [((rows + VECTOR_ROWS, columns), bf16)],
        [whole((rows + VECTOR_ROWS, columns))],
        table=place,
    )[0]


def whole_rows_kernel(table, *refs):
    pieces, out, held = refs[:4], refs[4], refs[5]
    pick_block(pieces, held)
    out[...] = held[...].astype(f32)


def whole_rows(table, pieces, gates):
    rows, width = pieces[0].shape
    return call(
        whole_rows_kernel,
        "whole_rows",
        len(pieces),
        pieces,
        [whole((rows, width))] * len(pieces),
        [((len(pieces), rows, width), f32)],
        [pl.BlockSpec((None, rows, width), lambda i, t: (t[i], 0, 0))],
        [pltpu.VMEM((rows, width), bf16)],
        table,
        gates,
    )[0].reshape(-1, width)


def put_windows(table, held, outs):
    for j in range(2 * len(outs)):
        start = pl.multiple_of(table[j] * BASE * HD, PAIR)
        outs[j // 2][j % 2] = held[:, pl.ds(start, SLOTS * HD)]


def norm_two_kernel(table, *refs):
    kept, far, middle, grad_out, gain, weights, grad_middle, low, keep, give, sums, held = refs
    grad = kept[...] + far[...].astype(f32)
    unit, scale = norm_stats(middle[...])
    back, grad_gain, grad_shift = norm_back(grad, unit, scale, gain[...])
    out = grad_out[...].astype(f32)
    value = out + back
    grad_middle[...] = value
    value_low = value.astype(bf16)
    low[...] = value_low
    held[...] = back_product(value_low, weights[...]).astype(bf16)
    put_windows(table, held, (keep, give))
    sums[0:1, :] = grad_gain[None]
    sums[1:2, :] = grad_shift[None]
    sums[2:3, :] = jnp.sum(value_low.astype(f32), axis=0, keepdims=True)
    sums[3:4, :] = jnp.sum(out, axis=0, keepdims=True)


def norm_two_back(table, kept, far, middle, grad_out, gain, weights, gates):
    count, width = middle.shape
    half = (2, count, SLOTS * HD)
    return call(
        norm_two_kernel,
        "norm_two_back",
        1,
        (kept, far, middle, grad_out, gain[None], weights),
        [whole((count, width))] * 4 + [whole((1, width)), whole(weights.shape)],
        [
            ((count, width), f32),
            ((count, width), bf16),
            (half, bf16),
            (half, bf16),
            ((4, width), f32),
        ],
        [
            whole((count, width)),
            whole((count, width)),
            whole(half),
            whole(half),
            whole((4, width)),
        ],
        [pltpu.VMEM((count, width), bf16)],
        table,
        gates=gates,
    )


def norm_one_kernel(kept, far, tokens, grad_middle, gain, grad_tokens, sums):
    grad = kept[...] + far[...].astype(f32)
    unit, scale = norm_stats(tokens[...].astype(f32))
    back, grad_gain, grad_shift = norm_back(grad, unit, scale, gain[...])
    grad_tokens[...] = grad_middle[...] + back
    sums[0:1, :] = grad_gain[None]
    sums[1:2, :] = grad_shift[None]


def norm_one_back(kept, far, tokens, grad_middle, gain, gates):
    shape = kept.shape
    return call(
        norm_one_kernel,
        "norm_one_back",
        1,
        (kept, far, tokens, grad_middle, gain[None]),
        [whole(shape)] * 4 + [whole((1, shape[1]))],
        [(shape, f32), ((2, shape[1]), f32)],
        [whole(shape), whole((2, shape[1]))],
        gates=gates,
    )


def out_grad_kernel(table, attended, low, keep, give, held):
    held[...] = outer_sum(attended[...], low[...]).astype(bf16)
    put_windows(table, held, (keep, give))


def out_weight_grad(table, attended, low, gates):
    count, width = attended.shape
    half = (2, width, SLOTS * HD)
    return call(
        out_grad_kernel,
        "out_weight_grad",
        1,
        (attended, low),
        [whole((count, width))] * 2,
        [(half, bf16)] * 2,
        [whole(half)] * 2,
        [pltpu.VMEM((width, width), bf16)],
        table,
        gates=gates,
    )


def whole_fc_kernel(table, *refs):
    pieces, out, held, sems = refs[:4], refs[4], refs[5], refs[6]
    copies = [
        pltpu.make_async_copy(piece, held.at[table[j]], sems.at[j])
        for j, piece in enumerate(pieces)
    ]
    for copy in copies:
        copy.start()
    for copy in copies:
        copy.wait()
    ranks = len(pieces)
    units = pieces[0].shape[0]
    for r in range(ranks):
        for i in range(pieces[0].shape[1] // units):
            first = (i * ranks + r) * units
            out[:, first : first + units] = held[r, :, i * units : (i + 1) * units].astype(f32)


def whole_fc(table, pieces, gates):
    rows, width = pieces[0].shape
    ranks = len(pieces)
    return call(
        whole_fc_kernel,
        "whole_fc",
        1,
        pieces,
        [pl.BlockSpec(memory_space=pl.ANY)] * ranks,
        [((rows, ranks * width), f32)],
        [whole((rows, ranks * width))],
        [pltpu.VMEM((ranks, rows, width), bf16), pltpu.SemaphoreType.DMA((ranks,))],
        table,
        gates,
    )[0]


def whole_qkv_kernel(table, *refs):
    pieces, out, held, sems = refs[:4], refs[4], refs[5], refs[6]
    copies = [
        pltpu.make_async_copy(piece, held.at[table[j]], sems.at[j])
        for j, piece in enumerate(pieces)
    ]
    for copy in copies:
        copy.start()
    for copy in copies:
        copy.wait()
    width = out.shape[1] // 3
    for rank in range(len(pieces)):
        for part in range(3):
            start = part * width + rank * BASE * HD
            for p in range(SLOTS // 2):
                tile = held[rank, :, (3 * p + part) * PAIR : (3 * p + part + 1) * PAIR]
                out[:, start + p * PAIR : start + (p + 1) * PAIR] = tile.astype(f32)
            if rank == len(pieces) - 1:
                first = 3 * (SLOTS // 2) * PAIR + part * HD
                tile = held[rank, :, first : first + HD]
                out[:, start + BASE * HD : start + SLOTS * HD] = tile.astype(f32)


def whole_qkv(table, pieces, width):
    rows = pieces[0].shape[0]
    return call(
        whole_qkv_kernel,
        "whole_qkv",
        1,
        pieces,
        [pl.BlockSpec(memory_space=pl.ANY)] * len(pieces),
        [((rows, 3 * width), f32)],
        [whole((rows, 3 * width))],
        [
            pltpu.VMEM((len(pieces),) + pieces[0].shape, bf16),
            pltpu.SemaphoreType.DMA((len(pieces),)),
        ],
        table,
    )[0]


def to_pairs(parts):
    pieces = []
    for p in range(SLOTS // 2):
        pieces += [part[:, p * PAIR : (p + 1) * PAIR] for part in parts]
    pieces += [part[:, (SLOTS - 1) * HD :] for part in parts]
    pieces.append(jnp.zeros((parts[0].shape[0], HD), parts[0].dtype))
    return jnp.concatenate(pieces, axis=1)


def from_pairs(matrix, part, last):
    pieces = [
        matrix[:, (3 * p + part) * PAIR : (3 * p + part + 1) * PAIR] for p in range(SLOTS // 2)
    ]
    if last:
        start = 3 * (SLOTS // 2) * PAIR + part * HD
        pieces.append(matrix[:, start : start + HD])
    return pieces


def per_device(
    tokens_in,
    group_order,
    out_grad,
    w_qkv,
    w_attn_out,
    b_query,
    b_value,
    b_attn_out,
    w_fc,
    w_proj,
    b_fc,
    b_proj,
    ln1_gain,
    ln1_bias,
    ln2_gain,
    ln2_bias,
):
    ctx = lax.axis_size("ctx")
    shards = lax.axis_size("fsdp")
    rank = lax.axis_index("ctx")
    tokens = tokens_in[0].astype(f32)
    count, width = tokens.shape
    span = SLOTS * HD
    step = BASE * HD
    mixed_width = (3 * span + PAIR - 1) // PAIR * PAIR
    attn_width = mixed_width + span
    shard_rows = w_qkv.shape[0]
    unit_rows = w_proj.shape[0] // ctx
    peers = [rank ^ bit for bit in PEERS]
    owners = ring_owners() if on_ring() else None

    peer_table = jnp.stack(peers).astype(jnp.int32)

    slots = jnp.argsort(group_order).astype(jnp.int32)
    place = jnp.take(jnp.asarray(np.argsort(np.array(PEERS)).astype(np.int32)), (slots // 2) ^ rank)
    slot_rows = (place * 2 + slots % 2) * GROUP
    table = jnp.concatenate([slot_rows, (rank == ctx - 1).astype(jnp.int32)[None]])

    attn_block = form_attn_block(
        rank[None].astype(jnp.int32),
        w_qkv,
        w_attn_out,
        (b_query, b_value, b_attn_out, b_proj, ln1_gain, ln1_bias, ln2_gain, ln2_bias),
        b_fc,
    )
    own_tokens = tokens_in[0]
    own_grad = out_grad[0]
    attn_gather = Gather(attn_block)
    attn_gather.hop()
    w_fc = after(w_fc, attn_block)
    fc_block = jnp.concatenate(
        [
            lax.dynamic_slice(
                w_fc, (0, (i * ctx + rank) * unit_rows), (shard_rows, unit_rows)
            )
            for i in range(shards)
        ],
        axis=1,
    )
    proj_block = lax.dynamic_slice(w_proj, (rank * unit_rows, 0), (unit_rows, width))
    feed_block = jnp.concatenate([fc_block, proj_block])
    token_blocks = gather_ctx(own_tokens)
    grad_blocks = gather_ctx(after(own_grad, token_blocks[1]))
    attn_gather.hop()
    attn_gather.hop(feed_block)
    feed_gather = Gather(after(feed_block, *attn_gather.arrived()))
    feed_gather.hop()
    attn_gather.hop()

    qkv_weights, out_columns, small = attn_gather.result(
        owners,
        (
            (0, mixed_width, 0, shard_rows),
            (mixed_width, span, 0, shard_rows),
            (0, attn_width, shard_rows, VECTOR_ROWS),
        ),
        feed_gather.arrived(),
    )
    qkv_weights = qkv_weights.reshape(width, mixed_width)
    small = small.astype(f32)
    bias_q, bias_v, bias_o, bias_p, gain_one, shift_one, gain_two, shift_two = [
        small[:, t, :shard_rows].reshape(-1) for t in range(VECTOR_ROWS)
    ]
    bias_fc = lax.dynamic_index_in_dim(
        small[:, 0, FC_START : FC_START + ctx * unit_rows].reshape(shards, ctx, unit_rows),
        rank,
        1,
        False,
    ).reshape(-1)

    def my_bias(vector):
        return lax.dynamic_slice(vector, (rank * step,), (span,))[None]

    bias_mixed = to_pairs([my_bias(bias_q), jnp.zeros((1, span), f32), my_bias(bias_v)])
    normed_all, mixed = norm_mixed(
        [after(token_blocks[0], grad_blocks[3])] + token_blocks[1:],
        gain_one,
        shift_one,
        qkv_weights,
        bias_mixed,
    )
    attended_mine, mass = attend(table, mixed, feed_gather.arrived())
    feed_gather.hop()
    out_blocks = gather_ctx(out_columns.reshape(width, span))
    out_weights = join_windows(peer_table, out_blocks, width)
    pieces = exchange_far(
        *exchange_near(*halves(after(row_major(attended_mine[:, :span]), out_blocks[1])))
    )
    middle, normed_two, attended = attn_out(
        peer_table,
        pieces,
        out_weights,
        after(own_tokens, *feed_gather.arrived()),
        bias_o,
        gain_two,
        shift_two,
    )
    feed_gather.hop()

    normed_far = ctx_swap(normed_two, 2)
    normed_blocks = [
        normed_two,
        normed_far,
        ctx_swap(normed_two, 1),
    ]
    feed_gather.hop()
    normed_blocks.append(ctx_swap(after(normed_far, *feed_gather.arrived()), 1))
    grad_all = row_major(jnp.concatenate([after(grad_blocks[0], normed_two)] + grad_blocks[1:]))
    fc_weights, proj_weights = feed_gather.result(
        owners, ((0, width, 0, shard_rows), (0, width, shard_rows, unit_rows))
    )
    fc_weights = fc_weights.reshape(width, -1)
    proj_weights = proj_weights.reshape(-1, width)
    activated, slope, normed_two_all = feed_up(
        [after(normed_blocks[0], grad_all)] + normed_blocks[1:], fc_weights, bias_fc
    )

    grad_proj = row_major(outer_sum(activated, grad_all).astype(bf16))
    proj_scatter = Scatter(grad_proj.reshape(shards, unit_rows, width), owners)
    proj_scatter.hop()
    before_low, grad_bias_fc = feed_back(grad_blocks, proj_weights, slope, proj_scatter.given)
    proj_scatter.hop(before_low)
    grad_two = plain_back(before_low, fc_weights, "feed_back_two", proj_scatter.given)
    kept_two, onward_two = scatter_near(*halves(grad_two))
    proj_scatter.hop()
    branch_two = row_major(
        product(after(activated, *proj_scatter.given), proj_weights).astype(bf16)
    )
    grad_fc = row_major(
        outer_sum(after(normed_two_all, onward_two, *proj_scatter.given), before_low).astype(bf16)
    )
    far_two = ctx_swap(onward_two, 2)
    kept_branch, onward_branch = scatter_near(*halves(branch_two))
    fc_scatter = Scatter(grad_fc.reshape(shards, shard_rows, shards * unit_rows), owners)
    fc_scatter.hop()
    proj_scatter.hop(*fc_scatter.given)
    grad_middle, middle_low, heads_keep, heads_give, sums_two = norm_two_back(
        peer_table,
        kept_two,
        far_two,
        middle,
        own_grad,
        gain_two,
        out_weights,
        (onward_branch, *fc_scatter.given, *proj_scatter.given),
    )
    far_branch = ctx_swap(after(onward_branch, far_two), 2)
    fc_scatter.hop()

    heads_near = exchange_near(heads_keep.reshape(-1, span), heads_give.reshape(-1, span))
    out_keep, out_give = out_weight_grad(
        peer_table,
        attended,
        middle_low,
        (*heads_near[1:], *fc_scatter.given, *proj_scatter.moved),
    )
    heads_far = exchange_far(heads_near[0], heads_near[1], after(heads_near[2], far_branch))
    grad_heads = jnp.pad(jnp.concatenate(heads_far), ((0, 0), (0, PAIR - span % PAIR)))
    tokens_out = (middle + added(kept_branch, far_branch) + bias_p).astype(bf16)[None]
    kept_out, onward_out = scatter_near(
        out_keep.reshape(-1, span), after(out_give.reshape(-1, span), heads_far[1])
    )
    grad_mixed = attend_back(table, mixed, grad_heads, mass, (out_give,))
    far_out = ctx_swap(onward_out, 2)
    fc_scatter.hop(grad_mixed)
    grad_qkv = row_major(
        outer_sum(normed_all, after(grad_mixed, onward_out, *fc_scatter.given)).astype(bf16)
    )
    qkv_scatter = Scatter(grad_qkv.reshape(shards, shard_rows, mixed_width), owners)
    qkv_scatter.hop()
    fc_scatter.hop(*qkv_scatter.given)
    qkv_scatter.hop(*fc_scatter.given)
    grad_one = plain_back(
        grad_mixed, qkv_weights, "mixed_back", (far_out, *fc_scatter.given, *qkv_scatter.given)
    )
    kept_one, onward_one = scatter_near(*halves(grad_one))
    shard_proj = proj_scatter.result(onward_one)
    grad_attn_out = added(kept_out, far_out).astype(bf16)
    out_scatter = Scatter(grad_attn_out.reshape(shards, shard_rows, span), owners)
    out_scatter.hop(onward_one)
    far_one = ctx_swap(onward_one, 2)
    proj_pieces = gather_ctx(after(shard_proj, far_one))
    qkv_scatter.hop(*fc_scatter.moved)
    out_scatter.hop(*qkv_scatter.given)
    fc_pieces = gather_ctx(after(fc_scatter.result(*qkv_scatter.given), proj_pieces[1]))
    grad_tokens, sums_one = norm_one_back(
        kept_one, far_one, own_tokens, grad_middle, gain_one, qkv_scatter.given
    )
    grad_tokens = grad_tokens[None]
    qkv_scatter.hop(far_one)
    out_scatter.hop(*qkv_scatter.given)
    grad_w_proj = whole_rows(peer_table, proj_pieces, qkv_scatter.given)
    shard_qkv = qkv_scatter.result(proj_pieces[1])
    out_scatter.hop(shard_qkv)
    qkv_pieces = gather_ctx(after(shard_qkv, fc_pieces[1]))
    grad_w_fc = whole_fc(peer_table, fc_pieces, (shard_qkv,))

    bias_sums = jnp.sum(grad_mixed.astype(f32), axis=0, keepdims=True)

    def all_heads(part):
        mine = jnp.concatenate(from_pairs(bias_sums, part, True), axis=1)
        return lax.dynamic_update_slice(jnp.zeros((1, width), f32), mine, (0, rank * step))

    grad_bias_fc = lax.dynamic_update_slice(
        jnp.zeros((shards, ctx, unit_rows), f32),
        grad_bias_fc.reshape(shards, 1, unit_rows),
        (0, rank, 0),
    )
    small_grads = [
        all_heads(0),
        all_heads(2),
        sums_two[2],
        sums_two[3],
        sums_one[0],
        sums_one[1],
        sums_two[0],
        sums_two[1],
        grad_bias_fc,
    ]
    summed = reduce_small(
        jnp.concatenate([value.reshape(shards, -1) for value in small_grads], axis=1)
    )
    shares = [summed[t * shard_rows : (t + 1) * shard_rows] for t in range(8)]
    share_fc = summed[8 * shard_rows :]

    whole_attn_out = join_windows(peer_table, gather_ctx(out_scatter.result()), width).astype(f32)
    grad_w_qkv = whole_qkv(peer_table, qkv_pieces, width)

    return (
        tokens_out,
        grad_tokens,
        grad_w_qkv,
        whole_attn_out,
        shares[0],
        shares[1],
        shares[2],
        grad_w_fc,
        grad_w_proj,
        share_fc,
        shares[3],
        shares[4],
        shares[5],
        shares[6],
        shares[7],
    )


def solution(mesh):
    placed = (
        P("fsdp", "ctx", None),
        P(),
        P("fsdp", "ctx", None),
        P("fsdp", None),
        P("fsdp", None),
        P("fsdp"),
        P("fsdp"),
        P("fsdp"),
        P("fsdp", None),
        P("fsdp", None),
        P("fsdp"),
        P("fsdp"),
        P("fsdp"),
        P("fsdp"),
        P("fsdp"),
        P("fsdp"),
    )
    return jax.shard_map(
        per_device,
        mesh=mesh,
        in_specs=placed,
        out_specs=(
            P("fsdp", "ctx", None),
            P("fsdp", "ctx", None),
            P("fsdp", None),
            P("fsdp", None),
            P("fsdp"),
            P("fsdp"),
            P("fsdp"),
            P("fsdp", None),
            P("fsdp", None),
            P("fsdp"),
            P("fsdp"),
            P("fsdp"),
            P("fsdp"),
            P("fsdp"),
            P("fsdp"),
        ),
        check_vma=False,
    )
```

```python
import functools

import jax
import jax.numpy as jnp
import numpy as np
from jax import lax
from jax.experimental import pallas as pl
from jax.experimental.layout import Layout, with_layout_constraint
from jax.experimental.pallas import tpu as pltpu
from jax.sharding import PartitionSpec as P

H = 25
HD = 64
GROUP = 128
QB = 256
PAIR = 2 * HD
RANKS = 4
BASE = H // RANKS
SLOTS = H - (RANKS - 1) * BASE
norm_eps = 1e-05
masked_low = -1e30
LIGHT = pl.CostEstimate(flops=1 << 20, transcendentals=0, bytes_accessed=1 << 16)
VMEM_LIMIT = 56 << 20
f32 = jnp.float32
bf16 = jnp.bfloat16


def outer_sum(left_op, right_op):
    return lax.dot_general(
        left_op, right_op, (((0,), (0,)), ((), ())), preferred_element_type=f32
    )


def back_product(left_op, right_op):
    return lax.dot_general(
        left_op, right_op, (((1,), (1,)), ((), ())), preferred_element_type=f32
    )


def product(left_op, right_op):
    return jnp.dot(left_op, right_op, preferred_element_type=f32)


def added(*terms):
    total = terms[0].astype(f32)
    for term in terms[1:]:
        total = total + term.astype(f32)
    return total


def row_major(matrix):
    return with_layout_constraint(matrix, Layout(major_to_minor=tuple(range(matrix.ndim))))


def slot(always, step):
    empty = jax.eval_shape(step)
    return lax.cond(
        always,
        step,
        lambda: jax.tree.map(lambda leaf: jnp.zeros(leaf.shape, leaf.dtype), empty),
    )


def after(value, *others):
    return lax.optimization_barrier((value,) + others)[0]


PEERS = (0, 2, 1, 3)


def tiled(block):
    if block.ndim != 2 or block.shape[0] % 8:
        return block
    return block.reshape(-1, 8, block.shape[1])


def ctx_swap(block, bit):
    pairs = [(i, i ^ bit) for i in range(lax.axis_size("ctx"))]
    got = row_major(lax.ppermute(row_major(tiled(block)), "ctx", pairs))
    return got.reshape(block.shape)


def gather_ctx(block):
    far = ctx_swap(block, 2)
    near = ctx_swap(block, 1)
    return [block, far, near, ctx_swap(far, 1)]


def halves(matrix):
    half = matrix.shape[0] // 2
    return matrix[:half], matrix[half:]


def pair_add_kernel(keep, got, kept, onward):
    rows = kept.shape[0]
    kept[...] = added(keep[:rows], got[:rows]).astype(kept.dtype)
    onward[...] = added(keep[rows:], got[rows:]).astype(bf16)


def pair_add(keep, got, kind=f32):
    rows, columns = keep.shape
    half = (rows // 2, columns)
    return call(
        pair_add_kernel,
        "pair_add",
        1,
        (keep, got),
        [whole(keep.shape)] * 2,
        [(half, kind), (half, bf16)],
        [whole(half)] * 2,
    )


def pair_split_kernel(keep, got, kept, first, second):
    rows = kept.shape[0]
    half = rows // 2
    kept[...] = added(keep[:rows], got[:rows]).astype(kept.dtype)
    first[...] = added(keep[rows : rows + half], got[rows : rows + half]).astype(bf16)
    second[...] = added(keep[rows + half :], got[rows + half :]).astype(bf16)


def pair_split(keep, got):
    rows, columns = keep.shape
    half, quarter = (rows // 2, columns), (rows // 4, columns)
    return call(
        pair_split_kernel,
        "pair_split",
        1,
        (keep, got),
        [whole(keep.shape)] * 2,
        [(half, bf16), (quarter, bf16), (quarter, bf16)],
        [whole(half), whole(quarter), whole(quarter)],
    )


def exchange_near(keep, give):
    quarter = keep.shape[0] // 2
    got = ctx_swap(give, 1)
    return keep[:quarter], got[:quarter], jnp.concatenate([keep[quarter:], got[quarter:]])


def exchange_far(mine, near, onward):
    quarter = mine.shape[0]
    got = ctx_swap(onward, 2)
    return [mine, got[:quarter], near, got[quarter:]]


RING = (0, 2, 4, 6, 7, 5, 3, 1)
HALF = len(RING) // 2


def ring_hop(value, step):
    count = len(RING)
    pairs = [(RING[q], RING[(q + step) % count]) for q in range(count)]
    return row_major(lax.ppermute(row_major(value), "fsdp", pairs))


def ring_owners():
    place = jnp.asarray(np.argsort(np.array(RING)).astype(np.int32))
    mine = lax.dynamic_index_in_dim(place, lax.axis_index("fsdp"), 0, False)
    offsets = np.array([0, -1, 1, -2, 2, -3, 3, 4], np.int32)
    return jnp.take(jnp.asarray(np.array(RING, np.int32)), (mine + offsets) % len(RING))


def on_ring():
    return lax.axis_size("fsdp") == len(RING)


def upper_part(rows):
    return rows // 16 * 8


class Gather:
    def __init__(self, block):
        self.block = block
        self.cut = upper_part(block.shape[0])
        self.pieces = [block]
        self.forth = self.back = block

    def hop(self, *gate):
        if not on_ring():
            return
        k = (len(self.pieces) + 1) // 2
        forth, back = self.forth, self.back
        if k == HALF:
            forth, back = forth[: self.cut], back[self.cut :]
        if gate:
            forth, back = after(forth, *gate), after(back, *gate)
        self.forth, self.back = ring_hop(forth, 1), ring_hop(back, -1)
        self.pieces += [self.forth, self.back]

    def arrived(self):
        return (self.forth, self.back) if on_ring() else ()

    def result(self, owners, columns, gates=()):
        if not on_ring():
            whole = lax.all_gather(self.block, "fsdp", axis=0, tiled=False)
            return [whole[:, top : top + n, c : c + w] for c, w, top, n in columns]
        return collect(self.pieces, owners, self.cut, columns, gates)


def collect_kernel(cut, columns, owners, *refs):
    pieces = refs[: 2 * HALF + 1]
    outs = refs[2 * HALF + 1 : 2 * HALF + 1 + len(columns)]
    sems = refs[-1]
    copies = []
    for out, (start, width, top, rows) in zip(outs, columns):
        for j, piece in enumerate(pieces):
            first = cut if j == 2 * HALF else 0
            low = max(top, first)
            high = min(top + rows, first + piece.shape[0])
            if low < high:
                copies.append(
                    pltpu.make_async_copy(
                        piece.at[pl.ds(low - first, high - low), pl.ds(start, width)],
                        out.at[owners[min(j, 2 * HALF - 1)], pl.ds(low - top, high - low)],
                        sems.at[len(copies)],
                    )
                )
    for copy in copies:
        copy.start()
    for copy in copies:
        copy.wait()


def collect(pieces, owners, cut, columns, gates):
    shapes = [(len(RING), rows, width) for _, width, _, rows in columns]
    return call(
        functools.partial(collect_kernel, cut, columns),
        "collect",
        1,
        pieces,
        [pl.BlockSpec(memory_space=pl.ANY)] * len(pieces),
        [(shape, pieces[0].dtype) for shape in shapes],
        [whole(shape) for shape in shapes],
        [pltpu.SemaphoreType.DMA((len(pieces) * len(columns),))],
        owners,
        gates,
    )


PLACE = {0: 0, -1: 1, 1: 2, -2: 3, 2: 4, -3: 5, 3: 6, 4: 7}


def half_blocks(cut, rows, width, forth, back):
    return forth[forth.shape[0] - cut :, :width], back[back.shape[0] - (rows - cut) :, :width]


def ring_part_kernel(distance, cut, owners, *refs):
    if distance == HALF:
        far, ahead, behind = refs
        ahead[...] = far[:cut]
        behind[...] = far[cut:]
    elif distance == 0:
        own, forth, back, out = refs
        rows = own.shape[0]
        out[...] = added(own[...], forth[:rows], back[:rows]).astype(bf16)
    else:
        mine_ahead, mine_behind, forth, back, ahead, behind = refs
        if distance == HALF - 1:
            rows, width = mine_ahead.shape
            from_forth, from_back = half_blocks(cut, rows, width, forth, back)
            ahead[:cut] = added(mine_ahead[:cut], from_forth).astype(bf16)
            ahead[cut:] = mine_ahead[cut:]
            behind[:cut] = mine_behind[:cut]
            behind[cut:] = added(mine_behind[cut:], from_back).astype(bf16)
        else:
            ahead[...] = added(mine_ahead[...], forth[...]).astype(bf16)
            behind[...] = added(mine_behind[...], back[...]).astype(bf16)


def ring_part(blocks, owners, distance, cut, moved, gates=()):
    rows, columns = blocks.shape[1:]
    distances = (distance,) if distance in (0, HALF) else (distance, -distance)
    if distance == HALF:
        shapes = [(cut, columns), (rows - cut, columns)]
    else:
        shapes = [(rows, columns)] * len(distances)
    places = [PLACE[d] for d in distances]
    return call(
        functools.partial(ring_part_kernel, distance, cut),
        "ring_part",
        1,
        (*[blocks] * len(places), *moved),
        [
            pl.BlockSpec((None, rows, columns), lambda i, t, p=p: (t[p], 0, 0)) for p in places
        ]
        + [whole(value.shape) for value in moved],
        [(shape, bf16) for shape in shapes],
        [whole(shape) for shape in shapes],
        table=owners,
        gates=gates,
    )


def packed_kernel(cut, owners, mine_ahead, mine_behind, forth, back, far, ahead, behind):
    rows, width = mine_ahead.shape
    second = far.shape[1]
    ahead[:rows] = added(mine_ahead[...], forth[...]).astype(bf16)
    behind[:rows] = added(mine_behind[...], back[...]).astype(bf16)
    ahead[rows:, :second] = far[:cut]
    behind[rows:, :second] = far[cut:]
    if second < width:
        ahead[rows:, second:] = jnp.zeros((cut, width - second), bf16)
        behind[rows:, second:] = jnp.zeros((rows - cut, width - second), bf16)


def packed_step(blocks, others, owners, moved):
    if not on_ring():
        return ()
    rows, width = blocks.shape[1:]
    cut = upper_part(rows)
    shapes = [(rows + cut, width), (2 * rows - cut, width)]
    ahead, behind = call(
        functools.partial(packed_kernel, cut),
        "packed_part",
        1,
        (blocks, blocks, *moved, others),
        [
            pl.BlockSpec((None, rows, width), lambda i, t, p=PLACE[d]: (t[p], 0, 0))
            for d in (1, -1)
        ]
        + [whole(value.shape) for value in moved]
        + [pl.BlockSpec((None,) + others.shape[1:], lambda i, t: (t[PLACE[HALF]], 0, 0))],
        [(shape, bf16) for shape in shapes],
        [whole(shape) for shape in shapes],
        table=owners,
    )
    return ring_hop(ahead, 1), ring_hop(behind, -1)


def ring_step(blocks, owners, distance, moved=()):
    if not on_ring():
        return ()
    ahead, behind = ring_part(blocks, owners, distance, upper_part(blocks.shape[1]), moved)
    return ring_hop(ahead, 1), ring_hop(behind, -1)


def twin_block(owners, place, refs):
    kept, first, second = refs
    low = owners[place] < HALF
    return added(kept[...], jnp.where(low, first[...], second[...]))


def twin_kernel(distance, lag, cut, owners, *refs):
    width = refs[0].shape[-1]
    if distance == 0:
        own, forth, back, *twins = refs
        out, ahead, behind = twins[-3:]
        out[...] = added(own[...], forth[:, :width], back[:, :width]).astype(bf16)
        value_ahead = twin_block(owners, PLACE[lag], twins[0:3])
        value_behind = twin_block(owners, PLACE[-lag], twins[3:6])
        ahead[...] = added(value_ahead, forth[:, width:]).astype(bf16)
        behind[...] = added(value_behind, back[:, width:]).astype(bf16)
        return
    mine_ahead, mine_behind, forth, back, *twins = refs
    ahead, behind = twins[-2:]
    if distance == HALF - 1:
        from_forth, from_back = half_blocks(cut, mine_ahead.shape[0], width, forth, back)
        ahead[:cut, :width] = added(mine_ahead[:cut], from_forth).astype(bf16)
        ahead[cut:, :width] = mine_ahead[cut:]
        behind[:cut, :width] = mine_behind[:cut]
        behind[cut:, :width] = added(mine_behind[cut:], from_back).astype(bf16)
        value = twin_block(owners, PLACE[HALF], twins[0:3]).astype(bf16)
        ahead[:cut, width:] = value[:cut]
        ahead[cut:, width:] = jnp.zeros_like(value[cut:])
        behind[:cut, width:] = jnp.zeros_like(value[:cut])
        behind[cut:, width:] = value[cut:]
    else:
        ahead[:, :width] = added(mine_ahead[...], forth[:, :width]).astype(bf16)
        behind[:, :width] = added(mine_behind[...], back[:, :width]).astype(bf16)
        value_ahead = twin_block(owners, PLACE[lag], twins[0:3])
        value_behind = twin_block(owners, PLACE[-lag], twins[3:6])
        ahead[:, width:] = added(value_ahead, forth[:, width:]).astype(bf16)
        behind[:, width:] = added(value_behind, back[:, width:]).astype(bf16)


def twin_part(blocks, twin, owners, distance, moved):
    rows, width = blocks.shape[1:]
    span = twin[0].shape[2]
    lag = distance + 1
    mains = (distance, -distance) if distance else (0,)
    lags = (lag, -lag) if lag < HALF else (lag,)
    specs = [
        pl.BlockSpec((None, rows, width), lambda i, t, p=PLACE[d]: (t[p], 0, 0)) for d in mains
    ]
    specs += [whole(value.shape) for value in moved]
    for d in lags:
        p = PLACE[d]
        specs += [
            pl.BlockSpec((None, rows, span), lambda i, t, p=p: (t[p], 0, 0)),
            pl.BlockSpec(
                (None, rows, span), lambda i, t, p=p: (jnp.minimum(t[p], HALF - 1), 0, 0)
            ),
            pl.BlockSpec((None, rows, span), lambda i, t, p=p: (jnp.maximum(t[p] - HALF, 0), 0, 0)),
        ]
    if distance:
        shapes = [(rows, width + span)] * 2
    else:
        shapes = [(rows, width), (rows, span), (rows, span)]
    return call(
        functools.partial(twin_kernel, distance, lag, upper_part(rows)),
        "twin_part",
        1,
        (*[blocks] * len(mains), *moved, *twin * len(lags)),
        specs,
        [(shape, bf16) for shape in shapes],
        [whole(shape) for shape in shapes],
        table=owners,
    )


def twin_last_kernel(owners, forth, back, kept, first, second, out):
    value = twin_block(owners, PLACE[0], (kept, first, second))
    out[...] = added(value, forth[...], back[...]).astype(bf16)


def twin_last(twin, owners, moved):
    if not on_ring():
        blocks = added(twin[0], jnp.concatenate(twin[1:])).astype(bf16)
        return ring_end(blocks, owners, moved)
    rows, span = twin[0].shape[1:]
    block = (None, rows, span)
    return call(
        twin_last_kernel,
        "twin_last",
        1,
        (*moved, *twin),
        [whole((rows, span))] * 2
        + [
            pl.BlockSpec(block, lambda i, t: (t[0], 0, 0)),
            pl.BlockSpec(block, lambda i, t: (jnp.minimum(t[0], HALF - 1), 0, 0)),
            pl.BlockSpec(block, lambda i, t: (jnp.maximum(t[0] - HALF, 0), 0, 0)),
        ],
        [((rows, span), bf16)],
        [whole((rows, span))],
        table=owners,
    )[0]


def twin_step(blocks, twin, owners, distance, moved):
    if not on_ring():
        return ()
    ahead, behind = twin_part(blocks, twin, owners, distance, moved)
    return ring_hop(ahead, 1), ring_hop(behind, -1)


def twin_end(blocks, twin, owners, moved):
    if not on_ring():
        return ring_end(blocks, owners, moved), ()
    out, ahead, behind = twin_part(blocks, twin, owners, 0, moved)
    return out, (ring_hop(ahead, 1), ring_hop(behind, -1))


def ring_end(blocks, owners, moved):
    if not on_ring():
        return lax.psum_scatter(blocks, "fsdp", scatter_dimension=0, tiled=False)
    return ring_part(blocks, owners, 0, upper_part(blocks.shape[1]), moved)[0]


def halve_small(held, bit):
    me = lax.axis_index("fsdp")
    parts = held.reshape(2, bit, -1)
    high = (me & bit) != 0
    keep = jnp.where(high, parts[1], parts[0])
    give = jnp.where(high, parts[0], parts[1])
    pairs = [(i, i ^ bit) for i in range(lax.axis_size("fsdp"))]
    return keep + lax.ppermute(give, "fsdp", pairs)


def finish_small(held, bit):
    while bit:
        held = halve_small(held, bit)
        bit //= 2
    return held


def norm_stats(values):
    centre = values - jnp.mean(values, axis=-1, keepdims=True)
    scale = lax.rsqrt(jnp.mean(centre * centre, axis=-1, keepdims=True) + norm_eps)
    return centre * scale, scale


def norm_back(grad, unit, scale, gain):
    inner = grad * gain
    back = scale * (
        inner
        - jnp.mean(inner, axis=-1, keepdims=True)
        - unit * jnp.mean(inner * unit, axis=-1, keepdims=True)
    )
    return back, jnp.sum(grad * unit, axis=0), jnp.sum(grad, axis=0)


def across(left_op, right_op, left_dim, right_dim):
    return lax.dot_general(
        left_op, right_op, (((left_dim,), (right_dim,)), ((), ())), preferred_element_type=f32
    )


def diagonal_kept():
    shape = (QB, QB)
    return lax.broadcasted_iota(jnp.int32, shape, 0) <= lax.broadcasted_iota(jnp.int32, shape, 1)


def sorted_tile(table, ref, columns):
    groups = ref.shape[0] // GROUP
    return jnp.concatenate(
        [ref[pl.ds(pl.multiple_of(table[g], GROUP), GROUP), columns] for g in range(groups)],
        axis=0,
    )


def put_sorted(table, ref, columns, first, value):
    for j in range(value.shape[0] // GROUP):
        start = pl.multiple_of(table[first + j], GROUP)
        ref[pl.ds(start, GROUP), columns] = value[j * GROUP : (j + 1) * GROUP]


def split_heads(tiles, last):
    if last:
        return [(tiles[0][:, :HD], tiles[0][:, HD:], tiles[1][:, :HD])]
    return [tuple(t[:, w * HD : (w + 1) * HD] for t in tiles) for w in range(2)]


def pair_columns(pair, last):
    if last:
        start = SLOTS // 2 * 3 * PAIR
        return [slice(start, start + PAIR), slice(start + PAIR, start + 2 * PAIR)]
    return [pl.ds(pl.multiple_of(pair * 3 * PAIR + t * PAIR, PAIR), PAIR) for t in range(3)]


def attend_pair(pair, last, table, qkv_ref, out_ref, mass_ref):
    tiles = [sorted_tile(table, qkv_ref, c) for c in pair_columns(pair, last)]
    heads = split_heads(tiles, last)
    length = qkv_ref.shape[0]
    kept = diagonal_kept()
    ready = [(q * bf16(HD**-0.5), k, v.T) for q, k, v in heads]
    for i in range(length // QB):
        rows = slice(i * QB, (i + 1) * QB)
        outs = []
        for w, (queries, keys, values_t) in enumerate(ready):
            mine = queries[rows]
            diag = jnp.where(kept, across(keys[rows], mine, 1, 1), masked_low)
            peak = jnp.max(diag, axis=0, keepdims=True)
            if i:
                rest = across(keys[: i * QB], mine, 1, 1)
                peak = jnp.maximum(peak, jnp.max(rest, axis=0, keepdims=True))
            diag = jnp.exp(diag - peak)
            mass = jnp.sum(diag, axis=0, keepdims=True)
            out = across(values_t[:, rows], diag.astype(bf16), 1, 0)
            if i:
                rest = jnp.exp(rest - peak)
                mass = mass + jnp.sum(rest, axis=0, keepdims=True)
                out = out + across(values_t[:, : i * QB], rest.astype(bf16), 1, 0)
            outs.append(out / mass)
            mass_ref[0, w : w + 1, rows] = peak + jnp.log(mass)
        if last:
            outs.append(jnp.zeros_like(outs[0]))
        tile = jnp.concatenate(outs, axis=0).T.astype(bf16)
        put_sorted(table, out_ref, slice(None), 2 * i, tile)


def attend_kernel(table, qkv_ref, out_ref, mass_ref):
    pair = pl.program_id(0)
    final = pl.num_programs(0) - 1

    @pl.when(pair < final)
    def _():
        attend_pair(pair, False, table, qkv_ref, out_ref, mass_ref)

    @pl.when(pair == final)
    def _():
        mass_ref[...] = jnp.zeros_like(mass_ref)

        @pl.when(table[table.shape[0] - 1] == 0)
        def _():
            out_ref[...] = jnp.zeros_like(out_ref)

        @pl.when(table[table.shape[0] - 1] != 0)
        def _():
            attend_pair(pair, True, table, qkv_ref, out_ref, mass_ref)


def attend_back_pair(pair, last, table, qkv_ref, grad_ref, mass_ref, out_ref, acc):
    places = pair_columns(pair, last)
    heads = split_heads([sorted_tile(table, qkv_ref, c) for c in places], last)
    grads = sorted_tile(table, grad_ref, slice(None))
    length = qkv_ref.shape[0]
    kept = diagonal_kept()
    ready = [
        (q * bf16(HD**-0.5), k, k.T, v, grads[:, w * HD : (w + 1) * HD])
        for w, (q, k, v) in enumerate(heads)
    ]
    for i in range(length // QB):
        rows = slice(i * QB, (i + 1) * QB)
        query_tiles = []
        for w, (queries, keys, keys_t, values, grads_w) in enumerate(ready):
            mine = queries[rows]
            grad = grads_w[rows]
            mass = mass_ref[0, w : w + 1, rows]
            spans = [(rows, True)] + ([(slice(0, i * QB), False)] if i else [])
            probs, both, delta = [], [], None
            for span, diagonal in spans:
                scores = across(keys[span], mine, 1, 1)
                if diagonal:
                    scores = jnp.where(kept, scores, masked_low)
                prob = jnp.exp(scores - mass)
                prod = prob * across(values[span], grad, 1, 1)
                part = jnp.sum(prod, axis=0, keepdims=True)
                delta = part if delta is None else delta + part
                probs.append(prob)
                both.append(prod)
            query_t = None
            for (span, diagonal), prob, prod in zip(spans, probs, both):
                grad_scores = (prod - prob * delta).astype(bf16)
                part = across(keys_t[:, span], grad_scores, 1, 0)
                query_t = part if query_t is None else query_t + part
                key_part = across(grad_scores, mine, 1, 0)
                value_part = across(prob.astype(bf16), grad, 1, 0)
                if diagonal:
                    acc[2 * w, span, :] = key_part
                    acc[2 * w + 1, span, :] = value_part
                else:
                    acc[2 * w, span, :] += key_part
                    acc[2 * w + 1, span, :] += value_part
            query_tiles.append(query_t * HD**-0.5)
        if last:
            query_tiles.append(jnp.zeros_like(query_tiles[0]))
        tile = jnp.concatenate(query_tiles, axis=0).T
        if last:
            tile = jnp.concatenate([tile[:, :HD], jnp.zeros_like(tile[:, HD:])], axis=1)
        put_sorted(table, out_ref, places[0], 2 * i, tile.astype(bf16))
    if last:
        old = sorted_tile(table, out_ref, places[0])
        tile = jnp.concatenate([old[:, :HD], acc[0].astype(bf16)], axis=1)
        put_sorted(table, out_ref, places[0], 0, tile)
        tile = jnp.concatenate([acc[1].astype(bf16), jnp.zeros((length, HD), bf16)], axis=1)
        put_sorted(table, out_ref, places[1], 0, tile)
    else:
        for t in range(2):
            tile = jnp.concatenate([acc[t].astype(bf16), acc[2 + t].astype(bf16)], axis=1)
            put_sorted(table, out_ref, places[1 + t], 0, tile)


def attend_back_kernel(table, *refs):
    grad_refs, (qkv_ref, mass_ref, out_ref, acc, held) = refs[:4], refs[4:]
    pair = pl.program_id(0)
    final = pl.num_programs(0) - 1

    @pl.when(pair == 0)
    def _():
        span = SLOTS * HD
        rows = grad_refs[0].shape[0]
        for j, ref in enumerate(grad_refs):
            for p in range(span // PAIR):
                held[p, j * rows : (j + 1) * rows, :] = ref[:, p * PAIR : (p + 1) * PAIR]
            tail = jnp.concatenate([ref[:, span - HD :], jnp.zeros((rows, HD), bf16)], axis=1)
            held[span // PAIR, j * rows : (j + 1) * rows, :] = tail

    refs = (table, qkv_ref, held.at[pair], mass_ref, out_ref, acc)

    @pl.when(pair < final)
    def _():
        attend_back_pair(pair, False, *refs)

    @pl.when(pair == final)
    def _():
        @pl.when(table[table.shape[0] - 1] == 0)
        def _():
            for columns in pair_columns(pair, True):
                out_ref[:, columns] = jnp.zeros((out_ref.shape[0], PAIR), bf16)

        @pl.when(table[table.shape[0] - 1] != 0)
        def _():
            attend_back_pair(pair, True, *refs)


def attend(table, qkv, gates):
    length, columns = qkv.shape
    pairs = (SLOTS + 1) // 2
    return call(
        attend_kernel,
        "attend",
        pairs,
        (qkv,),
        [whole((length, columns))],
        [((length, pairs * PAIR), bf16), ((pairs, 8, length), f32)],
        [
            pl.BlockSpec((length, PAIR), lambda p, t: (0, p)),
            pl.BlockSpec((1, 8, length), lambda p, t: (p, 0, 0)),
        ],
        table=table,
        gates=gates,
    )


def attend_back(table, qkv, grads, mass, gates):
    length, columns = qkv.shape
    pairs = (SLOTS + 1) // 2
    return call(
        attend_back_kernel,
        "attend_back",
        pairs,
        (*grads, qkv, mass),
        [whole(grad.shape) for grad in grads]
        + [whole((length, columns)), pl.BlockSpec((1, 8, length), lambda p, t: (p, 0, 0))],
        [((length, columns), bf16)],
        [whole((length, columns))],
        [pltpu.VMEM((4, length, HD), f32), pltpu.VMEM((pairs, length, PAIR), bf16)],
        table,
        gates,
    )[0]


def whole(shape):
    return pl.BlockSpec(shape, lambda *_: (0,) * len(shape))


def rows_spec(rows, columns):
    return pl.BlockSpec((rows, columns), lambda i, *_: (i, 0))


def call(kernel, name, grid, operands, specs, outs, out_specs, scratch=(), table=None, gates=()):
    tables = () if table is None else (table,)
    first = len(tables) + len(operands)
    count = len(gates)

    def body(*refs):
        kernel(*refs[:first], *refs[first + count :])

    return pl.pallas_call(
        body,
        grid_spec=pltpu.PrefetchScalarGridSpec(
            num_scalar_prefetch=len(tables),
            grid=(grid,),
            in_specs=list(specs) + [pl.BlockSpec(memory_space=pl.ANY)] * count,
            out_specs=out_specs,
            scratch_shapes=list(scratch),
        ),
        out_shape=[jax.ShapeDtypeStruct(shape, kind) for shape, kind in outs],
        compiler_params=pltpu.CompilerParams(vmem_limit_bytes=VMEM_LIMIT),
        cost_estimate=LIGHT,
        name=name,
    )(*tables, *operands, *gates)


def pick_block(refs, held):
    for j, ref in enumerate(refs):

        @pl.when(pl.program_id(0) == j)
        def _(ref=ref):
            held[...] = ref[...]


def norm_mixed_kernel(*refs):
    blocks, (gain, shift, weights, bias, normed, mixed, held) = refs[:4], refs[4:]
    pick_block(blocks, held)
    unit, _ = norm_stats(held[...].astype(f32))
    low = (unit * gain[...] + shift[...]).astype(bf16)
    normed[...] = low
    mixed[...] = (product(low, weights[...]) + bias[...]).astype(bf16)


def norm_mixed(blocks, gain, shift, weights, bias):
    count, width = blocks[0].shape
    mixed_width = weights.shape[1]
    length = count * len(blocks)
    return call(
        norm_mixed_kernel,
        "norm_mixed",
        len(blocks),
        (*blocks, gain[None], shift[None], weights, bias),
        [whole((count, width))] * len(blocks)
        + [whole((1, width))] * 2
        + [whole(weights.shape), whole((1, mixed_width))],
        [((length, width), bf16), ((length, mixed_width), bf16)],
        [rows_spec(count, width), rows_spec(count, mixed_width)],
        [pltpu.VMEM((count, width), bf16)],
    )


def join_kernel(table, *refs):
    pieces, out, sems, last_sem = refs[:4], refs[4], refs[5], refs[6]
    step, span = BASE * HD, SLOTS * HD
    width = out.shape[1]
    rest = span - step
    last = len(pieces) - 1

    def copies(j):
        start = pl.multiple_of(table[j] * step, PAIR)
        main = pltpu.make_async_copy(
            pieces[j].at[:, pl.ds(0, step)], out.at[:, pl.ds(start, step)], sems.at[j]
        )
        tail = pltpu.make_async_copy(
            pieces[j].at[:, pl.ds(step, rest)], out.at[:, pl.ds(width - rest, rest)], last_sem.at[0]
        )
        return main, tail

    for j in range(len(pieces)):
        main, tail = copies(j)
        main.start()

        @pl.when(table[j] == last)
        def _(tail=tail):
            tail.start()

    for j in range(len(pieces)):
        main, tail = copies(j)
        main.wait()

        @pl.when(table[j] == last)
        def _(tail=tail):
            tail.wait()


def join_windows(table, pieces, width):
    rows = pieces[0].shape[0]
    return call(
        join_kernel,
        "join_windows",
        1,
        pieces,
        [pl.BlockSpec(memory_space=pl.ANY)] * len(pieces),
        [((rows, width), pieces[0].dtype)],
        [whole((rows, width))],
        [pltpu.SemaphoreType.DMA((len(pieces),)), pltpu.SemaphoreType.DMA((1,))],
        table,
    )[0]


def attn_out_kernel(table, *refs):
    pieces, rest = refs[:4], refs[4:]
    weights, tokens, bias, gain, shift, middle, normed, attended = rest
    step, span = BASE * HD, SLOTS * HD
    width = attended.shape[1]
    for j, piece in enumerate(pieces):
        start = pl.multiple_of(table[j] * step, PAIR)
        attended[:, pl.ds(start, step)] = piece[:, :step]

        @pl.when(table[j] == len(pieces) - 1)
        def _(piece=piece):
            attended[:, width - (span - step) :] = piece[:, step:]

    value = tokens[...].astype(f32) + product(attended[...], weights[...]) + bias[...]
    middle[...] = value
    unit, _ = norm_stats(value)
    normed[...] = (unit * gain[...] + shift[...]).astype(bf16)


def attn_out(table, pieces, weights, tokens, bias, gain, shift):
    count, width = tokens.shape
    return call(
        attn_out_kernel,
        "attn_out",
        1,
        (*pieces, weights, tokens, bias[None], gain[None], shift[None]),
        [whole(piece.shape) for piece in pieces]
        + [whole(weights.shape), whole((count, width))]
        + [whole((1, width))] * 3,
        [((count, width), f32), ((count, width), bf16), ((count, width), bf16)],
        [whole((count, width))] * 3,
        table=table,
    )


def up_kernel(*refs):
    blocks, (weights, bias, activated, slope, normed, held) = refs[:4], refs[4:]
    pick_block(blocks, held)
    normed[...] = held[...]
    before = product(held[...], weights[...]) + bias[...]
    square = before * before
    inner = jnp.tanh(before * (0.7978845608028654 + 0.7978845608028654 * 0.044715 * square))
    half = 0.5 * (1.0 + inner)
    activated[...] = (before * half).astype(bf16)
    slope[...] = (
        half
        + 0.5
        * before
        * (1.0 - inner * inner)
        * (0.7978845608028654 + 3 * 0.7978845608028654 * 0.044715 * square)
    ).astype(bf16)


def feed_up(blocks, weights, bias):
    count, width = blocks[0].shape
    units = weights.shape[1]
    length = count * len(blocks)
    return call(
        up_kernel,
        "feed_up",
        len(blocks),
        (*blocks, weights, bias[None]),
        [whole((count, width))] * len(blocks) + [whole(weights.shape), whole((1, units))],
        [((length, units), bf16), ((length, units), bf16), ((length, width), bf16)],
        [rows_spec(count, units), rows_spec(count, units), rows_spec(count, width)],
        [pltpu.VMEM((count, width), bf16)],
    )


def back_kernel(*refs):
    blocks, (down, slope, low, sums, held) = refs[:4], refs[4:]
    pick_block(blocks, held)
    value = (back_product(held[...], down[...]) * slope[...].astype(f32)).astype(bf16)
    low[...] = value

    @pl.when(pl.program_id(0) == 0)
    def _():
        sums[...] = jnp.zeros_like(sums)

    sums[...] += jnp.sum(value.astype(f32), axis=0, keepdims=True)


def feed_back(blocks, down, slope, gates):
    count, width = blocks[0].shape
    units = slope.shape[1]
    length = count * len(blocks)
    return call(
        back_kernel,
        "feed_back",
        len(blocks),
        (*blocks, down, slope),
        [whole((count, width))] * len(blocks) + [whole(down.shape), rows_spec(count, units)],
        [((length, units), bf16), ((1, units), f32)],
        [rows_spec(count, units), whole((1, units))],
        [pltpu.VMEM((count, width), bf16)],
        gates=gates,
    )


def plain_back_kernel(left, right, keep, give):
    value = back_product(left[...], right[...]).astype(bf16)
    first = pl.program_id(0) < pl.num_programs(0) // 2

    @pl.when(first)
    def _():
        keep[...] = value

    @pl.when(jnp.logical_not(first))
    def _():
        give[...] = value


def plain_back(left, right, name):
    length, inner = left.shape
    width = right.shape[0]
    steps = length // QB
    half = steps // 2
    return call(
        plain_back_kernel,
        name,
        steps,
        (left, right),
        [rows_spec(QB, inner), whole(right.shape)],
        [((length // 2, width), bf16)] * 2,
        [
            pl.BlockSpec((QB, width), lambda i: (jnp.minimum(i, half - 1), 0)),
            pl.BlockSpec((QB, width), lambda i: (jnp.maximum(i - half, 0), 0)),
        ],
    )


VECTOR_ROWS = 8
FC_START = 2 * PAIR


def attn_block_kernel(place, qkv, out_weights, *refs):
    vectors, bias_fc, block = refs[:VECTOR_ROWS], refs[VECTOR_ROWS], refs[VECTOR_ROWS + 1]
    step, span = BASE * HD, SLOTS * HD
    width = out_weights.shape[1]
    rows = qkv.shape[0]
    parts = []
    for t in range(3):
        skip = t * width % PAIR
        start = pl.multiple_of(place[0] * step + (t * width - skip), PAIR)
        parts.append(qkv[:, pl.ds(start, span + skip)][:, skip:])
    for p in range(SLOTS // 2):
        for t in range(3):
            first = (3 * p + t) * PAIR
            block[:rows, first : first + PAIR] = parts[t][:, p * PAIR : (p + 1) * PAIR]
    rest = [part[:, (SLOTS - 1) * HD :] for part in parts] + [jnp.zeros((rows, HD), bf16)]
    first = 3 * (SLOTS // 2) * PAIR
    for p in range(2):
        block[:rows, first + p * PAIR : first + (p + 1) * PAIR] = jnp.concatenate(
            rest[2 * p : 2 * p + 2], axis=1
        )
    start = pl.multiple_of(place[0] * step, PAIR)
    block[:rows, first + 2 * PAIR :] = out_weights[:, pl.ds(start, span)]
    block[rows:, :] = jnp.zeros((VECTOR_ROWS, block.shape[1]), bf16)
    lines = jnp.stack([vector[...].astype(f32) for vector in vectors])
    block[rows:, : lines.shape[1]] = lines.astype(bf16)
    units = bias_fc.shape[0]
    line = jnp.broadcast_to(bias_fc[...].astype(f32)[None], (VECTOR_ROWS, units))
    block[rows:, FC_START : FC_START + units] = line.astype(bf16)


def form_attn_block(place, qkv, out_weights, vectors, bias_fc):
    rows = qkv.shape[0]
    columns = 3 * (SLOTS // 2) * PAIR + 2 * PAIR + SLOTS * HD
    vectors = [*vectors, bias_fc]
    return call(
        attn_block_kernel,
        "form_attn_block",
        1,
        (qkv, out_weights, *vectors),
        [whole(value.shape) for value in (qkv, out_weights, *vectors)],
        [((rows + VECTOR_ROWS, columns), bf16)],
        [whole((rows + VECTOR_ROWS, columns))],
        table=place,
    )[0]


def whole_rows_kernel(table, *refs):
    pieces, out, held = refs[:4], refs[4], refs[5]
    pick_block(pieces, held)
    out[...] = held[...].astype(f32)


def whole_rows(table, pieces, gates):
    rows, width = pieces[0].shape
    return call(
        whole_rows_kernel,
        "whole_rows",
        len(pieces),
        pieces,
        [whole((rows, width))] * len(pieces),
        [((len(pieces), rows, width), f32)],
        [pl.BlockSpec((None, rows, width), lambda i, t: (t[i], 0, 0))],
        [pltpu.VMEM((rows, width), bf16)],
        table,
        gates,
    )[0].reshape(-1, width)


def put_windows(table, held, outs):
    for j in range(2 * len(outs)):
        start = pl.multiple_of(table[j] * BASE * HD, PAIR)
        outs[j // 2][j % 2] = held[:, pl.ds(start, SLOTS * HD)]


def norm_two_kernel(table, *refs):
    kept, far, middle, grad_out, gain, weights, grad_middle, low, keep, give, sums, held = refs
    grad = kept[...] + far[...].astype(f32)
    unit, scale = norm_stats(middle[...])
    back, grad_gain, grad_shift = norm_back(grad, unit, scale, gain[...])
    out = grad_out[...].astype(f32)
    value = out + back
    grad_middle[...] = value
    value_low = value.astype(bf16)
    low[...] = value_low
    held[...] = back_product(value_low, weights[...]).astype(bf16)
    put_windows(table, held, (keep, give))
    sums[0:1, :] = grad_gain[None]
    sums[1:2, :] = grad_shift[None]
    sums[2:3, :] = jnp.sum(value_low.astype(f32), axis=0, keepdims=True)
    sums[3:4, :] = jnp.sum(out, axis=0, keepdims=True)


def norm_two_back(table, kept, far, middle, grad_out, gain, weights, gates):
    count, width = middle.shape
    half = (2, count, SLOTS * HD)
    return call(
        norm_two_kernel,
        "norm_two_back",
        1,
        (kept, far, middle, grad_out, gain[None], weights),
        [whole((count, width))] * 4 + [whole((1, width)), whole(weights.shape)],
        [
            ((count, width), f32),
            ((count, width), bf16),
            (half, bf16),
            (half, bf16),
            ((4, width), f32),
        ],
        [
            whole((count, width)),
            whole((count, width)),
            whole(half),
            whole(half),
            whole((4, width)),
        ],
        [pltpu.VMEM((count, width), bf16)],
        table,
        gates=gates,
    )


def norm_one_kernel(kept, far, tokens, grad_middle, gain, grad_tokens, sums):
    grad = kept[...] + far[...].astype(f32)
    unit, scale = norm_stats(tokens[...].astype(f32))
    back, grad_gain, grad_shift = norm_back(grad, unit, scale, gain[...])
    grad_tokens[...] = grad_middle[...] + back
    sums[0:1, :] = grad_gain[None]
    sums[1:2, :] = grad_shift[None]


def norm_one_back(kept, far, tokens, grad_middle, gain, gates):
    shape = kept.shape
    return call(
        norm_one_kernel,
        "norm_one_back",
        1,
        (kept, far, tokens, grad_middle, gain[None]),
        [whole(shape)] * 4 + [whole((1, shape[1]))],
        [(shape, f32), ((2, shape[1]), f32)],
        [whole(shape), whole((2, shape[1]))],
        gates=gates,
    )


def out_grad_kernel(table, attended, low, keep, give, held):
    held[...] = outer_sum(attended[...], low[...]).astype(bf16)
    put_windows(table, held, (keep, give))


def out_weight_grad(table, attended, low, gates):
    count, width = attended.shape
    half = (2, width, SLOTS * HD)
    return call(
        out_grad_kernel,
        "out_weight_grad",
        1,
        (attended, low),
        [whole((count, width))] * 2,
        [(half, bf16)] * 2,
        [whole(half)] * 2,
        [pltpu.VMEM((width, width), bf16)],
        table,
        gates=gates,
    )


def whole_fc_kernel(table, *refs):
    pieces, out, held, sems = refs[:4], refs[4], refs[5], refs[6]
    copies = [
        pltpu.make_async_copy(piece, held.at[table[j]], sems.at[j])
        for j, piece in enumerate(pieces)
    ]
    for copy in copies:
        copy.start()
    for copy in copies:
        copy.wait()
    ranks = len(pieces)
    units = pieces[0].shape[0]
    for r in range(ranks):
        for i in range(pieces[0].shape[1] // units):
            first = (i * ranks + r) * units
            out[:, first : first + units] = held[r, :, i * units : (i + 1) * units].astype(f32)


def whole_fc(table, pieces, gates):
    rows, width = pieces[0].shape
    ranks = len(pieces)
    return call(
        whole_fc_kernel,
        "whole_fc",
        1,
        pieces,
        [pl.BlockSpec(memory_space=pl.ANY)] * ranks,
        [((rows, ranks * width), f32)],
        [whole((rows, ranks * width))],
        [pltpu.VMEM((ranks, rows, width), bf16), pltpu.SemaphoreType.DMA((ranks,))],
        table,
        gates,
    )[0]


def whole_qkv_kernel(table, *refs):
    pieces, out, held, sems = refs[:4], refs[4], refs[5], refs[6]
    copies = [
        pltpu.make_async_copy(piece, held.at[table[j]], sems.at[j])
        for j, piece in enumerate(pieces)
    ]
    for copy in copies:
        copy.start()
    for copy in copies:
        copy.wait()
    width = out.shape[1] // 3
    for rank in range(len(pieces)):
        for part in range(3):
            start = part * width + rank * BASE * HD
            for p in range(SLOTS // 2):
                tile = held[rank, :, (3 * p + part) * PAIR : (3 * p + part + 1) * PAIR]
                out[:, start + p * PAIR : start + (p + 1) * PAIR] = tile.astype(f32)
            if rank == len(pieces) - 1:
                first = 3 * (SLOTS // 2) * PAIR + part * HD
                tile = held[rank, :, first : first + HD]
                out[:, start + BASE * HD : start + SLOTS * HD] = tile.astype(f32)


def whole_qkv(table, pieces, width):
    rows = pieces[0].shape[0]
    return call(
        whole_qkv_kernel,
        "whole_qkv",
        1,
        pieces,
        [pl.BlockSpec(memory_space=pl.ANY)] * len(pieces),
        [((rows, 3 * width), f32)],
        [whole((rows, 3 * width))],
        [
            pltpu.VMEM((len(pieces),) + pieces[0].shape, bf16),
            pltpu.SemaphoreType.DMA((len(pieces),)),
        ],
        table,
    )[0]


def to_pairs(parts):
    pieces = []
    for p in range(SLOTS // 2):
        pieces += [part[:, p * PAIR : (p + 1) * PAIR] for part in parts]
    pieces += [part[:, (SLOTS - 1) * HD :] for part in parts]
    pieces.append(jnp.zeros((parts[0].shape[0], HD), parts[0].dtype))
    return jnp.concatenate(pieces, axis=1)


def from_pairs(matrix, part, last):
    pieces = [
        matrix[:, (3 * p + part) * PAIR : (3 * p + part + 1) * PAIR] for p in range(SLOTS // 2)
    ]
    if last:
        start = 3 * (SLOTS // 2) * PAIR + part * HD
        pieces.append(matrix[:, start : start + HD])
    return pieces


def per_device(
    tokens_in,
    group_order,
    out_grad,
    w_qkv,
    w_attn_out,
    b_query,
    b_value,
    b_attn_out,
    w_fc,
    w_proj,
    b_fc,
    b_proj,
    ln1_gain,
    ln1_bias,
    ln2_gain,
    ln2_bias,
):
    ctx = lax.axis_size("ctx")
    shards = lax.axis_size("fsdp")
    rank = lax.axis_index("ctx")
    tokens = tokens_in[0].astype(f32)
    count, width = tokens.shape
    span = SLOTS * HD
    step = BASE * HD
    mixed_width = (3 * span + PAIR - 1) // PAIR * PAIR
    attn_width = mixed_width + span
    shard_rows = w_qkv.shape[0]
    unit_rows = w_proj.shape[0] // ctx
    peers = [rank ^ bit for bit in PEERS]
    owners = ring_owners() if on_ring() else None

    always = group_order[0] >= 0
    peer_table = jnp.stack(peers).astype(jnp.int32)

    slots = jnp.argsort(group_order).astype(jnp.int32)
    place = jnp.take(jnp.asarray(np.argsort(np.array(PEERS)).astype(np.int32)), (slots // 2) ^ rank)
    slot_rows = (place * 2 + slots % 2) * GROUP
    table = jnp.concatenate([slot_rows, (rank == ctx - 1).astype(jnp.int32)[None]])

    attn_block = form_attn_block(
        rank[None].astype(jnp.int32),
        w_qkv,
        w_attn_out,
        (b_query, b_value, b_attn_out, b_proj, ln1_gain, ln1_bias, ln2_gain, ln2_bias),
        b_fc,
    )
    own_tokens = tokens_in[0]
    own_grad = out_grad[0]
    attn_gather = Gather(attn_block)
    attn_gather.hop()
    w_fc = after(w_fc, attn_block)
    fc_block = jnp.concatenate(
        [
            lax.dynamic_slice(
                w_fc, (0, (i * ctx + rank) * unit_rows), (shard_rows, unit_rows)
            )
            for i in range(shards)
        ],
        axis=1,
    )
    proj_block = lax.dynamic_slice(w_proj, (rank * unit_rows, 0), (unit_rows, width))
    feed_block = jnp.concatenate([fc_block, proj_block])
    token_blocks = gather_ctx(own_tokens)
    grad_blocks = gather_ctx(after(own_grad, token_blocks[1]))
    attn_gather.hop()
    attn_gather.hop(feed_block)
    feed_gather = Gather(after(feed_block, *attn_gather.arrived()))
    feed_gather.hop()
    attn_gather.hop()

    qkv_weights, out_columns, small = attn_gather.result(
        owners,
        (
            (0, mixed_width, 0, shard_rows),
            (mixed_width, span, 0, shard_rows),
            (0, attn_width, shard_rows, VECTOR_ROWS),
        ),
        feed_gather.arrived(),
    )
    qkv_weights = qkv_weights.reshape(width, mixed_width)
    small = small.astype(f32)
    bias_q, bias_v, bias_o, bias_p, gain_one, shift_one, gain_two, shift_two = [
        small[:, t, :shard_rows].reshape(-1) for t in range(VECTOR_ROWS)
    ]
    bias_fc = lax.dynamic_index_in_dim(
        small[:, 0, FC_START : FC_START + ctx * unit_rows].reshape(shards, ctx, unit_rows),
        rank,
        1,
        False,
    ).reshape(-1)

    def my_bias(vector):
        return lax.dynamic_slice(vector, (rank * step,), (span,))[None]

    bias_mixed = to_pairs([my_bias(bias_q), jnp.zeros((1, span), f32), my_bias(bias_v)])
    normed_all, mixed = norm_mixed(
        [after(token_blocks[0], grad_blocks[3])] + token_blocks[1:],
        gain_one,
        shift_one,
        qkv_weights,
        bias_mixed,
    )
    attended_mine, mass = attend(table, mixed, feed_gather.arrived())
    feed_gather.hop()
    out_blocks = gather_ctx(out_columns.reshape(width, span))
    out_weights = join_windows(peer_table, out_blocks, width)
    pieces = exchange_far(
        *exchange_near(*halves(after(row_major(attended_mine[:, :span]), out_blocks[1])))
    )
    middle, normed_two, attended = attn_out(
        peer_table,
        pieces,
        out_weights,
        after(own_tokens, *feed_gather.arrived()),
        bias_o,
        gain_two,
        shift_two,
    )
    feed_gather.hop()

    normed_far = ctx_swap(normed_two, 2)
    normed_blocks = [
        normed_two,
        normed_far,
        ctx_swap(normed_two, 1),
    ]
    feed_gather.hop()
    normed_blocks.append(ctx_swap(after(normed_far, *feed_gather.arrived()), 1))
    grad_all = row_major(jnp.concatenate([after(grad_blocks[0], normed_two)] + grad_blocks[1:]))
    fc_weights, proj_weights = feed_gather.result(
        owners, ((0, width, 0, shard_rows), (0, width, shard_rows, unit_rows))
    )
    fc_weights = fc_weights.reshape(width, -1)
    proj_weights = proj_weights.reshape(-1, width)
    activated, slope, normed_two_all = feed_up(
        [after(normed_blocks[0], grad_all)] + normed_blocks[1:], fc_weights, bias_fc
    )

    grad_proj = row_major(outer_sum(activated, grad_all).astype(bf16))
    proj_blocks = grad_proj.reshape(shards, unit_rows, width)

    def slot_one():
        moved = ring_step(proj_blocks, owners, 4)
        return moved, feed_back(grad_blocks, proj_weights, slope, ())

    proj_moved, (before_low, grad_bias_fc) = slot(always, slot_one)

    def slot_two():
        moved = ring_step(proj_blocks, owners, 3, proj_moved)

        def beside():
            keep, give = plain_back(before_low, fc_weights, "feed_back_two")
            return keep, ctx_swap(give, 1)

        return moved, slot(always, beside)

    proj_moved, (keep_two, got_two) = slot(always, slot_two)

    def slot_three():
        moved = ring_step(proj_blocks, owners, 2, proj_moved)

        def beside():
            kept, onward = pair_add(keep_two, got_two)
            grad_fc = row_major(outer_sum(normed_two_all, before_low).astype(bf16))
            branch = row_major(product(activated, proj_weights).astype(bf16))
            return kept, ctx_swap(onward, 2), grad_fc, halves(branch)

        return moved, slot(always, beside)

    proj_moved, (kept_two, far_two, grad_fc, branch_halves) = slot(always, slot_three)
    fc_blocks = grad_fc.reshape(shards, shard_rows, shards * unit_rows)

    def slot_four():
        moved = packed_step(proj_blocks, fc_blocks, owners, proj_moved)

        def beside():
            grad_middle, low, keep, give, sums = norm_two_back(
                peer_table, kept_two, far_two, middle, own_grad, gain_two, out_weights, ()
            )
            near = exchange_near(keep.reshape(-1, span), give.reshape(-1, span))
            out_pair = out_weight_grad(peer_table, attended, low, ())
            return grad_middle, low, sums, exchange_far(*near), out_pair

        return moved, slot(always, beside)

    proj_moved, (grad_middle, middle_low, sums_two, heads, out_pair) = slot(
        always, slot_four
    )
    out_keep, out_give = [value.reshape(-1, span) for value in out_pair]

    def slot_five():
        moved = ring_step(fc_blocks, owners, 3, proj_moved)

        def beside():
            shard = ring_end(proj_blocks, owners, proj_moved)
            far, near, got = ctx_swap(shard, 2), ctx_swap(shard, 1), ctx_swap(out_give, 1)
            return [shard, far, near], got, attend_back(table, mixed, heads, mass, ())

        return moved, slot(always, beside)

    fc_moved, (proj_pieces, got_out, grad_mixed) = slot(always, slot_five)

    def slot_six():
        moved = ring_step(fc_blocks, owners, 2, fc_moved)

        def beside():
            last = ctx_swap(proj_pieces[1], 1)
            kept, first, second = pair_split(out_keep, got_out)
            far = ctx_swap(first, 2)
            grad_qkv = row_major(outer_sum(normed_all, grad_mixed).astype(bf16))
            return last, kept, second, far, grad_qkv

        return moved, slot(always, beside)

    fc_moved, (proj_last, kept_out, onward_out, far_first, grad_qkv) = slot(always, slot_six)
    proj_pieces = proj_pieces + [proj_last]
    qkv_blocks = grad_qkv.reshape(shards, shard_rows, mixed_width)

    def partial_table():
        bias_sums = jnp.sum(grad_mixed.astype(f32), axis=0, keepdims=True)

        def all_heads(part):
            mine = jnp.concatenate(from_pairs(bias_sums, part, True), axis=1)
            return lax.dynamic_update_slice(jnp.zeros((1, width), f32), mine, (0, rank * step))

        whole_bias_fc = lax.dynamic_update_slice(
            jnp.zeros((shards, ctx, unit_rows), f32),
            grad_bias_fc.reshape(shards, 1, unit_rows),
            (0, rank, 0),
        )
        return [
            value.reshape(shards, -1)
            for value in (all_heads(0), all_heads(2), *sums_two, whole_bias_fc)
        ]

    def whole_table(part, sums):
        one = [value.reshape(shards, -1) for value in sums]
        query, value, gain_two_sum, shift_two_sum, out, down, units = part
        return jnp.concatenate(
            [query, value, out, down, *one, gain_two_sum, shift_two_sum, units], axis=1
        )

    def slot_seven():
        moved = packed_step(fc_blocks, qkv_blocks, owners, fc_moved)

        def beside():
            far = ctx_swap(onward_out, 2)

            def inmost():
                keep, give = plain_back(grad_mixed, qkv_weights, "mixed_back")
                return pair_add(keep, ctx_swap(give, 1))

            return far, slot(always, inmost)

        return moved, slot(always, beside)

    fc_moved, (far_second, (kept_one, onward_one)) = slot(always, slot_seven)

    twin = [
        value.reshape(-1, shard_rows, span) for value in (kept_out, far_first, far_second)
    ]

    def slot_eight():
        qkv_next = twin_step(qkv_blocks, twin, owners, 3, fc_moved)

        def beside():
            far = ctx_swap(onward_one, 2)
            got = ctx_swap(branch_halves[1], 1)

            def inmost():
                shard = ring_end(fc_blocks, owners, fc_moved)
                return shard, partial_table(), whole_rows(peer_table, proj_pieces, ())

            return far, got, slot(always, inmost)

        return qkv_next, slot(always, beside)

    qkv_moved, (far_one, got_branch, (shard_fc, table_part, grad_w_proj)) = slot(
        always, slot_eight
    )

    def slot_nine():
        qkv_next = twin_step(qkv_blocks, twin, owners, 2, qkv_moved)

        def beside():
            far, near = ctx_swap(shard_fc, 2), ctx_swap(shard_fc, 1)

            def inmost():
                kept, onward = pair_add(branch_halves[0], got_branch)
                back, sums = norm_one_back(
                    kept_one, far_one, own_tokens, grad_middle, gain_one, ()
                )
                return kept, onward, back, whole_table(table_part, sums)

            return [shard_fc, far, near], slot(always, inmost)

        return qkv_next, slot(always, beside)

    qkv_moved, (fc_pieces, beside_nine) = slot(always, slot_nine)
    kept_branch, onward_branch, grad_tokens, small = beside_nine

    def slot_ten():
        held = halve_small(small, shards // 2)
        qkv_next = twin_step(qkv_blocks, twin, owners, 1, qkv_moved)
        far, last = ctx_swap(onward_branch, 2), ctx_swap(fc_pieces[1], 1)
        return qkv_next, held, far, last

    qkv_moved, held, far_branch, fc_last = slot(always, slot_ten)

    def slot_eleven():
        shard_qkv, out_next = twin_end(qkv_blocks, twin, owners, qkv_moved)
        far, near = ctx_swap(shard_qkv, 2), ctx_swap(shard_qkv, 1)
        next_held = halve_small(held, shards // 4)

        def beside():
            out = (middle + added(kept_branch, far_branch) + bias_p).astype(bf16)[None]
            return whole_fc(peer_table, fc_pieces + [fc_last], ()), out

        return [shard_qkv, far, near], out_next, next_held, slot(always, beside)

    qkv_pieces, out_moved, held, (grad_w_fc, tokens_out) = slot(always, slot_eleven)
    def slot_twelve():
        shard_out = twin_last(twin, owners, out_moved)
        swaps = [ctx_swap(shard_out, 2), ctx_swap(shard_out, 1)]
        return [shard_out, *swaps], ctx_swap(qkv_pieces[1], 1), halve_small(held, shards // 8)

    out_pieces, qkv_last, held = slot(always, slot_twelve)
    held = finish_small(held, shards // 16)

    def slot_thirteen():
        last = ctx_swap(out_pieces[1], 1)
        total = held[0] + ctx_swap(held[0], 1)
        return last, total, slot(
            always, lambda: whole_qkv(peer_table, qkv_pieces + [qkv_last], width)
        )

    out_last, summed, grad_w_qkv = slot(always, slot_thirteen)
    summed = summed + ctx_swap(summed, 2)
    whole_attn_out = join_windows(peer_table, out_pieces + [out_last], width).astype(f32)
    shares = [summed[t * shard_rows : (t + 1) * shard_rows] for t in range(8)]
    share_fc = summed[8 * shard_rows :]
    grad_tokens = grad_tokens[None]

    return (
        tokens_out,
        grad_tokens,
        grad_w_qkv,
        whole_attn_out,
        shares[0],
        shares[1],
        shares[2],
        grad_w_fc,
        grad_w_proj,
        share_fc,
        shares[3],
        shares[4],
        shares[5],
        shares[6],
        shares[7],
    )


def solution(mesh):
    placed = (
        P("fsdp", "ctx", None),
        P(),
        P("fsdp", "ctx", None),
        P("fsdp", None),
        P("fsdp", None),
        P("fsdp"),
        P("fsdp"),
        P("fsdp"),
        P("fsdp", None),
        P("fsdp", None),
        P("fsdp"),
        P("fsdp"),
        P("fsdp"),
        P("fsdp"),
        P("fsdp"),
        P("fsdp"),
    )
    return jax.shard_map(
        per_device,
        mesh=mesh,
        in_specs=placed,
        out_specs=(
            P("fsdp", "ctx", None),
            P("fsdp", "ctx", None),
            P("fsdp", None),
            P("fsdp", None),
            P("fsdp"),
            P("fsdp"),
            P("fsdp"),
            P("fsdp", None),
            P("fsdp", None),
            P("fsdp"),
            P("fsdp"),
            P("fsdp"),
            P("fsdp"),
            P("fsdp"),
            P("fsdp"),
        ),
        check_vma=False,
    )
```

```python
import functools

import jax
import jax.numpy as jnp
import numpy as np
from jax import lax
from jax.experimental import pallas as pl
from jax.experimental.layout import Layout, with_layout_constraint
from jax.experimental.pallas import tpu as pltpu
from jax.sharding import PartitionSpec as P

H = 25
HD = 64
GROUP = 128
QB = 256
PAIR = 2 * HD
RANKS = 4
BASE = H // RANKS
SLOTS = H - (RANKS - 1) * BASE
norm_eps = 1e-05
masked_low = -1e30
LIGHT = pl.CostEstimate(flops=1 << 20, transcendentals=0, bytes_accessed=1 << 16)
VMEM_LIMIT = 40 << 20
f32 = jnp.float32
bf16 = jnp.bfloat16


def outer_sum(left_op, right_op):
    return lax.dot_general(
        left_op, right_op, (((0,), (0,)), ((), ())), preferred_element_type=f32
    )


def back_product(left_op, right_op):
    return lax.dot_general(
        left_op, right_op, (((1,), (1,)), ((), ())), preferred_element_type=f32
    )


def product(left_op, right_op):
    return jnp.dot(left_op, right_op, preferred_element_type=f32)


def added(*terms):
    total = terms[0].astype(f32)
    for term in terms[1:]:
        total = total + term.astype(f32)
    return total


def row_major(matrix):
    return with_layout_constraint(matrix, Layout(major_to_minor=tuple(range(matrix.ndim))))


def slot(always, step):
    empty = jax.eval_shape(step)
    return lax.cond(
        always,
        step,
        lambda: jax.tree.map(lambda leaf: jnp.zeros(leaf.shape, leaf.dtype), empty),
    )


def after(value, *others):
    return lax.optimization_barrier((value,) + others)[0]


PEERS = (0, 2, 1, 3)


def tiled(block):
    if block.ndim != 2 or block.shape[0] % 8:
        return block
    return block.reshape(-1, 8, block.shape[1])


def ctx_swap(block, bit):
    pairs = [(i, i ^ bit) for i in range(lax.axis_size("ctx"))]
    got = row_major(lax.ppermute(row_major(tiled(block)), "ctx", pairs))
    return got.reshape(block.shape)


def gather_ctx(block):
    far = ctx_swap(block, 2)
    near = ctx_swap(block, 1)
    return [block, far, near, ctx_swap(far, 1)]


def halves(matrix):
    half = matrix.shape[0] // 2
    return matrix[:half], matrix[half:]


def pair_add_kernel(keep, got, kept, onward):
    rows = kept.shape[0]
    kept[...] = added(keep[:rows], got[:rows]).astype(kept.dtype)
    onward[...] = added(keep[rows:], got[rows:]).astype(bf16)


def pair_add(keep, got, kind=f32):
    rows, columns = keep.shape
    half = (rows // 2, columns)
    return call(
        pair_add_kernel,
        "pair_add",
        1,
        (keep, got),
        [whole(keep.shape)] * 2,
        [(half, kind), (half, bf16)],
        [whole(half)] * 2,
    )


def pair_split_kernel(keep, got, kept, first, second):
    rows = kept.shape[0]
    half = rows // 2
    kept[...] = added(keep[:rows], got[:rows]).astype(kept.dtype)
    first[...] = added(keep[rows : rows + half], got[rows : rows + half]).astype(bf16)
    second[...] = added(keep[rows + half :], got[rows + half :]).astype(bf16)


def pair_split(keep, got):
    rows, columns = keep.shape
    half, quarter = (rows // 2, columns), (rows // 4, columns)
    return call(
        pair_split_kernel,
        "pair_split",
        1,
        (keep, got),
        [whole(keep.shape)] * 2,
        [(half, bf16), (quarter, bf16), (quarter, bf16)],
        [whole(half), whole(quarter), whole(quarter)],
    )


def exchange_near(keep, give):
    quarter = keep.shape[0] // 2
    got = ctx_swap(give, 1)
    return keep[:quarter], got[:quarter], jnp.concatenate([keep[quarter:], got[quarter:]])


def exchange_far(mine, near, onward):
    quarter = mine.shape[0]
    got = ctx_swap(onward, 2)
    return [mine, got[:quarter], near, got[quarter:]]


RING = (0, 2, 4, 6, 7, 5, 3, 1)
HALF = len(RING) // 2


def ring_hop(value, step):
    count = len(RING)
    pairs = [(RING[q], RING[(q + step) % count]) for q in range(count)]
    return row_major(lax.ppermute(row_major(value), "fsdp", pairs))


def ring_owners():
    place = jnp.asarray(np.argsort(np.array(RING)).astype(np.int32))
    mine = lax.dynamic_index_in_dim(place, lax.axis_index("fsdp"), 0, False)
    offsets = np.array([0, -1, 1, -2, 2, -3, 3, 4], np.int32)
    return jnp.take(jnp.asarray(np.array(RING, np.int32)), (mine + offsets) % len(RING))


def on_ring():
    return lax.axis_size("fsdp") == len(RING)


def upper_part(rows):
    return rows // 16 * 8


class Gather:
    def __init__(self, block):
        self.block = block
        self.cut = upper_part(block.shape[0])
        self.pieces = [block]
        self.forth = self.back = block

    def step(self):
        if not on_ring():
            return ()
        forth, back = self.forth, self.back
        if len(self.pieces) == 2 * HALF - 1:
            forth, back = forth[: self.cut], back[self.cut :]
        return ring_hop(forth, 1), ring_hop(back, -1)

    def take(self, moved):
        if moved:
            self.forth, self.back = moved
            self.pieces += list(moved)

    def hop(self):
        self.take(self.step())

    def arrived(self):
        return (self.forth, self.back) if on_ring() else ()

    def result(self, owners, columns, gates=()):
        if not on_ring():
            whole = lax.all_gather(self.block, "fsdp", axis=0, tiled=False)
            return [whole[:, top : top + n, c : c + w] for c, w, top, n in columns]
        return collect(self.pieces, owners, self.cut, columns, gates)


def spread_small(held, bit):
    got = lax.ppermute(held, "fsdp", [(i, i ^ bit) for i in range(lax.axis_size("fsdp"))])
    low = (lax.axis_index("fsdp") & bit) == 0
    return jnp.concatenate([jnp.where(low, held, got), jnp.where(low, got, held)])


def collect_kernel(cut, columns, owners, *refs):
    pieces = refs[: 2 * HALF + 1]
    outs = refs[2 * HALF + 1 : 2 * HALF + 1 + len(columns)]
    sems = refs[-1]
    copies = []
    for out, (start, width, top, rows) in zip(outs, columns):
        for j, piece in enumerate(pieces):
            first = cut if j == 2 * HALF else 0
            low = max(top, first)
            high = min(top + rows, first + piece.shape[0])
            if low < high:
                copies.append(
                    pltpu.make_async_copy(
                        piece.at[pl.ds(low - first, high - low), pl.ds(start, width)],
                        out.at[owners[min(j, 2 * HALF - 1)], pl.ds(low - top, high - low)],
                        sems.at[len(copies)],
                    )
                )
    for copy in copies:
        copy.start()
    for copy in copies:
        copy.wait()


def collect(pieces, owners, cut, columns, gates):
    shapes = [(len(RING), rows, width) for _, width, _, rows in columns]
    return call(
        functools.partial(collect_kernel, cut, columns),
        "collect",
        1,
        pieces,
        [pl.BlockSpec(memory_space=pl.ANY)] * len(pieces),
        [(shape, pieces[0].dtype) for shape in shapes],
        [whole(shape) for shape in shapes],
        [pltpu.SemaphoreType.DMA((len(pieces) * len(columns),))],
        owners,
        gates,
    )


PLACE = {0: 0, -1: 1, 1: 2, -2: 3, 2: 4, -3: 5, 3: 6, 4: 7}


def half_blocks(cut, rows, width, forth, back):
    return forth[forth.shape[0] - cut :, :width], back[back.shape[0] - (rows - cut) :, :width]


def ring_part_kernel(distance, cut, owners, *refs):
    if distance == HALF:
        far, ahead, behind = refs
        ahead[...] = far[:cut]
        behind[...] = far[cut:]
    elif distance == 0:
        own, forth, back, out = refs
        rows = own.shape[0]
        out[...] = added(own[...], forth[:rows], back[:rows]).astype(bf16)
    else:
        mine_ahead, mine_behind, forth, back, ahead, behind = refs
        if distance == HALF - 1:
            rows, width = mine_ahead.shape
            from_forth, from_back = half_blocks(cut, rows, width, forth, back)
            ahead[:cut] = added(mine_ahead[:cut], from_forth).astype(bf16)
            ahead[cut:] = mine_ahead[cut:]
            behind[:cut] = mine_behind[:cut]
            behind[cut:] = added(mine_behind[cut:], from_back).astype(bf16)
        else:
            ahead[...] = added(mine_ahead[...], forth[...]).astype(bf16)
            behind[...] = added(mine_behind[...], back[...]).astype(bf16)


def ring_part(blocks, owners, distance, cut, moved, gates=()):
    rows, columns = blocks.shape[1:]
    distances = (distance,) if distance in (0, HALF) else (distance, -distance)
    if distance == HALF:
        shapes = [(cut, columns), (rows - cut, columns)]
    else:
        shapes = [(rows, columns)] * len(distances)
    places = [PLACE[d] for d in distances]
    return call(
        functools.partial(ring_part_kernel, distance, cut),
        "ring_part",
        1,
        (*[blocks] * len(places), *moved),
        [
            pl.BlockSpec((None, rows, columns), lambda i, t, p=p: (t[p], 0, 0)) for p in places
        ]
        + [whole(value.shape) for value in moved],
        [(shape, bf16) for shape in shapes],
        [whole(shape) for shape in shapes],
        table=owners,
        gates=gates,
    )


def packed_kernel(cut, owners, mine_ahead, mine_behind, forth, back, far, ahead, behind):
    rows, width = mine_ahead.shape
    second = far.shape[1]
    ahead[:rows] = added(mine_ahead[...], forth[...]).astype(bf16)
    behind[:rows] = added(mine_behind[...], back[...]).astype(bf16)
    ahead[rows:, :second] = far[:cut]
    behind[rows:, :second] = far[cut:]
    if second < width:
        ahead[rows:, second:] = jnp.zeros((cut, width - second), bf16)
        behind[rows:, second:] = jnp.zeros((rows - cut, width - second), bf16)


def packed_step(blocks, others, owners, moved):
    if not on_ring():
        return ()
    rows, width = blocks.shape[1:]
    cut = upper_part(rows)
    shapes = [(rows + cut, width), (2 * rows - cut, width)]
    ahead, behind = call(
        functools.partial(packed_kernel, cut),
        "packed_part",
        1,
        (blocks, blocks, *moved, others),
        [
            pl.BlockSpec((None, rows, width), lambda i, t, p=PLACE[d]: (t[p], 0, 0))
            for d in (1, -1)
        ]
        + [whole(value.shape) for value in moved]
        + [pl.BlockSpec((None,) + others.shape[1:], lambda i, t: (t[PLACE[HALF]], 0, 0))],
        [(shape, bf16) for shape in shapes],
        [whole(shape) for shape in shapes],
        table=owners,
    )
    return ring_hop(ahead, 1), ring_hop(behind, -1)


def ring_step(blocks, owners, distance, moved=()):
    if not on_ring():
        return ()
    ahead, behind = ring_part(blocks, owners, distance, upper_part(blocks.shape[1]), moved)
    return ring_hop(ahead, 1), ring_hop(behind, -1)


def twin_block(owners, place, refs):
    kept, first, second = refs
    low = owners[place] < HALF
    return added(kept[...], jnp.where(low, first[...], second[...]))


def twin_kernel(distance, lag, cut, owners, *refs):
    width = refs[0].shape[-1]
    if distance == 0:
        own, forth, back, *twins = refs
        out, ahead, behind = twins[-3:]
        out[...] = added(own[...], forth[:, :width], back[:, :width]).astype(bf16)
        value_ahead = twin_block(owners, PLACE[lag], twins[0:3])
        value_behind = twin_block(owners, PLACE[-lag], twins[3:6])
        ahead[...] = added(value_ahead, forth[:, width:]).astype(bf16)
        behind[...] = added(value_behind, back[:, width:]).astype(bf16)
        return
    mine_ahead, mine_behind, forth, back, *twins = refs
    ahead, behind = twins[-2:]
    if distance == HALF - 1:
        from_forth, from_back = half_blocks(cut, mine_ahead.shape[0], width, forth, back)
        ahead[:cut, :width] = added(mine_ahead[:cut], from_forth).astype(bf16)
        ahead[cut:, :width] = mine_ahead[cut:]
        behind[:cut, :width] = mine_behind[:cut]
        behind[cut:, :width] = added(mine_behind[cut:], from_back).astype(bf16)
        value = twin_block(owners, PLACE[HALF], twins[0:3]).astype(bf16)
        ahead[:cut, width:] = value[:cut]
        ahead[cut:, width:] = jnp.zeros_like(value[cut:])
        behind[:cut, width:] = jnp.zeros_like(value[:cut])
        behind[cut:, width:] = value[cut:]
    else:
        ahead[:, :width] = added(mine_ahead[...], forth[:, :width]).astype(bf16)
        behind[:, :width] = added(mine_behind[...], back[:, :width]).astype(bf16)
        value_ahead = twin_block(owners, PLACE[lag], twins[0:3])
        value_behind = twin_block(owners, PLACE[-lag], twins[3:6])
        ahead[:, width:] = added(value_ahead, forth[:, width:]).astype(bf16)
        behind[:, width:] = added(value_behind, back[:, width:]).astype(bf16)


def twin_part(blocks, twin, owners, distance, moved):
    rows, width = blocks.shape[1:]
    span = twin[0].shape[2]
    lag = distance + 1
    mains = (distance, -distance) if distance else (0,)
    lags = (lag, -lag) if lag < HALF else (lag,)
    specs = [
        pl.BlockSpec((None, rows, width), lambda i, t, p=PLACE[d]: (t[p], 0, 0)) for d in mains
    ]
    specs += [whole(value.shape) for value in moved]
    for d in lags:
        p = PLACE[d]
        specs += [
            pl.BlockSpec((None, rows, span), lambda i, t, p=p: (t[p], 0, 0)),
            pl.BlockSpec(
                (None, rows, span), lambda i, t, p=p: (jnp.minimum(t[p], HALF - 1), 0, 0)
            ),
            pl.BlockSpec((None, rows, span), lambda i, t, p=p: (jnp.maximum(t[p] - HALF, 0), 0, 0)),
        ]
    if distance:
        shapes = [(rows, width + span)] * 2
    else:
        shapes = [(rows, width), (rows, span), (rows, span)]
    return call(
        functools.partial(twin_kernel, distance, lag, upper_part(rows)),
        "twin_part",
        1,
        (*[blocks] * len(mains), *moved, *twin * len(lags)),
        specs,
        [(shape, bf16) for shape in shapes],
        [whole(shape) for shape in shapes],
        table=owners,
    )


def twin_last_kernel(owners, forth, back, kept, first, second, out):
    value = twin_block(owners, PLACE[0], (kept, first, second))
    out[...] = added(value, forth[...], back[...]).astype(bf16)


def twin_last(twin, owners, moved):
    if not on_ring():
        blocks = added(twin[0], jnp.concatenate(twin[1:])).astype(bf16)
        return ring_end(blocks, owners, moved)
    rows, span = twin[0].shape[1:]
    block = (None, rows, span)
    return call(
        twin_last_kernel,
        "twin_last",
        1,
        (*moved, *twin),
        [whole((rows, span))] * 2
        + [
            pl.BlockSpec(block, lambda i, t: (t[0], 0, 0)),
            pl.BlockSpec(block, lambda i, t: (jnp.minimum(t[0], HALF - 1), 0, 0)),
            pl.BlockSpec(block, lambda i, t: (jnp.maximum(t[0] - HALF, 0), 0, 0)),
        ],
        [((rows, span), bf16)],
        [whole((rows, span))],
        table=owners,
    )[0]


def twin_step(blocks, twin, owners, distance, moved):
    if not on_ring():
        return ()
    ahead, behind = twin_part(blocks, twin, owners, distance, moved)
    return ring_hop(ahead, 1), ring_hop(behind, -1)


def twin_end(blocks, twin, owners, moved):
    if not on_ring():
        return ring_end(blocks, owners, moved), ()
    out, ahead, behind = twin_part(blocks, twin, owners, 0, moved)
    return out, (ring_hop(ahead, 1), ring_hop(behind, -1))


def ring_end(blocks, owners, moved):
    if not on_ring():
        return lax.psum_scatter(blocks, "fsdp", scatter_dimension=0, tiled=False)
    return ring_part(blocks, owners, 0, upper_part(blocks.shape[1]), moved)[0]


def halve_small(held, bit):
    me = lax.axis_index("fsdp")
    parts = held.reshape(2, bit, -1)
    high = (me & bit) != 0
    keep = jnp.where(high, parts[1], parts[0])
    give = jnp.where(high, parts[0], parts[1])
    pairs = [(i, i ^ bit) for i in range(lax.axis_size("fsdp"))]
    return keep + lax.ppermute(give, "fsdp", pairs)


def finish_small(held, bit):
    while bit:
        held = halve_small(held, bit)
        bit //= 2
    return held


def norm_stats(values):
    centre = values - jnp.mean(values, axis=-1, keepdims=True)
    scale = lax.rsqrt(jnp.mean(centre * centre, axis=-1, keepdims=True) + norm_eps)
    return centre * scale, scale


def norm_back(grad, unit, scale, gain):
    inner = grad * gain
    back = scale * (
        inner
        - jnp.mean(inner, axis=-1, keepdims=True)
        - unit * jnp.mean(inner * unit, axis=-1, keepdims=True)
    )
    return back, jnp.sum(grad * unit, axis=0), jnp.sum(grad, axis=0)


def across(left_op, right_op, left_dim, right_dim):
    return lax.dot_general(
        left_op, right_op, (((left_dim,), (right_dim,)), ((), ())), preferred_element_type=f32
    )


def diagonal_kept():
    shape = (QB, QB)
    return lax.broadcasted_iota(jnp.int32, shape, 0) <= lax.broadcasted_iota(jnp.int32, shape, 1)


def sorted_tile(table, ref, columns):
    groups = ref.shape[0] // GROUP
    return jnp.concatenate(
        [ref[pl.ds(pl.multiple_of(table[g], GROUP), GROUP), columns] for g in range(groups)],
        axis=0,
    )


def put_sorted(table, ref, columns, first, value):
    for j in range(value.shape[0] // GROUP):
        start = pl.multiple_of(table[first + j], GROUP)
        ref[pl.ds(start, GROUP), columns] = value[j * GROUP : (j + 1) * GROUP]


def split_heads(tiles, last):
    if last:
        return [(tiles[0][:, :HD], tiles[0][:, HD:], tiles[1][:, :HD])]
    return [tuple(t[:, w * HD : (w + 1) * HD] for t in tiles) for w in range(2)]


def pair_columns(pair, last):
    if last:
        start = SLOTS // 2 * 3 * PAIR
        return [slice(start, start + PAIR), slice(start + PAIR, start + 2 * PAIR)]
    return [pl.ds(pl.multiple_of(pair * 3 * PAIR + t * PAIR, PAIR), PAIR) for t in range(3)]


def attend_pair(pair, last, table, qkv_ref, out_ref, mass_ref):
    tiles = [sorted_tile(table, qkv_ref, c) for c in pair_columns(pair, last)]
    heads = split_heads(tiles, last)
    length = qkv_ref.shape[0]
    kept = diagonal_kept()
    ready = [(q * bf16(HD**-0.5), k, v.T) for q, k, v in heads]
    for i in range(length // QB):
        rows = slice(i * QB, (i + 1) * QB)
        outs = []
        for w, (queries, keys, values_t) in enumerate(ready):
            mine = queries[rows]
            diag = jnp.where(kept, across(keys[rows], mine, 1, 1), masked_low)
            peak = jnp.max(diag, axis=0, keepdims=True)
            if i:
                rest = across(keys[: i * QB], mine, 1, 1)
                peak = jnp.maximum(peak, jnp.max(rest, axis=0, keepdims=True))
            diag = jnp.exp(diag - peak)
            mass = jnp.sum(diag, axis=0, keepdims=True)
            out = across(values_t[:, rows], diag.astype(bf16), 1, 0)
            if i:
                rest = jnp.exp(rest - peak)
                mass = mass + jnp.sum(rest, axis=0, keepdims=True)
                out = out + across(values_t[:, : i * QB], rest.astype(bf16), 1, 0)
            outs.append(out / mass)
            mass_ref[0, w : w + 1, rows] = peak + jnp.log(mass)
        if last:
            outs.append(jnp.zeros_like(outs[0]))
        tile = jnp.concatenate(outs, axis=0).T.astype(bf16)
        put_sorted(table, out_ref, slice(None), 2 * i, tile)


def attend_kernel(table, qkv_ref, out_ref, mass_ref):
    pair = pl.program_id(0)
    final = pl.num_programs(0) - 1

    @pl.when(pair < final)
    def _():
        attend_pair(pair, False, table, qkv_ref, out_ref, mass_ref)

    @pl.when(pair == final)
    def _():
        mass_ref[...] = jnp.zeros_like(mass_ref)

        @pl.when(table[table.shape[0] - 1] == 0)
        def _():
            out_ref[...] = jnp.zeros_like(out_ref)

        @pl.when(table[table.shape[0] - 1] != 0)
        def _():
            attend_pair(pair, True, table, qkv_ref, out_ref, mass_ref)


def attend_back_pair(pair, last, table, qkv_ref, grad_ref, mass_ref, out_ref, acc):
    places = pair_columns(pair, last)
    heads = split_heads([sorted_tile(table, qkv_ref, c) for c in places], last)
    grads = sorted_tile(table, grad_ref, slice(None))
    length = qkv_ref.shape[0]
    kept = diagonal_kept()
    ready = [
        (q * bf16(HD**-0.5), k, k.T, v, grads[:, w * HD : (w + 1) * HD])
        for w, (q, k, v) in enumerate(heads)
    ]
    for i in range(length // QB):
        rows = slice(i * QB, (i + 1) * QB)
        query_tiles = []
        for w, (queries, keys, keys_t, values, grads_w) in enumerate(ready):
            mine = queries[rows]
            grad = grads_w[rows]
            mass = mass_ref[0, w : w + 1, rows]
            spans = [(rows, True)] + ([(slice(0, i * QB), False)] if i else [])
            probs, both, delta = [], [], None
            for span, diagonal in spans:
                scores = across(keys[span], mine, 1, 1)
                if diagonal:
                    scores = jnp.where(kept, scores, masked_low)
                prob = jnp.exp(scores - mass)
                prod = prob * across(values[span], grad, 1, 1)
                part = jnp.sum(prod, axis=0, keepdims=True)
                delta = part if delta is None else delta + part
                probs.append(prob)
                both.append(prod)
            query_t = None
            for (span, diagonal), prob, prod in zip(spans, probs, both):
                grad_scores = (prod - prob * delta).astype(bf16)
                part = across(keys_t[:, span], grad_scores, 1, 0)
                query_t = part if query_t is None else query_t + part
                key_part = across(grad_scores, mine, 1, 0)
                value_part = across(prob.astype(bf16), grad, 1, 0)
                if diagonal:
                    acc[2 * w, span, :] = key_part
                    acc[2 * w + 1, span, :] = value_part
                else:
                    acc[2 * w, span, :] += key_part
                    acc[2 * w + 1, span, :] += value_part
            query_tiles.append(query_t * HD**-0.5)
        if last:
            query_tiles.append(jnp.zeros_like(query_tiles[0]))
        tile = jnp.concatenate(query_tiles, axis=0).T
        if last:
            tile = jnp.concatenate([tile[:, :HD], jnp.zeros_like(tile[:, HD:])], axis=1)
        put_sorted(table, out_ref, places[0], 2 * i, tile.astype(bf16))
    if last:
        old = sorted_tile(table, out_ref, places[0])
        tile = jnp.concatenate([old[:, :HD], acc[0].astype(bf16)], axis=1)
        put_sorted(table, out_ref, places[0], 0, tile)
        tile = jnp.concatenate([acc[1].astype(bf16), jnp.zeros((length, HD), bf16)], axis=1)
        put_sorted(table, out_ref, places[1], 0, tile)
    else:
        for t in range(2):
            tile = jnp.concatenate([acc[t].astype(bf16), acc[2 + t].astype(bf16)], axis=1)
            put_sorted(table, out_ref, places[1 + t], 0, tile)


def attend_back_kernel(table, *refs):
    grad_refs, (qkv_ref, mass_ref, out_ref, acc, held) = refs[:4], refs[4:]
    pair = pl.program_id(0)
    final = pl.num_programs(0) - 1

    @pl.when(pair == 0)
    def _():
        span = SLOTS * HD
        rows = grad_refs[0].shape[0]
        for j, ref in enumerate(grad_refs):
            for p in range(span // PAIR):
                held[p, j * rows : (j + 1) * rows, :] = ref[:, p * PAIR : (p + 1) * PAIR]
            tail = jnp.concatenate([ref[:, span - HD :], jnp.zeros((rows, HD), bf16)], axis=1)
            held[span // PAIR, j * rows : (j + 1) * rows, :] = tail

    refs = (table, qkv_ref, held.at[pair], mass_ref, out_ref, acc)

    @pl.when(pair < final)
    def _():
        attend_back_pair(pair, False, *refs)

    @pl.when(pair == final)
    def _():
        @pl.when(table[table.shape[0] - 1] == 0)
        def _():
            for columns in pair_columns(pair, True):
                out_ref[:, columns] = jnp.zeros((out_ref.shape[0], PAIR), bf16)

        @pl.when(table[table.shape[0] - 1] != 0)
        def _():
            attend_back_pair(pair, True, *refs)


def attend(table, qkv, gates):
    length, columns = qkv.shape
    pairs = (SLOTS + 1) // 2
    return call(
        attend_kernel,
        "attend",
        pairs,
        (qkv,),
        [whole((length, columns))],
        [((length, pairs * PAIR), bf16), ((pairs, 8, length), f32)],
        [
            pl.BlockSpec((length, PAIR), lambda p, t: (0, p)),
            pl.BlockSpec((1, 8, length), lambda p, t: (p, 0, 0)),
        ],
        table=table,
        gates=gates,
    )


def attend_back(table, qkv, grads, mass, gates):
    length, columns = qkv.shape
    pairs = (SLOTS + 1) // 2
    return call(
        attend_back_kernel,
        "attend_back",
        pairs,
        (*grads, qkv, mass),
        [whole(grad.shape) for grad in grads]
        + [whole((length, columns)), pl.BlockSpec((1, 8, length), lambda p, t: (p, 0, 0))],
        [((length, columns), bf16)],
        [whole((length, columns))],
        [pltpu.VMEM((4, length, HD), f32), pltpu.VMEM((pairs, length, PAIR), bf16)],
        table,
        gates,
    )[0]


def whole(shape):
    return pl.BlockSpec(shape, lambda *_: (0,) * len(shape))


def rows_spec(rows, columns):
    return pl.BlockSpec((rows, columns), lambda i, *_: (i, 0))


def call(
    kernel,
    name,
    grid,
    operands,
    specs,
    outs,
    out_specs,
    scratch=(),
    table=None,
    gates=(),
    limit=VMEM_LIMIT,
):
    tables = () if table is None else (table,)
    first = len(tables) + len(operands)
    count = len(gates)

    def body(*refs):
        kernel(*refs[:first], *refs[first + count :])

    return pl.pallas_call(
        body,
        grid_spec=pltpu.PrefetchScalarGridSpec(
            num_scalar_prefetch=len(tables),
            grid=(grid,),
            in_specs=list(specs) + [pl.BlockSpec(memory_space=pl.ANY)] * count,
            out_specs=out_specs,
            scratch_shapes=list(scratch),
        ),
        out_shape=[jax.ShapeDtypeStruct(shape, kind) for shape, kind in outs],
        compiler_params=pltpu.CompilerParams(vmem_limit_bytes=limit),
        cost_estimate=LIGHT,
        name=name,
    )(*tables, *operands, *gates)


def pick_block(refs, held):
    for j, ref in enumerate(refs):

        @pl.when(pl.program_id(0) == j)
        def _(ref=ref):
            held[...] = ref[...]


def norm_mixed_kernel(*refs):
    blocks, (gain, shift, weights, bias, normed, mixed, held) = refs[:4], refs[4:]
    pick_block(blocks, held)
    unit, _ = norm_stats(held[...].astype(f32))
    low = (unit * gain[...] + shift[...]).astype(bf16)
    normed[...] = low
    mixed[...] = (product(low, weights[...]) + bias[...]).astype(bf16)


def norm_mixed(blocks, gain, shift, weights, bias):
    count, width = blocks[0].shape
    mixed_width = weights.shape[1]
    length = count * len(blocks)
    return call(
        norm_mixed_kernel,
        "norm_mixed",
        len(blocks),
        (*blocks, gain[None], shift[None], weights, bias),
        [whole((count, width))] * len(blocks)
        + [whole((1, width))] * 2
        + [whole(weights.shape), whole((1, mixed_width))],
        [((length, width), bf16), ((length, mixed_width), bf16)],
        [rows_spec(count, width), rows_spec(count, mixed_width)],
        [pltpu.VMEM((count, width), bf16)],
    )


def join_kernel(table, *refs):
    pieces, out, sems, last_sem = refs[:4], refs[4], refs[5], refs[6]
    step, span = BASE * HD, SLOTS * HD
    width = out.shape[1]
    rest = span - step
    last = len(pieces) - 1

    def copies(j):
        start = pl.multiple_of(table[j] * step, PAIR)
        main = pltpu.make_async_copy(
            pieces[j].at[:, pl.ds(0, step)], out.at[:, pl.ds(start, step)], sems.at[j]
        )
        tail = pltpu.make_async_copy(
            pieces[j].at[:, pl.ds(step, rest)], out.at[:, pl.ds(width - rest, rest)], last_sem.at[0]
        )
        return main, tail

    for j in range(len(pieces)):
        main, tail = copies(j)
        main.start()

        @pl.when(table[j] == last)
        def _(tail=tail):
            tail.start()

    for j in range(len(pieces)):
        main, tail = copies(j)
        main.wait()

        @pl.when(table[j] == last)
        def _(tail=tail):
            tail.wait()


def join_windows(table, pieces, width):
    rows = pieces[0].shape[0]
    return call(
        join_kernel,
        "join_windows",
        1,
        pieces,
        [pl.BlockSpec(memory_space=pl.ANY)] * len(pieces),
        [((rows, width), pieces[0].dtype)],
        [whole((rows, width))],
        [pltpu.SemaphoreType.DMA((len(pieces),)), pltpu.SemaphoreType.DMA((1,))],
        table,
    )[0]


def attn_out_kernel(table, *refs):
    pieces, rest = refs[:4], refs[4:]
    weights, tokens, bias, gain, shift, middle, normed, attended = rest
    step, span = BASE * HD, SLOTS * HD
    width = attended.shape[1]
    for j, piece in enumerate(pieces):
        start = pl.multiple_of(table[j] * step, PAIR)
        attended[:, pl.ds(start, step)] = piece[:, :step]

        @pl.when(table[j] == len(pieces) - 1)
        def _(piece=piece):
            attended[:, width - (span - step) :] = piece[:, step:]

    value = tokens[...].astype(f32) + product(attended[...], weights[...]) + bias[...]
    middle[...] = value
    unit, _ = norm_stats(value)
    normed[...] = (unit * gain[...] + shift[...]).astype(bf16)


def attn_out(table, pieces, weights, tokens, bias, gain, shift):
    count, width = tokens.shape
    return call(
        attn_out_kernel,
        "attn_out",
        1,
        (*pieces, weights, tokens, bias[None], gain[None], shift[None]),
        [whole(piece.shape) for piece in pieces]
        + [whole(weights.shape), whole((count, width))]
        + [whole((1, width))] * 3,
        [((count, width), f32), ((count, width), bf16), ((count, width), bf16)],
        [whole((count, width))] * 3,
        table=table,
    )


def up_kernel(*refs):
    blocks, (weights, bias, activated, slope, normed, held) = refs[:4], refs[4:]
    pick_block(blocks, held)
    normed[...] = held[...]
    before = product(held[...], weights[...]) + bias[...]
    square = before * before
    inner = jnp.tanh(before * (0.7978845608028654 + 0.7978845608028654 * 0.044715 * square))
    half = 0.5 * (1.0 + inner)
    activated[...] = (before * half).astype(bf16)
    slope[...] = (
        half
        + 0.5
        * before
        * (1.0 - inner * inner)
        * (0.7978845608028654 + 3 * 0.7978845608028654 * 0.044715 * square)
    ).astype(bf16)


def feed_up(blocks, weights, bias):
    count, width = blocks[0].shape
    units = weights.shape[1]
    length = count * len(blocks)
    return call(
        up_kernel,
        "feed_up",
        len(blocks),
        (*blocks, weights, bias[None]),
        [whole((count, width))] * len(blocks) + [whole(weights.shape), whole((1, units))],
        [((length, units), bf16), ((length, units), bf16), ((length, width), bf16)],
        [rows_spec(count, units), rows_spec(count, units), rows_spec(count, width)],
        [pltpu.VMEM((count, width), bf16)],
    )


def back_kernel(*refs):
    blocks, (down, slope, low, sums, held) = refs[:4], refs[4:]
    pick_block(blocks, held)
    value = (back_product(held[...], down[...]) * slope[...].astype(f32)).astype(bf16)
    low[...] = value

    @pl.when(pl.program_id(0) == 0)
    def _():
        sums[...] = jnp.zeros_like(sums)

    sums[...] += jnp.sum(value.astype(f32), axis=0, keepdims=True)


def feed_back(blocks, down, slope, gates):
    count, width = blocks[0].shape
    units = slope.shape[1]
    length = count * len(blocks)
    return call(
        back_kernel,
        "feed_back",
        len(blocks),
        (*blocks, down, slope),
        [whole((count, width))] * len(blocks) + [whole(down.shape), rows_spec(count, units)],
        [((length, units), bf16), ((1, units), f32)],
        [rows_spec(count, units), whole((1, units))],
        [pltpu.VMEM((count, width), bf16)],
        gates=gates,
    )


def plain_back_kernel(left, right, keep, give):
    value = back_product(left[...], right[...]).astype(bf16)
    first = pl.program_id(0) < pl.num_programs(0) // 2

    @pl.when(first)
    def _():
        keep[...] = value

    @pl.when(jnp.logical_not(first))
    def _():
        give[...] = value


def plain_back(left, right, name):
    length, inner = left.shape
    width = right.shape[0]
    steps = length // QB
    half = steps // 2
    return call(
        plain_back_kernel,
        name,
        steps,
        (left, right),
        [rows_spec(QB, inner), whole(right.shape)],
        [((length // 2, width), bf16)] * 2,
        [
            pl.BlockSpec((QB, width), lambda i: (jnp.minimum(i, half - 1), 0)),
            pl.BlockSpec((QB, width), lambda i: (jnp.maximum(i - half, 0), 0)),
        ],
    )


VECTOR_ROWS = 8
FC_START = 2 * PAIR
VECTOR_WIDTH = 9 * PAIR


def attn_block_kernel(place, qkv, out_weights, *refs):
    vectors, (bias_fc, block, lines_out) = refs[:VECTOR_ROWS], refs[VECTOR_ROWS:]
    step, span = BASE * HD, SLOTS * HD
    width = out_weights.shape[1]
    rows = qkv.shape[0]
    parts = []
    for t in range(3):
        skip = t * width % PAIR
        start = pl.multiple_of(place[0] * step + (t * width - skip), PAIR)
        parts.append(qkv[:, pl.ds(start, span + skip)][:, skip:])
    for p in range(SLOTS // 2):
        for t in range(3):
            first = (3 * p + t) * PAIR
            block[:, first : first + PAIR] = parts[t][:, p * PAIR : (p + 1) * PAIR]
    rest = [part[:, (SLOTS - 1) * HD :] for part in parts] + [jnp.zeros((rows, HD), bf16)]
    first = 3 * (SLOTS // 2) * PAIR
    for p in range(2):
        block[:, first + p * PAIR : first + (p + 1) * PAIR] = jnp.concatenate(
            rest[2 * p : 2 * p + 2], axis=1
        )
    start = pl.multiple_of(place[0] * step, PAIR)
    block[:, first + 2 * PAIR :] = out_weights[:, pl.ds(start, span)]
    lines = jnp.stack([vector[...].astype(f32) for vector in vectors])
    lines_out[...] = jnp.zeros_like(lines_out)
    lines_out[:, : lines.shape[1]] = lines.astype(bf16)
    units = bias_fc.shape[0]
    line = jnp.broadcast_to(bias_fc[...].astype(f32)[None], (VECTOR_ROWS, units))
    lines_out[:, FC_START : FC_START + units] = line.astype(bf16)


def form_attn_block(place, qkv, out_weights, vectors, bias_fc):
    rows = qkv.shape[0]
    columns = 3 * (SLOTS // 2) * PAIR + 2 * PAIR + SLOTS * HD
    vectors = [*vectors, bias_fc]
    return call(
        attn_block_kernel,
        "form_attn_block",
        1,
        (qkv, out_weights, *vectors),
        [whole(value.shape) for value in (qkv, out_weights, *vectors)],
        [((rows, columns), bf16), ((VECTOR_ROWS, VECTOR_WIDTH), bf16)],
        [whole((rows, columns)), whole((VECTOR_ROWS, VECTOR_WIDTH))],
        table=place,
        limit=56 << 20,
    )


def whole_rows_kernel(table, *refs):
    pieces, out, held = refs[:4], refs[4], refs[5]
    pick_block(pieces, held)
    out[...] = held[...].astype(f32)


def whole_rows(table, pieces, gates):
    rows, width = pieces[0].shape
    return call(
        whole_rows_kernel,
        "whole_rows",
        len(pieces),
        pieces,
        [whole((rows, width))] * len(pieces),
        [((len(pieces), rows, width), f32)],
        [pl.BlockSpec((None, rows, width), lambda i, t: (t[i], 0, 0))],
        [pltpu.VMEM((rows, width), bf16)],
        table,
        gates,
    )[0].reshape(-1, width)


def put_windows(table, held, outs):
    for j in range(2 * len(outs)):
        start = pl.multiple_of(table[j] * BASE * HD, PAIR)
        outs[j // 2][j % 2] = held[:, pl.ds(start, SLOTS * HD)]


def norm_two_kernel(table, *refs):
    kept, far, middle, grad_out, gain, weights, grad_middle, low, keep, give, sums, held = refs
    grad = kept[...] + far[...].astype(f32)
    unit, scale = norm_stats(middle[...])
    back, grad_gain, grad_shift = norm_back(grad, unit, scale, gain[...])
    out = grad_out[...].astype(f32)
    value = out + back
    grad_middle[...] = value
    value_low = value.astype(bf16)
    low[...] = value_low
    held[...] = back_product(value_low, weights[...]).astype(bf16)
    put_windows(table, held, (keep, give))
    sums[0:1, :] = grad_gain[None]
    sums[1:2, :] = grad_shift[None]
    sums[2:3, :] = jnp.sum(value_low.astype(f32), axis=0, keepdims=True)
    sums[3:4, :] = jnp.sum(out, axis=0, keepdims=True)


def norm_two_back(table, kept, far, middle, grad_out, gain, weights, gates):
    count, width = middle.shape
    half = (2, count, SLOTS * HD)
    return call(
        norm_two_kernel,
        "norm_two_back",
        1,
        (kept, far, middle, grad_out, gain[None], weights),
        [whole((count, width))] * 4 + [whole((1, width)), whole(weights.shape)],
        [
            ((count, width), f32),
            ((count, width), bf16),
            (half, bf16),
            (half, bf16),
            ((4, width), f32),
        ],
        [
            whole((count, width)),
            whole((count, width)),
            whole(half),
            whole(half),
            whole((4, width)),
        ],
        [pltpu.VMEM((count, width), bf16)],
        table,
        gates=gates,
    )


def norm_one_kernel(kept, far, tokens, grad_middle, gain, grad_tokens, sums):
    grad = kept[...] + far[...].astype(f32)
    unit, scale = norm_stats(tokens[...].astype(f32))
    back, grad_gain, grad_shift = norm_back(grad, unit, scale, gain[...])
    grad_tokens[...] = grad_middle[...] + back
    sums[0:1, :] = grad_gain[None]
    sums[1:2, :] = grad_shift[None]


def norm_one_back(kept, far, tokens, grad_middle, gain, gates):
    shape = kept.shape
    return call(
        norm_one_kernel,
        "norm_one_back",
        1,
        (kept, far, tokens, grad_middle, gain[None]),
        [whole(shape)] * 4 + [whole((1, shape[1]))],
        [(shape, f32), ((2, shape[1]), f32)],
        [whole(shape), whole((2, shape[1]))],
        gates=gates,
    )


def out_grad_kernel(table, attended, low, keep, give, held):
    held[...] = outer_sum(attended[...], low[...]).astype(bf16)
    put_windows(table, held, (keep, give))


def out_weight_grad(table, attended, low, gates):
    count, width = attended.shape
    half = (2, width, SLOTS * HD)
    return call(
        out_grad_kernel,
        "out_weight_grad",
        1,
        (attended, low),
        [whole((count, width))] * 2,
        [(half, bf16)] * 2,
        [whole(half)] * 2,
        [pltpu.VMEM((width, width), bf16)],
        table,
        gates=gates,
    )


def whole_fc_kernel(table, *refs):
    pieces, out, held, sems = refs[:4], refs[4], refs[5], refs[6]
    copies = [
        pltpu.make_async_copy(piece, held.at[table[j]], sems.at[j])
        for j, piece in enumerate(pieces)
    ]
    for copy in copies:
        copy.start()
    for copy in copies:
        copy.wait()
    ranks = len(pieces)
    units = pieces[0].shape[0]
    for r in range(ranks):
        for i in range(pieces[0].shape[1] // units):
            first = (i * ranks + r) * units
            out[:, first : first + units] = held[r, :, i * units : (i + 1) * units].astype(f32)


def whole_fc(table, pieces, gates):
    rows, width = pieces[0].shape
    ranks = len(pieces)
    return call(
        whole_fc_kernel,
        "whole_fc",
        1,
        pieces,
        [pl.BlockSpec(memory_space=pl.ANY)] * ranks,
        [((rows, ranks * width), f32)],
        [whole((rows, ranks * width))],
        [pltpu.VMEM((ranks, rows, width), bf16), pltpu.SemaphoreType.DMA((ranks,))],
        table,
        gates,
    )[0]


def whole_qkv_kernel(table, *refs):
    pieces, out, held, sems = refs[:4], refs[4], refs[5], refs[6]
    copies = [
        pltpu.make_async_copy(piece, held.at[table[j]], sems.at[j])
        for j, piece in enumerate(pieces)
    ]
    for copy in copies:
        copy.start()
    for copy in copies:
        copy.wait()
    width = out.shape[1] // 3
    for rank in range(len(pieces)):
        for part in range(3):
            start = part * width + rank * BASE * HD
            for p in range(SLOTS // 2):
                tile = held[rank, :, (3 * p + part) * PAIR : (3 * p + part + 1) * PAIR]
                out[:, start + p * PAIR : start + (p + 1) * PAIR] = tile.astype(f32)
            if rank == len(pieces) - 1:
                first = 3 * (SLOTS // 2) * PAIR + part * HD
                tile = held[rank, :, first : first + HD]
                out[:, start + BASE * HD : start + SLOTS * HD] = tile.astype(f32)


def whole_qkv(table, pieces, width):
    rows = pieces[0].shape[0]
    return call(
        whole_qkv_kernel,
        "whole_qkv",
        1,
        pieces,
        [pl.BlockSpec(memory_space=pl.ANY)] * len(pieces),
        [((rows, 3 * width), f32)],
        [whole((rows, 3 * width))],
        [
            pltpu.VMEM((len(pieces),) + pieces[0].shape, bf16),
            pltpu.SemaphoreType.DMA((len(pieces),)),
        ],
        table,
    )[0]


def to_pairs(parts):
    pieces = []
    for p in range(SLOTS // 2):
        pieces += [part[:, p * PAIR : (p + 1) * PAIR] for part in parts]
    pieces += [part[:, (SLOTS - 1) * HD :] for part in parts]
    pieces.append(jnp.zeros((parts[0].shape[0], HD), parts[0].dtype))
    return jnp.concatenate(pieces, axis=1)


def from_pairs(matrix, part, last):
    pieces = [
        matrix[:, (3 * p + part) * PAIR : (3 * p + part + 1) * PAIR] for p in range(SLOTS // 2)
    ]
    if last:
        start = 3 * (SLOTS // 2) * PAIR + part * HD
        pieces.append(matrix[:, start : start + HD])
    return pieces


def per_device(
    tokens_in,
    group_order,
    out_grad,
    w_qkv,
    w_attn_out,
    b_query,
    b_value,
    b_attn_out,
    w_fc,
    w_proj,
    b_fc,
    b_proj,
    ln1_gain,
    ln1_bias,
    ln2_gain,
    ln2_bias,
):
    ctx = lax.axis_size("ctx")
    shards = lax.axis_size("fsdp")
    rank = lax.axis_index("ctx")
    tokens = tokens_in[0].astype(f32)
    count, width = tokens.shape
    span = SLOTS * HD
    step = BASE * HD
    mixed_width = (3 * span + PAIR - 1) // PAIR * PAIR
    attn_width = mixed_width + span
    shard_rows = w_qkv.shape[0]
    unit_rows = w_proj.shape[0] // ctx
    peers = [rank ^ bit for bit in PEERS]
    owners = ring_owners() if on_ring() else None

    always = group_order[0] >= 0
    peer_table = jnp.stack(peers).astype(jnp.int32)

    slots = jnp.argsort(group_order).astype(jnp.int32)
    place = jnp.take(jnp.asarray(np.argsort(np.array(PEERS)).astype(np.int32)), (slots // 2) ^ rank)
    slot_rows = (place * 2 + slots % 2) * GROUP
    table = jnp.concatenate([slot_rows, (rank == ctx - 1).astype(jnp.int32)[None]])

    attn_block, vectors = form_attn_block(
        rank[None].astype(jnp.int32),
        w_qkv,
        w_attn_out,
        (b_query, b_value, b_attn_out, b_proj, ln1_gain, ln1_bias, ln2_gain, ln2_bias),
        b_fc,
    )
    own_tokens = tokens_in[0]
    own_grad = out_grad[0]
    attn_gather = Gather(attn_block)
    attn_gather.hop()
    small, bit = vectors[None], 1
    while bit < shards:
        small = spread_small(small, bit)
        bit *= 2
    w_fc = after(w_fc, attn_block)
    fc_block = jnp.concatenate(
        [
            lax.dynamic_slice(
                w_fc, (0, (i * ctx + rank) * unit_rows), (shard_rows, unit_rows)
            )
            for i in range(shards)
        ],
        axis=1,
    )
    proj_block = lax.dynamic_slice(w_proj, (rank * unit_rows, 0), (unit_rows, width))
    feed_block = jnp.concatenate([fc_block, proj_block])
    token_blocks = gather_ctx(own_tokens)
    grad_blocks = gather_ctx(after(own_grad, token_blocks[1]))
    attn_gather.hop()
    attn_gather.hop()
    feed_gather = Gather(feed_block)

    def my_bias(vector):
        return lax.dynamic_slice(vector, (rank * step,), (span,))[None]

    def slot_zero():
        moved = attn_gather.step(), feed_gather.step()

        def beside():
            lines = small.astype(f32)
            values = [lines[:, t, :shard_rows].reshape(-1) for t in range(VECTOR_ROWS)]
            units = lax.dynamic_index_in_dim(
                lines[:, 0, FC_START : FC_START + ctx * unit_rows].reshape(
                    shards, ctx, unit_rows
                ),
                rank,
                1,
                False,
            ).reshape(-1)
            mixed_bias = to_pairs(
                [my_bias(values[0]), jnp.zeros((1, span), f32), my_bias(values[1])]
            )
            return mixed_bias, values[2:], units

        return moved, slot(always, beside)

    (attn_moved, feed_moved), (bias_mixed, values, bias_fc) = slot(always, slot_zero)
    attn_gather.take(attn_moved)
    feed_gather.take(feed_moved)
    bias_o, bias_p, gain_one, shift_one, gain_two, shift_two = values
    qkv_weights, out_columns = attn_gather.result(
        owners, ((0, mixed_width, 0, shard_rows), (mixed_width, span, 0, shard_rows))
    )
    qkv_weights = qkv_weights.reshape(width, mixed_width)

    normed_all, mixed = norm_mixed(
        [after(token_blocks[0], grad_blocks[3])] + token_blocks[1:],
        gain_one,
        shift_one,
        qkv_weights,
        bias_mixed,
    )
    attended_mine, mass = attend(table, mixed, feed_gather.arrived())
    feed_gather.hop()
    out_blocks = gather_ctx(out_columns.reshape(width, span))
    out_weights = join_windows(peer_table, out_blocks, width)
    pieces = exchange_far(
        *exchange_near(*halves(after(row_major(attended_mine[:, :span]), out_blocks[1])))
    )
    middle, normed_two, attended = attn_out(
        peer_table,
        pieces,
        out_weights,
        after(own_tokens, *feed_gather.arrived()),
        bias_o,
        gain_two,
        shift_two,
    )
    feed_gather.hop()

    normed_far = ctx_swap(normed_two, 2)
    normed_blocks = [
        normed_two,
        normed_far,
        ctx_swap(normed_two, 1),
    ]
    feed_gather.hop()
    normed_blocks.append(ctx_swap(after(normed_far, *feed_gather.arrived()), 1))
    grad_all = row_major(jnp.concatenate([after(grad_blocks[0], normed_two)] + grad_blocks[1:]))
    fc_weights, proj_weights = feed_gather.result(
        owners, ((0, width, 0, shard_rows), (0, width, shard_rows, unit_rows))
    )
    fc_weights = fc_weights.reshape(width, -1)
    proj_weights = proj_weights.reshape(-1, width)
    activated, slope, normed_two_all = feed_up(
        [after(normed_blocks[0], grad_all)] + normed_blocks[1:], fc_weights, bias_fc
    )

    grad_proj = row_major(outer_sum(activated, grad_all).astype(bf16))
    proj_blocks = grad_proj.reshape(shards, unit_rows, width)

    def slot_one():
        moved = ring_step(proj_blocks, owners, 4)
        return moved, feed_back(grad_blocks, proj_weights, slope, ())

    proj_moved, (before_low, grad_bias_fc) = slot(always, slot_one)

    def slot_two():
        moved = ring_step(proj_blocks, owners, 3, proj_moved)

        def beside():
            keep, give = plain_back(before_low, fc_weights, "feed_back_two")
            return keep, ctx_swap(give, 1)

        return moved, slot(always, beside)

    proj_moved, (keep_two, got_two) = slot(always, slot_two)

    def slot_three():
        moved = ring_step(proj_blocks, owners, 2, proj_moved)

        def beside():
            kept, onward = pair_add(keep_two, got_two)
            grad_fc = row_major(outer_sum(normed_two_all, before_low).astype(bf16))
            branch = row_major(product(activated, proj_weights).astype(bf16))
            return kept, ctx_swap(onward, 2), grad_fc, halves(branch)

        return moved, slot(always, beside)

    proj_moved, (kept_two, far_two, grad_fc, branch_halves) = slot(always, slot_three)
    fc_blocks = grad_fc.reshape(shards, shard_rows, shards * unit_rows)

    def slot_four():
        moved = packed_step(proj_blocks, fc_blocks, owners, proj_moved)

        def beside():
            grad_middle, low, keep, give, sums = norm_two_back(
                peer_table, kept_two, far_two, middle, own_grad, gain_two, out_weights, ()
            )
            near = exchange_near(keep.reshape(-1, span), give.reshape(-1, span))
            out_pair = out_weight_grad(peer_table, attended, low, ())
            return grad_middle, low, sums, exchange_far(*near), out_pair

        return moved, slot(always, beside)

    proj_moved, (grad_middle, middle_low, sums_two, heads, out_pair) = slot(
        always, slot_four
    )
    out_keep, out_give = [value.reshape(-1, span) for value in out_pair]

    def slot_five():
        moved = ring_step(fc_blocks, owners, 3, proj_moved)

        def beside():
            shard = ring_end(proj_blocks, owners, proj_moved)
            far, near, got = ctx_swap(shard, 2), ctx_swap(shard, 1), ctx_swap(out_give, 1)
            return [shard, far, near], got, attend_back(table, mixed, heads, mass, ())

        return moved, slot(always, beside)

    fc_moved, (proj_pieces, got_out, grad_mixed) = slot(always, slot_five)

    def slot_six():
        moved = ring_step(fc_blocks, owners, 2, fc_moved)

        def beside():
            last = ctx_swap(proj_pieces[1], 1)
            kept, first, second = pair_split(out_keep, got_out)
            far = ctx_swap(first, 2)
            grad_qkv = row_major(outer_sum(normed_all, grad_mixed).astype(bf16))
            return last, kept, second, far, grad_qkv

        return moved, slot(always, beside)

    fc_moved, (proj_last, kept_out, onward_out, far_first, grad_qkv) = slot(always, slot_six)
    proj_pieces = proj_pieces + [proj_last]
    qkv_blocks = grad_qkv.reshape(shards, shard_rows, mixed_width)

    def partial_table():
        bias_sums = jnp.sum(grad_mixed.astype(f32), axis=0, keepdims=True)

        def all_heads(part):
            mine = jnp.concatenate(from_pairs(bias_sums, part, True), axis=1)
            return lax.dynamic_update_slice(jnp.zeros((1, width), f32), mine, (0, rank * step))

        whole_bias_fc = lax.dynamic_update_slice(
            jnp.zeros((shards, ctx, unit_rows), f32),
            grad_bias_fc.reshape(shards, 1, unit_rows),
            (0, rank, 0),
        )
        return [
            value.reshape(shards, -1)
            for value in (all_heads(0), all_heads(2), *sums_two, whole_bias_fc)
        ]

    def whole_table(part, sums):
        one = [value.reshape(shards, -1) for value in sums]
        query, value, gain_two_sum, shift_two_sum, out, down, units = part
        return jnp.concatenate(
            [query, value, out, down, *one, gain_two_sum, shift_two_sum, units], axis=1
        )

    def slot_seven():
        moved = packed_step(fc_blocks, qkv_blocks, owners, fc_moved)

        def beside():
            far = ctx_swap(onward_out, 2)

            def inmost():
                keep, give = plain_back(grad_mixed, qkv_weights, "mixed_back")
                return pair_add(keep, ctx_swap(give, 1))

            return far, slot(always, inmost)

        return moved, slot(always, beside)

    fc_moved, (far_second, (kept_one, onward_one)) = slot(always, slot_seven)

    twin = [
        value.reshape(-1, shard_rows, span) for value in (kept_out, far_first, far_second)
    ]

    def slot_eight():
        qkv_next = twin_step(qkv_blocks, twin, owners, 3, fc_moved)

        def beside():
            far = ctx_swap(onward_one, 2)
            got = ctx_swap(branch_halves[1], 1)

            def inmost():
                shard = ring_end(fc_blocks, owners, fc_moved)
                return shard, partial_table(), whole_rows(peer_table, proj_pieces, ())

            return far, got, slot(always, inmost)

        return qkv_next, slot(always, beside)

    qkv_moved, (far_one, got_branch, (shard_fc, table_part, grad_w_proj)) = slot(
        always, slot_eight
    )

    def slot_nine():
        qkv_next = twin_step(qkv_blocks, twin, owners, 2, qkv_moved)

        def beside():
            far, near = ctx_swap(shard_fc, 2), ctx_swap(shard_fc, 1)

            def inmost():
                kept, onward = pair_add(branch_halves[0], got_branch)
                back, sums = norm_one_back(
                    kept_one, far_one, own_tokens, grad_middle, gain_one, ()
                )
                return kept, onward, back, whole_table(table_part, sums)

            return [shard_fc, far, near], slot(always, inmost)

        return qkv_next, slot(always, beside)

    qkv_moved, (fc_pieces, beside_nine) = slot(always, slot_nine)
    kept_branch, onward_branch, grad_tokens, small = beside_nine

    def slot_ten():
        held = halve_small(small, shards // 2)
        qkv_next = twin_step(qkv_blocks, twin, owners, 1, qkv_moved)
        far, last = ctx_swap(onward_branch, 2), ctx_swap(fc_pieces[1], 1)
        return qkv_next, held, far, last

    qkv_moved, held, far_branch, fc_last = slot(always, slot_ten)

    def slot_eleven():
        shard_qkv, out_next = twin_end(qkv_blocks, twin, owners, qkv_moved)
        far, near = ctx_swap(shard_qkv, 2), ctx_swap(shard_qkv, 1)
        next_held = halve_small(held, shards // 4)

        def beside():
            out = (middle + added(kept_branch, far_branch) + bias_p).astype(bf16)[None]
            return whole_fc(peer_table, fc_pieces + [fc_last], ()), out

        return [shard_qkv, far, near], out_next, next_held, slot(always, beside)

    qkv_pieces, out_moved, held, (grad_w_fc, tokens_out) = slot(always, slot_eleven)
    def slot_twelve():
        shard_out = twin_last(twin, owners, out_moved)
        swaps = [ctx_swap(shard_out, 2), ctx_swap(shard_out, 1)]
        return [shard_out, *swaps], ctx_swap(qkv_pieces[1], 1), halve_small(held, shards // 8)

    out_pieces, qkv_last, held = slot(always, slot_twelve)
    held = finish_small(held, shards // 16)

    def slot_thirteen():
        last = ctx_swap(out_pieces[1], 1)
        total = held[0] + ctx_swap(held[0], 1)
        return last, total, slot(
            always, lambda: whole_qkv(peer_table, qkv_pieces + [qkv_last], width)
        )

    out_last, summed, grad_w_qkv = slot(always, slot_thirteen)
    summed = summed + ctx_swap(summed, 2)
    whole_attn_out = join_windows(peer_table, out_pieces + [out_last], width).astype(f32)
    shares = [summed[t * shard_rows : (t + 1) * shard_rows] for t in range(8)]
    share_fc = summed[8 * shard_rows :]
    grad_tokens = grad_tokens[None]

    return (
        tokens_out,
        grad_tokens,
        grad_w_qkv,
        whole_attn_out,
        shares[0],
        shares[1],
        shares[2],
        grad_w_fc,
        grad_w_proj,
        share_fc,
        shares[3],
        shares[4],
        shares[5],
        shares[6],
        shares[7],
    )


def solution(mesh):
    placed = (
        P("fsdp", "ctx", None),
        P(),
        P("fsdp", "ctx", None),
        P("fsdp", None),
        P("fsdp", None),
        P("fsdp"),
        P("fsdp"),
        P("fsdp"),
        P("fsdp", None),
        P("fsdp", None),
        P("fsdp"),
        P("fsdp"),
        P("fsdp"),
        P("fsdp"),
        P("fsdp"),
        P("fsdp"),
    )
    return jax.shard_map(
        per_device,
        mesh=mesh,
        in_specs=placed,
        out_specs=(
            P("fsdp", "ctx", None),
            P("fsdp", "ctx", None),
            P("fsdp", None),
            P("fsdp", None),
            P("fsdp"),
            P("fsdp"),
            P("fsdp"),
            P("fsdp", None),
            P("fsdp", None),
            P("fsdp"),
            P("fsdp"),
            P("fsdp"),
            P("fsdp"),
            P("fsdp"),
            P("fsdp"),
        ),
        check_vma=False,
    )
```

```python
import functools

import jax
import jax.numpy as jnp
import numpy as np
from jax import lax
from jax.experimental import pallas as pl
from jax.experimental.layout import Layout, with_layout_constraint
from jax.experimental.pallas import tpu as pltpu
from jax.sharding import PartitionSpec as P

H = 25
HD = 64
GROUP = 128
QB = 256
PAIR = 2 * HD
RANKS = 4
BASE = H // RANKS
SLOTS = H - (RANKS - 1) * BASE
norm_eps = 1e-05
masked_low = -1e30
LIGHT = pl.CostEstimate(flops=1 << 20, transcendentals=0, bytes_accessed=1 << 16)
VMEM_LIMIT = 40 << 20
f32 = jnp.float32
bf16 = jnp.bfloat16


def outer_sum(left_op, right_op):
    return lax.dot_general(
        left_op, right_op, (((0,), (0,)), ((), ())), preferred_element_type=f32
    )


def back_product(left_op, right_op):
    return lax.dot_general(
        left_op, right_op, (((1,), (1,)), ((), ())), preferred_element_type=f32
    )


def product(left_op, right_op):
    return jnp.dot(left_op, right_op, preferred_element_type=f32)


def added(*terms):
    total = terms[0].astype(f32)
    for term in terms[1:]:
        total = total + term.astype(f32)
    return total


def row_major(matrix):
    return with_layout_constraint(matrix, Layout(major_to_minor=tuple(range(matrix.ndim))))


def slot(always, step):
    empty = jax.eval_shape(step)
    return lax.cond(
        always,
        step,
        lambda: jax.tree.map(lambda leaf: jnp.zeros(leaf.shape, leaf.dtype), empty),
    )


def after(value, *others):
    return lax.optimization_barrier((value,) + others)[0]


PEERS = (0, 2, 1, 3)


def tiled(block):
    if block.ndim != 2 or block.shape[0] % 8:
        return block
    return block.reshape(-1, 8, block.shape[1])


def ctx_swap(block, bit):
    pairs = [(i, i ^ bit) for i in range(lax.axis_size("ctx"))]
    got = row_major(lax.ppermute(row_major(tiled(block)), "ctx", pairs))
    return got.reshape(block.shape)


def gather_ctx(block):
    far = ctx_swap(block, 2)
    near = ctx_swap(block, 1)
    return [block, far, near, ctx_swap(far, 1)]


def halves(matrix):
    half = matrix.shape[0] // 2
    return matrix[:half], matrix[half:]


def pair_add_kernel(keep, got, kept, onward):
    rows = kept.shape[0]
    kept[...] = added(keep[:rows], got[:rows]).astype(kept.dtype)
    onward[...] = added(keep[rows:], got[rows:]).astype(bf16)


def pair_add(keep, got, kind=f32):
    rows, columns = keep.shape
    half = (rows // 2, columns)
    return call(
        pair_add_kernel,
        "pair_add",
        1,
        (keep, got),
        [whole(keep.shape)] * 2,
        [(half, kind), (half, bf16)],
        [whole(half)] * 2,
    )


def pair_split_kernel(keep, got, kept, first, second):
    rows = kept.shape[0]
    half = rows // 2
    kept[...] = added(keep[:rows], got[:rows]).astype(kept.dtype)
    first[...] = added(keep[rows : rows + half], got[rows : rows + half]).astype(bf16)
    second[...] = added(keep[rows + half :], got[rows + half :]).astype(bf16)


def pair_split(keep, got):
    rows, columns = keep.shape
    half, quarter = (rows // 2, columns), (rows // 4, columns)
    return call(
        pair_split_kernel,
        "pair_split",
        1,
        (keep, got),
        [whole(keep.shape)] * 2,
        [(half, bf16), (quarter, bf16), (quarter, bf16)],
        [whole(half), whole(quarter), whole(quarter)],
    )


def exchange_near(keep, give):
    quarter = keep.shape[0] // 2
    got = ctx_swap(give, 1)
    return keep[:quarter], got[:quarter], jnp.concatenate([keep[quarter:], got[quarter:]])


def exchange_far(mine, near, onward):
    quarter = mine.shape[0]
    got = ctx_swap(onward, 2)
    return [mine, got[:quarter], near, got[quarter:]]


RING = (0, 2, 4, 6, 7, 5, 3, 1)
HALF = len(RING) // 2


def ring_hop(value, step):
    count = len(RING)
    pairs = [(RING[q], RING[(q + step) % count]) for q in range(count)]
    return row_major(lax.ppermute(row_major(value), "fsdp", pairs))


def ring_owners():
    place = jnp.asarray(np.argsort(np.array(RING)).astype(np.int32))
    mine = lax.dynamic_index_in_dim(place, lax.axis_index("fsdp"), 0, False)
    offsets = np.array([0, -1, 1, -2, 2, -3, 3, 4], np.int32)
    return jnp.take(jnp.asarray(np.array(RING, np.int32)), (mine + offsets) % len(RING))


def on_ring():
    return lax.axis_size("fsdp") == len(RING)


def upper_part(rows):
    return rows // 16 * 8


class Gather:
    def __init__(self, block):
        self.block = block
        self.cut = upper_part(block.shape[0])
        self.pieces = [block]
        self.forth = self.back = block

    def step(self):
        if not on_ring():
            return ()
        forth, back = self.forth, self.back
        if len(self.pieces) == 2 * HALF - 1:
            forth, back = forth[: self.cut], back[self.cut :]
        return ring_hop(forth, 1), ring_hop(back, -1)

    def take(self, moved):
        if moved:
            self.forth, self.back = moved
            self.pieces += list(moved)

    def hop(self):
        self.take(self.step())

    def arrived(self):
        return (self.forth, self.back) if on_ring() else ()

    def result(self, owners, columns, gates=()):
        if not on_ring():
            whole = lax.all_gather(self.block, "fsdp", axis=0, tiled=False)
            return [whole[:, top : top + n, c : c + w] for c, w, top, n in columns]
        return collect(self.pieces, owners, self.cut, columns, gates)


def spread_small(held, bit):
    got = lax.ppermute(held, "fsdp", [(i, i ^ bit) for i in range(lax.axis_size("fsdp"))])
    low = (lax.axis_index("fsdp") & bit) == 0
    return jnp.concatenate([jnp.where(low, held, got), jnp.where(low, got, held)])


def collect_kernel(cut, columns, owners, *refs):
    pieces = refs[: 2 * HALF + 1]
    outs = refs[2 * HALF + 1 : 2 * HALF + 1 + len(columns)]
    sems = refs[-1]
    copies = []
    for out, (start, width, top, rows) in zip(outs, columns):
        for j, piece in enumerate(pieces):
            first = cut if j == 2 * HALF else 0
            low = max(top, first)
            high = min(top + rows, first + piece.shape[0])
            if low < high:
                copies.append(
                    pltpu.make_async_copy(
                        piece.at[pl.ds(low - first, high - low), pl.ds(start, width)],
                        out.at[owners[min(j, 2 * HALF - 1)], pl.ds(low - top, high - low)],
                        sems.at[len(copies)],
                    )
                )
    for copy in copies:
        copy.start()
    for copy in copies:
        copy.wait()


def collect(pieces, owners, cut, columns, gates):
    shapes = [(len(RING), rows, width) for _, width, _, rows in columns]
    return call(
        functools.partial(collect_kernel, cut, columns),
        "collect",
        1,
        pieces,
        [pl.BlockSpec(memory_space=pl.ANY)] * len(pieces),
        [(shape, pieces[0].dtype) for shape in shapes],
        [whole(shape) for shape in shapes],
        [pltpu.SemaphoreType.DMA((len(pieces) * len(columns),))],
        owners,
        gates,
    )


PLACE = {0: 0, -1: 1, 1: 2, -2: 3, 2: 4, -3: 5, 3: 6, 4: 7}


def half_blocks(cut, rows, width, forth, back):
    return forth[forth.shape[0] - cut :, :width], back[back.shape[0] - (rows - cut) :, :width]


def ring_part_kernel(distance, cut, owners, *refs):
    if distance == HALF:
        far, ahead, behind = refs
        ahead[...] = far[:cut]
        behind[...] = far[cut:]
    elif distance == 0:
        own, forth, back, out = refs
        rows = own.shape[0]
        out[...] = added(own[...], forth[:rows], back[:rows]).astype(bf16)
    else:
        mine_ahead, mine_behind, forth, back, ahead, behind = refs
        if distance == HALF - 1:
            rows, width = mine_ahead.shape
            from_forth, from_back = half_blocks(cut, rows, width, forth, back)
            ahead[:cut] = added(mine_ahead[:cut], from_forth).astype(bf16)
            ahead[cut:] = mine_ahead[cut:]
            behind[:cut] = mine_behind[:cut]
            behind[cut:] = added(mine_behind[cut:], from_back).astype(bf16)
        else:
            ahead[...] = added(mine_ahead[...], forth[...]).astype(bf16)
            behind[...] = added(mine_behind[...], back[...]).astype(bf16)


def ring_part(blocks, owners, distance, cut, moved, gates=()):
    rows, columns = blocks.shape[1:]
    distances = (distance,) if distance in (0, HALF) else (distance, -distance)
    if distance == HALF:
        shapes = [(cut, columns), (rows - cut, columns)]
    else:
        shapes = [(rows, columns)] * len(distances)
    places = [PLACE[d] for d in distances]
    return call(
        functools.partial(ring_part_kernel, distance, cut),
        "ring_part",
        1,
        (*[blocks] * len(places), *moved),
        [
            pl.BlockSpec((None, rows, columns), lambda i, t, p=p: (t[p], 0, 0)) for p in places
        ]
        + [whole(value.shape) for value in moved],
        [(shape, bf16) for shape in shapes],
        [whole(shape) for shape in shapes],
        table=owners,
        gates=gates,
    )


def packed_kernel(cut, owners, mine_ahead, mine_behind, forth, back, far, ahead, behind):
    rows, width = mine_ahead.shape
    second = far.shape[1]
    ahead[:rows] = added(mine_ahead[...], forth[...]).astype(bf16)
    behind[:rows] = added(mine_behind[...], back[...]).astype(bf16)
    ahead[rows:, :second] = far[:cut]
    behind[rows:, :second] = far[cut:]
    if second < width:
        ahead[rows:, second:] = jnp.zeros((cut, width - second), bf16)
        behind[rows:, second:] = jnp.zeros((rows - cut, width - second), bf16)


def packed_step(blocks, others, owners, moved):
    if not on_ring():
        return ()
    rows, width = blocks.shape[1:]
    cut = upper_part(rows)
    shapes = [(rows + cut, width), (2 * rows - cut, width)]
    ahead, behind = call(
        functools.partial(packed_kernel, cut),
        "packed_part",
        1,
        (blocks, blocks, *moved, others),
        [
            pl.BlockSpec((None, rows, width), lambda i, t, p=PLACE[d]: (t[p], 0, 0))
            for d in (1, -1)
        ]
        + [whole(value.shape) for value in moved]
        + [pl.BlockSpec((None,) + others.shape[1:], lambda i, t: (t[PLACE[HALF]], 0, 0))],
        [(shape, bf16) for shape in shapes],
        [whole(shape) for shape in shapes],
        table=owners,
    )
    return ring_hop(ahead, 1), ring_hop(behind, -1)


def ring_step(blocks, owners, distance, moved=()):
    if not on_ring():
        return ()
    ahead, behind = ring_part(blocks, owners, distance, upper_part(blocks.shape[1]), moved)
    return ring_hop(ahead, 1), ring_hop(behind, -1)


def twin_block(owners, place, refs):
    kept, first, second = refs
    low = owners[place] < HALF
    return added(kept[...], jnp.where(low, first[...], second[...]))


def twin_kernel(distance, lag, cut, owners, *refs):
    width = refs[0].shape[-1]
    if distance == 0:
        own, forth, back, *twins = refs
        out, ahead, behind = twins[-3:]
        out[...] = added(own[...], forth[:, :width], back[:, :width]).astype(bf16)
        value_ahead = twin_block(owners, PLACE[lag], twins[0:3])
        value_behind = twin_block(owners, PLACE[-lag], twins[3:6])
        ahead[...] = added(value_ahead, forth[:, width:]).astype(bf16)
        behind[...] = added(value_behind, back[:, width:]).astype(bf16)
        return
    mine_ahead, mine_behind, forth, back, *twins = refs
    ahead, behind = twins[-2:]
    if distance == HALF - 1:
        from_forth, from_back = half_blocks(cut, mine_ahead.shape[0], width, forth, back)
        ahead[:cut, :width] = added(mine_ahead[:cut], from_forth).astype(bf16)
        ahead[cut:, :width] = mine_ahead[cut:]
        behind[:cut, :width] = mine_behind[:cut]
        behind[cut:, :width] = added(mine_behind[cut:], from_back).astype(bf16)
        value = twin_block(owners, PLACE[HALF], twins[0:3]).astype(bf16)
        ahead[:cut, width:] = value[:cut]
        ahead[cut:, width:] = jnp.zeros_like(value[cut:])
        behind[:cut, width:] = jnp.zeros_like(value[:cut])
        behind[cut:, width:] = value[cut:]
    else:
        ahead[:, :width] = added(mine_ahead[...], forth[:, :width]).astype(bf16)
        behind[:, :width] = added(mine_behind[...], back[:, :width]).astype(bf16)
        value_ahead = twin_block(owners, PLACE[lag], twins[0:3])
        value_behind = twin_block(owners, PLACE[-lag], twins[3:6])
        ahead[:, width:] = added(value_ahead, forth[:, width:]).astype(bf16)
        behind[:, width:] = added(value_behind, back[:, width:]).astype(bf16)


def twin_part(blocks, twin, owners, distance, moved):
    rows, width = blocks.shape[1:]
    span = twin[0].shape[2]
    lag = distance + 1
    mains = (distance, -distance) if distance else (0,)
    lags = (lag, -lag) if lag < HALF else (lag,)
    specs = [
        pl.BlockSpec((None, rows, width), lambda i, t, p=PLACE[d]: (t[p], 0, 0)) for d in mains
    ]
    specs += [whole(value.shape) for value in moved]
    for d in lags:
        p = PLACE[d]
        specs += [
            pl.BlockSpec((None, rows, span), lambda i, t, p=p: (t[p], 0, 0)),
            pl.BlockSpec(
                (None, rows, span), lambda i, t, p=p: (jnp.minimum(t[p], HALF - 1), 0, 0)
            ),
            pl.BlockSpec((None, rows, span), lambda i, t, p=p: (jnp.maximum(t[p] - HALF, 0), 0, 0)),
        ]
    if distance:
        shapes = [(rows, width + span)] * 2
    else:
        shapes = [(rows, width), (rows, span), (rows, span)]
    return call(
        functools.partial(twin_kernel, distance, lag, upper_part(rows)),
        "twin_part",
        1,
        (*[blocks] * len(mains), *moved, *twin * len(lags)),
        specs,
        [(shape, bf16) for shape in shapes],
        [whole(shape) for shape in shapes],
        table=owners,
    )


def twin_last_kernel(owners, forth, back, kept, first, second, out):
    value = twin_block(owners, PLACE[0], (kept, first, second))
    out[...] = added(value, forth[...], back[...]).astype(bf16)


def twin_last(twin, owners, moved):
    if not on_ring():
        blocks = added(twin[0], jnp.concatenate(twin[1:])).astype(bf16)
        return ring_end(blocks, owners, moved)
    rows, span = twin[0].shape[1:]
    block = (None, rows, span)
    return call(
        twin_last_kernel,
        "twin_last",
        1,
        (*moved, *twin),
        [whole((rows, span))] * 2
        + [
            pl.BlockSpec(block, lambda i, t: (t[0], 0, 0)),
            pl.BlockSpec(block, lambda i, t: (jnp.minimum(t[0], HALF - 1), 0, 0)),
            pl.BlockSpec(block, lambda i, t: (jnp.maximum(t[0] - HALF, 0), 0, 0)),
        ],
        [((rows, span), bf16)],
        [whole((rows, span))],
        table=owners,
    )[0]


def twin_step(blocks, twin, owners, distance, moved):
    if not on_ring():
        return ()
    ahead, behind = twin_part(blocks, twin, owners, distance, moved)
    return ring_hop(ahead, 1), ring_hop(behind, -1)


def twin_end(blocks, twin, owners, moved):
    if not on_ring():
        return ring_end(blocks, owners, moved), ()
    out, ahead, behind = twin_part(blocks, twin, owners, 0, moved)
    return out, (ring_hop(ahead, 1), ring_hop(behind, -1))


def ring_end(blocks, owners, moved):
    if not on_ring():
        return lax.psum_scatter(blocks, "fsdp", scatter_dimension=0, tiled=False)
    return ring_part(blocks, owners, 0, upper_part(blocks.shape[1]), moved)[0]


def halve_small(held, bit):
    me = lax.axis_index("fsdp")
    parts = held.reshape(2, bit, -1)
    high = (me & bit) != 0
    keep = jnp.where(high, parts[1], parts[0])
    give = jnp.where(high, parts[0], parts[1])
    pairs = [(i, i ^ bit) for i in range(lax.axis_size("fsdp"))]
    return keep + lax.ppermute(give, "fsdp", pairs)


def finish_small(held, bit):
    while bit:
        held = halve_small(held, bit)
        bit //= 2
    return held


def norm_stats(values):
    centre = values - jnp.mean(values, axis=-1, keepdims=True)
    scale = lax.rsqrt(jnp.mean(centre * centre, axis=-1, keepdims=True) + norm_eps)
    return centre * scale, scale


def norm_back(grad, unit, scale, gain):
    inner = grad * gain
    back = scale * (
        inner
        - jnp.mean(inner, axis=-1, keepdims=True)
        - unit * jnp.mean(inner * unit, axis=-1, keepdims=True)
    )
    return back, jnp.sum(grad * unit, axis=0), jnp.sum(grad, axis=0)


def across(left_op, right_op, left_dim, right_dim):
    return lax.dot_general(
        left_op, right_op, (((left_dim,), (right_dim,)), ((), ())), preferred_element_type=f32
    )


def diagonal_kept():
    shape = (QB, QB)
    return lax.broadcasted_iota(jnp.int32, shape, 0) <= lax.broadcasted_iota(jnp.int32, shape, 1)


def sorted_tile(table, ref, columns):
    groups = ref.shape[0] // GROUP
    return jnp.concatenate(
        [ref[pl.ds(pl.multiple_of(table[g], GROUP), GROUP), columns] for g in range(groups)],
        axis=0,
    )


def put_sorted(table, ref, columns, first, value):
    for j in range(value.shape[0] // GROUP):
        start = pl.multiple_of(table[first + j], GROUP)
        ref[pl.ds(start, GROUP), columns] = value[j * GROUP : (j + 1) * GROUP]


def split_heads(tiles, last):
    if last:
        return [(tiles[0][:, :HD], tiles[0][:, HD:], tiles[1][:, :HD])]
    return [tuple(t[:, w * HD : (w + 1) * HD] for t in tiles) for w in range(2)]


def pair_columns(pair, last):
    if last:
        start = SLOTS // 2 * 3 * PAIR
        return [slice(start, start + PAIR), slice(start + PAIR, start + 2 * PAIR)]
    return [pl.ds(pl.multiple_of(pair * 3 * PAIR + t * PAIR, PAIR), PAIR) for t in range(3)]


def attend_pair(pair, last, table, qkv_ref, out_ref, mass_ref):
    tiles = [sorted_tile(table, qkv_ref, c) for c in pair_columns(pair, last)]
    heads = split_heads(tiles, last)
    length = qkv_ref.shape[0]
    kept = diagonal_kept()
    ready = [(q * bf16(HD**-0.5), k, v.T) for q, k, v in heads]
    for i in range(length // QB):
        rows = slice(i * QB, (i + 1) * QB)
        outs = []
        for w, (queries, keys, values_t) in enumerate(ready):
            mine = queries[rows]
            diag = jnp.where(kept, across(keys[rows], mine, 1, 1), masked_low)
            peak = jnp.max(diag, axis=0, keepdims=True)
            if i:
                rest = across(keys[: i * QB], mine, 1, 1)
                peak = jnp.maximum(peak, jnp.max(rest, axis=0, keepdims=True))
            diag = jnp.exp(diag - peak)
            mass = jnp.sum(diag, axis=0, keepdims=True)
            out = across(values_t[:, rows], diag.astype(bf16), 1, 0)
            if i:
                rest = jnp.exp(rest - peak)
                mass = mass + jnp.sum(rest, axis=0, keepdims=True)
                out = out + across(values_t[:, : i * QB], rest.astype(bf16), 1, 0)
            outs.append(out / mass)
            mass_ref[0, w : w + 1, rows] = peak + jnp.log(mass)
        if last:
            outs.append(jnp.zeros_like(outs[0]))
        tile = jnp.concatenate(outs, axis=0).T.astype(bf16)
        put_sorted(table, out_ref, slice(None), 2 * i, tile)


def attend_kernel(table, qkv_ref, out_ref, mass_ref):
    pair = pl.program_id(0)
    final = pl.num_programs(0) - 1

    @pl.when(pair < final)
    def _():
        attend_pair(pair, False, table, qkv_ref, out_ref, mass_ref)

    @pl.when(pair == final)
    def _():
        mass_ref[...] = jnp.zeros_like(mass_ref)

        @pl.when(table[table.shape[0] - 1] == 0)
        def _():
            out_ref[...] = jnp.zeros_like(out_ref)

        @pl.when(table[table.shape[0] - 1] != 0)
        def _():
            attend_pair(pair, True, table, qkv_ref, out_ref, mass_ref)


def attend_back_pair(pair, last, table, qkv_ref, grad_ref, mass_ref, out_ref, acc):
    places = pair_columns(pair, last)
    heads = split_heads([sorted_tile(table, qkv_ref, c) for c in places], last)
    grads = sorted_tile(table, grad_ref, slice(None))
    length = qkv_ref.shape[0]
    kept = diagonal_kept()
    ready = [
        (q * bf16(HD**-0.5), k, k.T, v, grads[:, w * HD : (w + 1) * HD])
        for w, (q, k, v) in enumerate(heads)
    ]
    for i in range(length // QB):
        rows = slice(i * QB, (i + 1) * QB)
        query_tiles = []
        for w, (queries, keys, keys_t, values, grads_w) in enumerate(ready):
            mine = queries[rows]
            grad = grads_w[rows]
            mass = mass_ref[0, w : w + 1, rows]
            spans = [(rows, True)] + ([(slice(0, i * QB), False)] if i else [])
            probs, both, delta = [], [], None
            for span, diagonal in spans:
                scores = across(keys[span], mine, 1, 1)
                if diagonal:
                    scores = jnp.where(kept, scores, masked_low)
                prob = jnp.exp(scores - mass)
                prod = prob * across(values[span], grad, 1, 1)
                part = jnp.sum(prod, axis=0, keepdims=True)
                delta = part if delta is None else delta + part
                probs.append(prob)
                both.append(prod)
            query_t = None
            for (span, diagonal), prob, prod in zip(spans, probs, both):
                grad_scores = (prod - prob * delta).astype(bf16)
                part = across(keys_t[:, span], grad_scores, 1, 0)
                query_t = part if query_t is None else query_t + part
                key_part = across(grad_scores, mine, 1, 0)
                value_part = across(prob.astype(bf16), grad, 1, 0)
                if diagonal:
                    acc[2 * w, span, :] = key_part
                    acc[2 * w + 1, span, :] = value_part
                else:
                    acc[2 * w, span, :] += key_part
                    acc[2 * w + 1, span, :] += value_part
            query_tiles.append(query_t * HD**-0.5)
        if last:
            query_tiles.append(jnp.zeros_like(query_tiles[0]))
        tile = jnp.concatenate(query_tiles, axis=0).T
        if last:
            tile = jnp.concatenate([tile[:, :HD], jnp.zeros_like(tile[:, HD:])], axis=1)
        put_sorted(table, out_ref, places[0], 2 * i, tile.astype(bf16))
    if last:
        old = sorted_tile(table, out_ref, places[0])
        tile = jnp.concatenate([old[:, :HD], acc[0].astype(bf16)], axis=1)
        put_sorted(table, out_ref, places[0], 0, tile)
        tile = jnp.concatenate([acc[1].astype(bf16), jnp.zeros((length, HD), bf16)], axis=1)
        put_sorted(table, out_ref, places[1], 0, tile)
    else:
        for t in range(2):
            tile = jnp.concatenate([acc[t].astype(bf16), acc[2 + t].astype(bf16)], axis=1)
            put_sorted(table, out_ref, places[1 + t], 0, tile)


def attend_back_kernel(table, *refs):
    grad_refs, (qkv_ref, mass_ref, out_ref, acc, held) = refs[:4], refs[4:]
    pair = pl.program_id(0)
    final = pl.num_programs(0) - 1

    @pl.when(pair == 0)
    def _():
        span = SLOTS * HD
        rows = grad_refs[0].shape[0]
        for j, ref in enumerate(grad_refs):
            for p in range(span // PAIR):
                held[p, j * rows : (j + 1) * rows, :] = ref[:, p * PAIR : (p + 1) * PAIR]
            tail = jnp.concatenate([ref[:, span - HD :], jnp.zeros((rows, HD), bf16)], axis=1)
            held[span // PAIR, j * rows : (j + 1) * rows, :] = tail

    refs = (table, qkv_ref, held.at[pair], mass_ref, out_ref, acc)

    @pl.when(pair < final)
    def _():
        attend_back_pair(pair, False, *refs)

    @pl.when(pair == final)
    def _():
        @pl.when(table[table.shape[0] - 1] == 0)
        def _():
            for columns in pair_columns(pair, True):
                out_ref[:, columns] = jnp.zeros((out_ref.shape[0], PAIR), bf16)

        @pl.when(table[table.shape[0] - 1] != 0)
        def _():
            attend_back_pair(pair, True, *refs)


def attend(table, qkv, gates):
    length, columns = qkv.shape
    pairs = (SLOTS + 1) // 2
    return call(
        attend_kernel,
        "attend",
        pairs,
        (qkv,),
        [whole((length, columns))],
        [((length, pairs * PAIR), bf16), ((pairs, 8, length), f32)],
        [
            pl.BlockSpec((length, PAIR), lambda p, t: (0, p)),
            pl.BlockSpec((1, 8, length), lambda p, t: (p, 0, 0)),
        ],
        table=table,
        gates=gates,
    )


def attend_back(table, qkv, grads, mass, gates):
    length, columns = qkv.shape
    pairs = (SLOTS + 1) // 2
    return call(
        attend_back_kernel,
        "attend_back",
        pairs,
        (*grads, qkv, mass),
        [whole(grad.shape) for grad in grads]
        + [whole((length, columns)), pl.BlockSpec((1, 8, length), lambda p, t: (p, 0, 0))],
        [((length, columns), bf16)],
        [whole((length, columns))],
        [pltpu.VMEM((4, length, HD), f32), pltpu.VMEM((pairs, length, PAIR), bf16)],
        table,
        gates,
    )[0]


def whole(shape):
    return pl.BlockSpec(shape, lambda *_: (0,) * len(shape))


def rows_spec(rows, columns):
    return pl.BlockSpec((rows, columns), lambda i, *_: (i, 0))


def call(
    kernel,
    name,
    grid,
    operands,
    specs,
    outs,
    out_specs,
    scratch=(),
    table=None,
    gates=(),
    limit=VMEM_LIMIT,
):
    tables = () if table is None else (table,)
    first = len(tables) + len(operands)
    count = len(gates)

    def body(*refs):
        kernel(*refs[:first], *refs[first + count :])

    return pl.pallas_call(
        body,
        grid_spec=pltpu.PrefetchScalarGridSpec(
            num_scalar_prefetch=len(tables),
            grid=(grid,),
            in_specs=list(specs) + [pl.BlockSpec(memory_space=pl.ANY)] * count,
            out_specs=out_specs,
            scratch_shapes=list(scratch),
        ),
        out_shape=[jax.ShapeDtypeStruct(shape, kind) for shape, kind in outs],
        compiler_params=pltpu.CompilerParams(vmem_limit_bytes=limit),
        cost_estimate=LIGHT,
        name=name,
    )(*tables, *operands, *gates)


def pick_block(refs, held):
    for j, ref in enumerate(refs):

        @pl.when(pl.program_id(0) == j)
        def _(ref=ref):
            held[...] = ref[...]


def norm_mixed_kernel(*refs):
    blocks, (gain, shift, weights, bias, normed, mixed, held) = refs[:4], refs[4:]
    pick_block(blocks, held)
    unit, _ = norm_stats(held[...].astype(f32))
    low = (unit * gain[...] + shift[...]).astype(bf16)
    normed[...] = low
    mixed[...] = (product(low, weights[...]) + bias[...]).astype(bf16)


def norm_mixed(blocks, gain, shift, weights, bias):
    count, width = blocks[0].shape
    mixed_width = weights.shape[1]
    length = count * len(blocks)
    return call(
        norm_mixed_kernel,
        "norm_mixed",
        len(blocks),
        (*blocks, gain[None], shift[None], weights, bias),
        [whole((count, width))] * len(blocks)
        + [whole((1, width))] * 2
        + [whole(weights.shape), whole((1, mixed_width))],
        [((length, width), bf16), ((length, mixed_width), bf16)],
        [rows_spec(count, width), rows_spec(count, mixed_width)],
        [pltpu.VMEM((count, width), bf16)],
    )


def join_kernel(table, *refs):
    pieces, out, sems, last_sem = refs[:4], refs[4], refs[5], refs[6]
    step, span = BASE * HD, SLOTS * HD
    width = out.shape[1]
    rest = span - step
    last = len(pieces) - 1

    def copies(j):
        start = pl.multiple_of(table[j] * step, PAIR)
        main = pltpu.make_async_copy(
            pieces[j].at[:, pl.ds(0, step)], out.at[:, pl.ds(start, step)], sems.at[j]
        )
        tail = pltpu.make_async_copy(
            pieces[j].at[:, pl.ds(step, rest)], out.at[:, pl.ds(width - rest, rest)], last_sem.at[0]
        )
        return main, tail

    for j in range(len(pieces)):
        main, tail = copies(j)
        main.start()

        @pl.when(table[j] == last)
        def _(tail=tail):
            tail.start()

    for j in range(len(pieces)):
        main, tail = copies(j)
        main.wait()

        @pl.when(table[j] == last)
        def _(tail=tail):
            tail.wait()


def join_windows(table, pieces, width):
    rows = pieces[0].shape[0]
    return call(
        join_kernel,
        "join_windows",
        1,
        pieces,
        [pl.BlockSpec(memory_space=pl.ANY)] * len(pieces),
        [((rows, width), pieces[0].dtype)],
        [whole((rows, width))],
        [pltpu.SemaphoreType.DMA((len(pieces),)), pltpu.SemaphoreType.DMA((1,))],
        table,
    )[0]


def attn_out_kernel(table, *refs):
    pieces, rest = refs[:4], refs[4:]
    weights, tokens, bias, gain, shift, middle, normed, attended = rest
    step, span = BASE * HD, SLOTS * HD
    width = attended.shape[1]
    for j, piece in enumerate(pieces):
        start = pl.multiple_of(table[j] * step, PAIR)
        attended[:, pl.ds(start, step)] = piece[:, :step]

        @pl.when(table[j] == len(pieces) - 1)
        def _(piece=piece):
            attended[:, width - (span - step) :] = piece[:, step:]

    value = tokens[...].astype(f32) + product(attended[...], weights[...]) + bias[...]
    middle[...] = value
    unit, _ = norm_stats(value)
    normed[...] = (unit * gain[...] + shift[...]).astype(bf16)


def attn_out(table, pieces, weights, tokens, bias, gain, shift):
    count, width = tokens.shape
    return call(
        attn_out_kernel,
        "attn_out",
        1,
        (*pieces, weights, tokens, bias[None], gain[None], shift[None]),
        [whole(piece.shape) for piece in pieces]
        + [whole(weights.shape), whole((count, width))]
        + [whole((1, width))] * 3,
        [((count, width), f32), ((count, width), bf16), ((count, width), bf16)],
        [whole((count, width))] * 3,
        table=table,
    )


def up_kernel(*refs):
    blocks, (weights, bias, activated, slope, normed, held) = refs[:4], refs[4:]
    pick_block(blocks, held)
    normed[...] = held[...]
    before = product(held[...], weights[...]) + bias[...]
    square = before * before
    inner = jnp.tanh(before * (0.7978845608028654 + 0.7978845608028654 * 0.044715 * square))
    half = 0.5 * (1.0 + inner)
    activated[...] = (before * half).astype(bf16)
    slope[...] = (
        half
        + 0.5
        * before
        * (1.0 - inner * inner)
        * (0.7978845608028654 + 3 * 0.7978845608028654 * 0.044715 * square)
    ).astype(bf16)


def feed_up(blocks, weights, bias):
    count, width = blocks[0].shape
    units = weights.shape[1]
    length = count * len(blocks)
    return call(
        up_kernel,
        "feed_up",
        len(blocks),
        (*blocks, weights, bias[None]),
        [whole((count, width))] * len(blocks) + [whole(weights.shape), whole((1, units))],
        [((length, units), bf16), ((length, units), bf16), ((length, width), bf16)],
        [rows_spec(count, units), rows_spec(count, units), rows_spec(count, width)],
        [pltpu.VMEM((count, width), bf16)],
    )


def back_kernel(*refs):
    blocks, (down, slope, low, sums, held) = refs[:4], refs[4:]
    pick_block(blocks, held)
    value = (back_product(held[...], down[...]) * slope[...].astype(f32)).astype(bf16)
    low[...] = value

    @pl.when(pl.program_id(0) == 0)
    def _():
        sums[...] = jnp.zeros_like(sums)

    sums[...] += jnp.sum(value.astype(f32), axis=0, keepdims=True)


def feed_back(blocks, down, slope, gates):
    count, width = blocks[0].shape
    units = slope.shape[1]
    length = count * len(blocks)
    return call(
        back_kernel,
        "feed_back",
        len(blocks),
        (*blocks, down, slope),
        [whole((count, width))] * len(blocks) + [whole(down.shape), rows_spec(count, units)],
        [((length, units), bf16), ((1, units), f32)],
        [rows_spec(count, units), whole((1, units))],
        [pltpu.VMEM((count, width), bf16)],
        gates=gates,
    )


def plain_back_kernel(left, right, keep, give):
    value = back_product(left[...], right[...]).astype(bf16)
    first = pl.program_id(0) < pl.num_programs(0) // 2

    @pl.when(first)
    def _():
        keep[...] = value

    @pl.when(jnp.logical_not(first))
    def _():
        give[...] = value


def plain_back(left, right, name):
    length, inner = left.shape
    width = right.shape[0]
    steps = length // QB
    half = steps // 2
    return call(
        plain_back_kernel,
        name,
        steps,
        (left, right),
        [rows_spec(QB, inner), whole(right.shape)],
        [((length // 2, width), bf16)] * 2,
        [
            pl.BlockSpec((QB, width), lambda i: (jnp.minimum(i, half - 1), 0)),
            pl.BlockSpec((QB, width), lambda i: (jnp.maximum(i - half, 0), 0)),
        ],
    )


VECTOR_ROWS = 8
FC_START = 2 * PAIR
VECTOR_WIDTH = 9 * PAIR


def attn_block_kernel(place, qkv, out_weights, *refs):
    vectors, (bias_fc, block, lines_out) = refs[:VECTOR_ROWS], refs[VECTOR_ROWS:]
    step, span = BASE * HD, SLOTS * HD
    width = out_weights.shape[1]
    rows = qkv.shape[0]
    parts = []
    for t in range(3):
        skip = t * width % PAIR
        start = pl.multiple_of(place[0] * step + (t * width - skip), PAIR)
        parts.append(qkv[:, pl.ds(start, span + skip)][:, skip:])
    for p in range(SLOTS // 2):
        for t in range(3):
            first = (3 * p + t) * PAIR
            block[:, first : first + PAIR] = parts[t][:, p * PAIR : (p + 1) * PAIR]
    rest = [part[:, (SLOTS - 1) * HD :] for part in parts] + [jnp.zeros((rows, HD), bf16)]
    first = 3 * (SLOTS // 2) * PAIR
    for p in range(2):
        block[:, first + p * PAIR : first + (p + 1) * PAIR] = jnp.concatenate(
            rest[2 * p : 2 * p + 2], axis=1
        )
    start = pl.multiple_of(place[0] * step, PAIR)
    block[:, first + 2 * PAIR :] = out_weights[:, pl.ds(start, span)]
    lines = jnp.stack([vector[...].astype(f32) for vector in vectors])
    lines_out[...] = jnp.zeros_like(lines_out)
    lines_out[:, : lines.shape[1]] = lines.astype(bf16)
    units = bias_fc.shape[0]
    line = jnp.broadcast_to(bias_fc[...].astype(f32)[None], (VECTOR_ROWS, units))
    lines_out[:, FC_START : FC_START + units] = line.astype(bf16)


def form_attn_block(place, qkv, out_weights, vectors, bias_fc):
    rows = qkv.shape[0]
    columns = 3 * (SLOTS // 2) * PAIR + 2 * PAIR + SLOTS * HD
    vectors = [*vectors, bias_fc]
    return call(
        attn_block_kernel,
        "form_attn_block",
        1,
        (qkv, out_weights, *vectors),
        [whole(value.shape) for value in (qkv, out_weights, *vectors)],
        [((rows, columns), bf16), ((VECTOR_ROWS, VECTOR_WIDTH), bf16)],
        [whole((rows, columns)), whole((VECTOR_ROWS, VECTOR_WIDTH))],
        table=place,
        limit=56 << 20,
    )


def whole_rows_kernel(table, *refs):
    pieces, out, held = refs[:4], refs[4], refs[5]
    pick_block(pieces, held)
    out[...] = held[...].astype(f32)


def whole_rows(table, pieces, gates):
    rows, width = pieces[0].shape
    return call(
        whole_rows_kernel,
        "whole_rows",
        len(pieces),
        pieces,
        [whole((rows, width))] * len(pieces),
        [((len(pieces), rows, width), f32)],
        [pl.BlockSpec((None, rows, width), lambda i, t: (t[i], 0, 0))],
        [pltpu.VMEM((rows, width), bf16)],
        table,
        gates,
    )[0].reshape(-1, width)


def put_windows(table, held, outs):
    for j in range(2 * len(outs)):
        start = pl.multiple_of(table[j] * BASE * HD, PAIR)
        outs[j // 2][j % 2] = held[:, pl.ds(start, SLOTS * HD)]


def norm_two_kernel(table, *refs):
    kept, far, middle, grad_out, gain, weights, grad_middle, low, keep, give, sums, held = refs
    grad = kept[...] + far[...].astype(f32)
    unit, scale = norm_stats(middle[...])
    back, grad_gain, grad_shift = norm_back(grad, unit, scale, gain[...])
    out = grad_out[...].astype(f32)
    value = out + back
    grad_middle[...] = value
    value_low = value.astype(bf16)
    low[...] = value_low
    held[...] = back_product(value_low, weights[...]).astype(bf16)
    put_windows(table, held, (keep, give))
    sums[0:1, :] = grad_gain[None]
    sums[1:2, :] = grad_shift[None]
    sums[2:3, :] = jnp.sum(value_low.astype(f32), axis=0, keepdims=True)
    sums[3:4, :] = jnp.sum(out, axis=0, keepdims=True)


def norm_two_back(table, kept, far, middle, grad_out, gain, weights, gates):
    count, width = middle.shape
    half = (2, count, SLOTS * HD)
    return call(
        norm_two_kernel,
        "norm_two_back",
        1,
        (kept, far, middle, grad_out, gain[None], weights),
        [whole((count, width))] * 4 + [whole((1, width)), whole(weights.shape)],
        [
            ((count, width), f32),
            ((count, width), bf16),
            (half, bf16),
            (half, bf16),
            ((4, width), f32),
        ],
        [
            whole((count, width)),
            whole((count, width)),
            whole(half),
            whole(half),
            whole((4, width)),
        ],
        [pltpu.VMEM((count, width), bf16)],
        table,
        gates=gates,
    )


def norm_one_kernel(kept, far, tokens, grad_middle, gain, grad_tokens, sums):
    grad = kept[...] + far[...].astype(f32)
    unit, scale = norm_stats(tokens[...].astype(f32))
    back, grad_gain, grad_shift = norm_back(grad, unit, scale, gain[...])
    grad_tokens[...] = grad_middle[...] + back
    sums[0:1, :] = grad_gain[None]
    sums[1:2, :] = grad_shift[None]


def norm_one_back(kept, far, tokens, grad_middle, gain, gates):
    shape = kept.shape
    return call(
        norm_one_kernel,
        "norm_one_back",
        1,
        (kept, far, tokens, grad_middle, gain[None]),
        [whole(shape)] * 4 + [whole((1, shape[1]))],
        [(shape, f32), ((2, shape[1]), f32)],
        [whole(shape), whole((2, shape[1]))],
        gates=gates,
    )


def out_grad_kernel(table, attended, low, keep, give, held):
    held[...] = outer_sum(attended[...], low[...]).astype(bf16)
    put_windows(table, held, (keep, give))


def out_weight_grad(table, attended, low, gates):
    count, width = attended.shape
    half = (2, width, SLOTS * HD)
    return call(
        out_grad_kernel,
        "out_weight_grad",
        1,
        (attended, low),
        [whole((count, width))] * 2,
        [(half, bf16)] * 2,
        [whole(half)] * 2,
        [pltpu.VMEM((width, width), bf16)],
        table,
        gates=gates,
    )


def whole_out_kernel(table, *refs):
    pieces, out = refs[:4], refs[4]
    step, span = BASE * HD, SLOTS * HD
    width = out.shape[1]
    for j, piece in enumerate(pieces):
        start = pl.multiple_of(table[j] * step, PAIR)
        out[:, pl.ds(start, step)] = piece[:, :step].astype(f32)

        @pl.when(table[j] == len(pieces) - 1)
        def _(piece=piece):
            out[:, width - (span - step) :] = piece[:, step:].astype(f32)


def whole_out(table, pieces, width):
    rows = pieces[0].shape[0]
    return call(
        whole_out_kernel,
        "whole_out",
        1,
        pieces,
        [whole(piece.shape) for piece in pieces],
        [((rows, width), f32)],
        [whole((rows, width))],
        table=table,
    )[0]


def whole_fc_kernel(table, *refs):
    pieces, out, held, sems = refs[:4], refs[4], refs[5], refs[6]
    copies = [
        pltpu.make_async_copy(piece, held.at[table[j]], sems.at[j])
        for j, piece in enumerate(pieces)
    ]
    for copy in copies:
        copy.start()
    for copy in copies:
        copy.wait()
    ranks = len(pieces)
    units = pieces[0].shape[0]
    for r in range(ranks):
        for i in range(pieces[0].shape[1] // units):
            first = (i * ranks + r) * units
            out[:, first : first + units] = held[r, :, i * units : (i + 1) * units].astype(f32)


def whole_fc(table, pieces, gates):
    rows, width = pieces[0].shape
    ranks = len(pieces)
    return call(
        whole_fc_kernel,
        "whole_fc",
        1,
        pieces,
        [pl.BlockSpec(memory_space=pl.ANY)] * ranks,
        [((rows, ranks * width), f32)],
        [whole((rows, ranks * width))],
        [pltpu.VMEM((ranks, rows, width), bf16), pltpu.SemaphoreType.DMA((ranks,))],
        table,
        gates,
    )[0]


def whole_qkv_kernel(table, *refs):
    pieces, out, held, sems = refs[:4], refs[4], refs[5], refs[6]
    copies = [
        pltpu.make_async_copy(piece, held.at[table[j]], sems.at[j])
        for j, piece in enumerate(pieces)
    ]
    for copy in copies:
        copy.start()
    for copy in copies:
        copy.wait()
    width = out.shape[1] // 3
    for rank in range(len(pieces)):
        for part in range(3):
            start = part * width + rank * BASE * HD
            for p in range(SLOTS // 2):
                tile = held[rank, :, (3 * p + part) * PAIR : (3 * p + part + 1) * PAIR]
                out[:, start + p * PAIR : start + (p + 1) * PAIR] = tile.astype(f32)
            if rank == len(pieces) - 1:
                first = 3 * (SLOTS // 2) * PAIR + part * HD
                tile = held[rank, :, first : first + HD]
                out[:, start + BASE * HD : start + SLOTS * HD] = tile.astype(f32)


def whole_qkv(table, pieces, width):
    rows = pieces[0].shape[0]
    return call(
        whole_qkv_kernel,
        "whole_qkv",
        1,
        pieces,
        [pl.BlockSpec(memory_space=pl.ANY)] * len(pieces),
        [((rows, 3 * width), f32)],
        [whole((rows, 3 * width))],
        [
            pltpu.VMEM((len(pieces),) + pieces[0].shape, bf16),
            pltpu.SemaphoreType.DMA((len(pieces),)),
        ],
        table,
    )[0]


def to_pairs(parts):
    pieces = []
    for p in range(SLOTS // 2):
        pieces += [part[:, p * PAIR : (p + 1) * PAIR] for part in parts]
    pieces += [part[:, (SLOTS - 1) * HD :] for part in parts]
    pieces.append(jnp.zeros((parts[0].shape[0], HD), parts[0].dtype))
    return jnp.concatenate(pieces, axis=1)


def from_pairs(matrix, part, last):
    pieces = [
        matrix[:, (3 * p + part) * PAIR : (3 * p + part + 1) * PAIR] for p in range(SLOTS // 2)
    ]
    if last:
        start = 3 * (SLOTS // 2) * PAIR + part * HD
        pieces.append(matrix[:, start : start + HD])
    return pieces


def per_device(
    tokens_in,
    group_order,
    out_grad,
    w_qkv,
    w_attn_out,
    b_query,
    b_value,
    b_attn_out,
    w_fc,
    w_proj,
    b_fc,
    b_proj,
    ln1_gain,
    ln1_bias,
    ln2_gain,
    ln2_bias,
):
    ctx = lax.axis_size("ctx")
    shards = lax.axis_size("fsdp")
    rank = lax.axis_index("ctx")
    tokens = tokens_in[0].astype(f32)
    count, width = tokens.shape
    span = SLOTS * HD
    step = BASE * HD
    mixed_width = (3 * span + PAIR - 1) // PAIR * PAIR
    attn_width = mixed_width + span
    shard_rows = w_qkv.shape[0]
    unit_rows = w_proj.shape[0] // ctx
    peers = [rank ^ bit for bit in PEERS]
    owners = ring_owners() if on_ring() else None

    always = group_order[0] >= 0
    peer_table = jnp.stack(peers).astype(jnp.int32)

    slots = jnp.argsort(group_order).astype(jnp.int32)
    place = jnp.take(jnp.asarray(np.argsort(np.array(PEERS)).astype(np.int32)), (slots // 2) ^ rank)
    slot_rows = (place * 2 + slots % 2) * GROUP
    table = jnp.concatenate([slot_rows, (rank == ctx - 1).astype(jnp.int32)[None]])

    attn_block, vectors = form_attn_block(
        rank[None].astype(jnp.int32),
        w_qkv,
        w_attn_out,
        (b_query, b_value, b_attn_out, b_proj, ln1_gain, ln1_bias, ln2_gain, ln2_bias),
        b_fc,
    )
    own_tokens = tokens_in[0]
    own_grad = out_grad[0]
    attn_gather = Gather(attn_block)
    attn_gather.hop()
    small, bit = vectors[None], 1
    while bit < shards:
        small = spread_small(small, bit)
        bit *= 2
    w_fc = after(w_fc, attn_block)
    fc_block = jnp.concatenate(
        [
            lax.dynamic_slice(
                w_fc, (0, (i * ctx + rank) * unit_rows), (shard_rows, unit_rows)
            )
            for i in range(shards)
        ],
        axis=1,
    )
    proj_block = lax.dynamic_slice(w_proj, (rank * unit_rows, 0), (unit_rows, width))
    feed_block = jnp.concatenate([fc_block, proj_block])
    token_blocks = gather_ctx(own_tokens)
    grad_blocks = gather_ctx(after(own_grad, token_blocks[1]))
    attn_gather.hop()
    attn_gather.hop()
    feed_gather = Gather(feed_block)

    def my_bias(vector):
        return lax.dynamic_slice(vector, (rank * step,), (span,))[None]

    def slot_zero():
        moved = attn_gather.step(), feed_gather.step()

        def beside():
            lines = small.astype(f32)
            values = [lines[:, t, :shard_rows].reshape(-1) for t in range(VECTOR_ROWS)]
            units = lax.dynamic_index_in_dim(
                lines[:, 0, FC_START : FC_START + ctx * unit_rows].reshape(
                    shards, ctx, unit_rows
                ),
                rank,
                1,
                False,
            ).reshape(-1)
            mixed_bias = to_pairs(
                [my_bias(values[0]), jnp.zeros((1, span), f32), my_bias(values[1])]
            )
            return mixed_bias, values[2:], units

        return moved, slot(always, beside)

    (attn_moved, feed_moved), (bias_mixed, values, bias_fc) = slot(always, slot_zero)
    attn_gather.take(attn_moved)
    feed_gather.take(feed_moved)
    bias_o, bias_p, gain_one, shift_one, gain_two, shift_two = values
    qkv_weights, out_columns = attn_gather.result(
        owners, ((0, mixed_width, 0, shard_rows), (mixed_width, span, 0, shard_rows))
    )
    qkv_weights = qkv_weights.reshape(width, mixed_width)

    normed_all, mixed = norm_mixed(
        [after(token_blocks[0], grad_blocks[3])] + token_blocks[1:],
        gain_one,
        shift_one,
        qkv_weights,
        bias_mixed,
    )
    attended_mine, mass = attend(table, mixed, feed_gather.arrived())
    feed_gather.hop()
    out_blocks = gather_ctx(out_columns.reshape(width, span))
    out_weights = join_windows(peer_table, out_blocks, width)
    pieces = exchange_far(
        *exchange_near(*halves(after(row_major(attended_mine[:, :span]), out_blocks[1])))
    )
    middle, normed_two, attended = attn_out(
        peer_table,
        pieces,
        out_weights,
        after(own_tokens, *feed_gather.arrived()),
        bias_o,
        gain_two,
        shift_two,
    )
    feed_gather.hop()

    normed_far = ctx_swap(normed_two, 2)
    normed_blocks = [
        normed_two,
        normed_far,
        ctx_swap(normed_two, 1),
    ]
    feed_gather.hop()
    normed_blocks.append(ctx_swap(after(normed_far, *feed_gather.arrived()), 1))
    grad_all = row_major(jnp.concatenate([after(grad_blocks[0], normed_two)] + grad_blocks[1:]))
    fc_weights, proj_weights = feed_gather.result(
        owners, ((0, width, 0, shard_rows), (0, width, shard_rows, unit_rows))
    )
    fc_weights = fc_weights.reshape(width, -1)
    proj_weights = proj_weights.reshape(-1, width)
    activated, slope, normed_two_all = feed_up(
        [after(normed_blocks[0], grad_all)] + normed_blocks[1:], fc_weights, bias_fc
    )

    grad_proj = row_major(outer_sum(activated, grad_all).astype(bf16))
    proj_blocks = grad_proj.reshape(shards, unit_rows, width)

    def slot_one():
        moved = ring_step(proj_blocks, owners, 4)
        return moved, feed_back(grad_blocks, proj_weights, slope, ())

    proj_moved, (before_low, grad_bias_fc) = slot(always, slot_one)

    def slot_two():
        moved = ring_step(proj_blocks, owners, 3, proj_moved)

        def beside():
            keep, give = plain_back(before_low, fc_weights, "feed_back_two")
            return keep, ctx_swap(give, 1)

        return moved, slot(always, beside)

    proj_moved, (keep_two, got_two) = slot(always, slot_two)

    def slot_three():
        moved = ring_step(proj_blocks, owners, 2, proj_moved)

        def beside():
            kept, onward = pair_add(keep_two, got_two)
            grad_fc = row_major(outer_sum(normed_two_all, before_low).astype(bf16))
            branch = row_major(product(activated, proj_weights).astype(bf16))
            return kept, ctx_swap(onward, 2), grad_fc, halves(branch)

        return moved, slot(always, beside)

    proj_moved, (kept_two, far_two, grad_fc, branch_halves) = slot(always, slot_three)
    fc_blocks = grad_fc.reshape(shards, shard_rows, shards * unit_rows)

    def slot_four():
        moved = packed_step(proj_blocks, fc_blocks, owners, proj_moved)

        def beside():
            grad_middle, low, keep, give, sums = norm_two_back(
                peer_table, kept_two, far_two, middle, own_grad, gain_two, out_weights, ()
            )
            near = exchange_near(keep.reshape(-1, span), give.reshape(-1, span))
            out_pair = out_weight_grad(peer_table, attended, low, ())
            return grad_middle, low, sums, exchange_far(*near), out_pair

        return moved, slot(always, beside)

    proj_moved, (grad_middle, middle_low, sums_two, heads, out_pair) = slot(
        always, slot_four
    )
    out_keep, out_give = [value.reshape(-1, span) for value in out_pair]

    def slot_five():
        moved = ring_step(fc_blocks, owners, 3, proj_moved)

        def beside():
            shard = ring_end(proj_blocks, owners, proj_moved)
            far, near, got = ctx_swap(shard, 2), ctx_swap(shard, 1), ctx_swap(out_give, 1)
            return [shard, far, near], got, attend_back(table, mixed, heads, mass, ())

        return moved, slot(always, beside)

    fc_moved, (proj_pieces, got_out, grad_mixed) = slot(always, slot_five)

    def slot_six():
        moved = ring_step(fc_blocks, owners, 2, fc_moved)

        def beside():
            last = ctx_swap(proj_pieces[1], 1)
            kept, first, second = pair_split(out_keep, got_out)
            far = ctx_swap(first, 2)
            grad_qkv = row_major(outer_sum(normed_all, grad_mixed).astype(bf16))
            return last, kept, second, far, grad_qkv

        return moved, slot(always, beside)

    fc_moved, (proj_last, kept_out, onward_out, far_first, grad_qkv) = slot(always, slot_six)
    proj_pieces = proj_pieces + [proj_last]
    qkv_blocks = grad_qkv.reshape(shards, shard_rows, mixed_width)

    def partial_table():
        bias_sums = jnp.sum(grad_mixed.astype(f32), axis=0, keepdims=True)

        def all_heads(part):
            mine = jnp.concatenate(from_pairs(bias_sums, part, True), axis=1)
            return lax.dynamic_update_slice(jnp.zeros((1, width), f32), mine, (0, rank * step))

        whole_bias_fc = lax.dynamic_update_slice(
            jnp.zeros((shards, ctx, unit_rows), f32),
            grad_bias_fc.reshape(shards, 1, unit_rows),
            (0, rank, 0),
        )
        return [
            value.reshape(shards, -1)
            for value in (all_heads(0), all_heads(2), *sums_two, whole_bias_fc)
        ]

    def whole_table(part, sums):
        one = [value.reshape(shards, -1) for value in sums]
        query, value, gain_two_sum, shift_two_sum, out, down, units = part
        return jnp.concatenate(
            [query, value, out, down, *one, gain_two_sum, shift_two_sum, units], axis=1
        )

    def slot_seven():
        moved = packed_step(fc_blocks, qkv_blocks, owners, fc_moved)

        def beside():
            far = ctx_swap(onward_out, 2)

            def inmost():
                keep, give = plain_back(grad_mixed, qkv_weights, "mixed_back")
                return pair_add(keep, ctx_swap(give, 1))

            return far, slot(always, inmost)

        return moved, slot(always, beside)

    fc_moved, (far_second, (kept_one, onward_one)) = slot(always, slot_seven)

    twin = [
        value.reshape(-1, shard_rows, span) for value in (kept_out, far_first, far_second)
    ]

    def slot_eight():
        qkv_next = twin_step(qkv_blocks, twin, owners, 3, fc_moved)

        def beside():
            far = ctx_swap(onward_one, 2)
            got = ctx_swap(branch_halves[1], 1)

            def inmost():
                shard = ring_end(fc_blocks, owners, fc_moved)
                return shard, partial_table(), whole_rows(peer_table, proj_pieces, ())

            return far, got, slot(always, inmost)

        return qkv_next, slot(always, beside)

    qkv_moved, (far_one, got_branch, (shard_fc, table_part, grad_w_proj)) = slot(
        always, slot_eight
    )

    def slot_nine():
        qkv_next = twin_step(qkv_blocks, twin, owners, 2, qkv_moved)

        def beside():
            far, near = ctx_swap(shard_fc, 2), ctx_swap(shard_fc, 1)

            def inmost():
                kept, onward = pair_add(branch_halves[0], got_branch)
                back, sums = norm_one_back(
                    kept_one, far_one, own_tokens, grad_middle, gain_one, ()
                )
                return kept, onward, back, whole_table(table_part, sums)

            return [shard_fc, far, near], slot(always, inmost)

        return qkv_next, slot(always, beside)

    qkv_moved, (fc_pieces, beside_nine) = slot(always, slot_nine)
    kept_branch, onward_branch, grad_tokens, small = beside_nine

    def slot_ten():
        held = halve_small(small, shards // 2)
        qkv_next = twin_step(qkv_blocks, twin, owners, 1, qkv_moved)
        far, last = ctx_swap(onward_branch, 2), ctx_swap(fc_pieces[1], 1)
        return qkv_next, held, far, last

    qkv_moved, held, far_branch, fc_last = slot(always, slot_ten)

    def slot_eleven():
        shard_qkv, out_next = twin_end(qkv_blocks, twin, owners, qkv_moved)
        far, near = ctx_swap(shard_qkv, 2), ctx_swap(shard_qkv, 1)
        next_held = halve_small(held, shards // 4)

        def beside():
            out = (middle + added(kept_branch, far_branch) + bias_p).astype(bf16)[None]
            return whole_fc(peer_table, fc_pieces + [fc_last], ()), out

        return [shard_qkv, far, near], out_next, next_held, slot(always, beside)

    qkv_pieces, out_moved, held, (grad_w_fc, tokens_out) = slot(always, slot_eleven)
    def slot_twelve():
        last = ctx_swap(qkv_pieces[1], 1)
        return last, slot(always, lambda: twin_last(twin, owners, out_moved))

    qkv_last, shard_out = slot(always, slot_twelve)

    def slot_thirteen():
        far, near = ctx_swap(shard_out, 2), ctx_swap(shard_out, 1)
        next_held = halve_small(held, shards // 8)

        def beside():
            return whole_qkv(peer_table, qkv_pieces + [qkv_last], width)

        return [shard_out, far, near], next_held, slot(always, beside)

    out_pieces, held, grad_w_qkv = slot(always, slot_thirteen)
    held = finish_small(held, shards // 16)
    out_last = ctx_swap(out_pieces[1], 1)
    summed = held[0] + ctx_swap(held[0], 1)
    summed = summed + ctx_swap(summed, 2)
    whole_attn_out = whole_out(peer_table, out_pieces + [out_last], width)
    shares = [summed[t * shard_rows : (t + 1) * shard_rows] for t in range(8)]
    share_fc = summed[8 * shard_rows :]
    grad_tokens = grad_tokens[None]

    return (
        tokens_out,
        grad_tokens,
        grad_w_qkv,
        whole_attn_out,
        shares[0],
        shares[1],
        shares[2],
        grad_w_fc,
        grad_w_proj,
        share_fc,
        shares[3],
        shares[4],
        shares[5],
        shares[6],
        shares[7],
    )


def solution(mesh):
    placed = (
        P("fsdp", "ctx", None),
        P(),
        P("fsdp", "ctx", None),
        P("fsdp", None),
        P("fsdp", None),
        P("fsdp"),
        P("fsdp"),
        P("fsdp"),
        P("fsdp", None),
        P("fsdp", None),
        P("fsdp"),
        P("fsdp"),
        P("fsdp"),
        P("fsdp"),
        P("fsdp"),
        P("fsdp"),
    )
    return jax.shard_map(
        per_device,
        mesh=mesh,
        in_specs=placed,
        out_specs=(
            P("fsdp", "ctx", None),
            P("fsdp", "ctx", None),
            P("fsdp", None),
            P("fsdp", None),
            P("fsdp"),
            P("fsdp"),
            P("fsdp"),
            P("fsdp", None),
            P("fsdp", None),
            P("fsdp"),
            P("fsdp"),
            P("fsdp"),
            P("fsdp"),
            P("fsdp"),
            P("fsdp"),
        ),
        check_vma=False,
    )
```

```python
import functools

import jax
import jax.numpy as jnp
import numpy as np
from jax import lax
from jax.experimental import pallas as pl
from jax.experimental.layout import Layout, with_layout_constraint
from jax.experimental.pallas import tpu as pltpu
from jax.sharding import PartitionSpec as P

H = 25
HD = 64
GROUP = 128
QB = 256
PAIR = 2 * HD
RANKS = 4
BASE = H // RANKS
SLOTS = H - (RANKS - 1) * BASE
norm_eps = 1e-05
masked_low = -1e30
LIGHT = pl.CostEstimate(flops=1 << 20, transcendentals=0, bytes_accessed=1 << 16)
VMEM_LIMIT = 30 << 20
f32 = jnp.float32
bf16 = jnp.bfloat16


def outer_sum(left_op, right_op):
    return lax.dot_general(
        left_op, right_op, (((0,), (0,)), ((), ())), preferred_element_type=f32
    )


def back_product(left_op, right_op):
    return lax.dot_general(
        left_op, right_op, (((1,), (1,)), ((), ())), preferred_element_type=f32
    )


def product(left_op, right_op):
    return jnp.dot(left_op, right_op, preferred_element_type=f32)


def added(*terms):
    total = terms[0].astype(f32)
    for term in terms[1:]:
        total = total + term.astype(f32)
    return total


def row_major(matrix):
    return with_layout_constraint(matrix, Layout(major_to_minor=tuple(range(matrix.ndim))))


def slot(always, step):
    empty = jax.eval_shape(step)
    return lax.cond(
        always,
        step,
        lambda: jax.tree.map(lambda leaf: jnp.zeros(leaf.shape, leaf.dtype), empty),
    )


def after(value, *others):
    return lax.optimization_barrier((value,) + others)[0]


PEERS = (0, 2, 1, 3)


def tiled(block):
    if block.ndim != 2 or block.shape[0] % 8:
        return block
    return block.reshape(-1, 8, block.shape[1])


def ctx_swap(block, bit):
    pairs = [(i, i ^ bit) for i in range(lax.axis_size("ctx"))]
    got = row_major(lax.ppermute(row_major(tiled(block)), "ctx", pairs))
    return got.reshape(block.shape)


def gather_ctx(block):
    far = ctx_swap(block, 2)
    near = ctx_swap(block, 1)
    return [block, far, near, ctx_swap(far, 1)]


def halves(matrix):
    half = matrix.shape[0] // 2
    return matrix[:half], matrix[half:]


def pair_add_kernel(keep, got, kept, onward):
    rows = kept.shape[0]
    kept[...] = added(keep[:rows], got[:rows]).astype(kept.dtype)
    onward[...] = added(keep[rows:], got[rows:]).astype(bf16)


def pair_add(keep, got, kind=f32):
    rows, columns = keep.shape
    half = (rows // 2, columns)
    return call(
        pair_add_kernel,
        "pair_add",
        1,
        (keep, got),
        [whole(keep.shape)] * 2,
        [(half, kind), (half, bf16)],
        [whole(half)] * 2,
    )


def pair_split_kernel(keep, got, kept, first, second):
    rows = kept.shape[0]
    half = rows // 2
    kept[...] = added(keep[:rows], got[:rows]).astype(kept.dtype)
    first[...] = added(keep[rows : rows + half], got[rows : rows + half]).astype(bf16)
    second[...] = added(keep[rows + half :], got[rows + half :]).astype(bf16)


def pair_split(keep, got):
    rows, columns = keep.shape
    half, quarter = (rows // 2, columns), (rows // 4, columns)
    return call(
        pair_split_kernel,
        "pair_split",
        1,
        (keep, got),
        [whole(keep.shape)] * 2,
        [(half, bf16), (quarter, bf16), (quarter, bf16)],
        [whole(half), whole(quarter), whole(quarter)],
    )


def exchange_near(keep, give):
    quarter = keep.shape[0] // 2
    got = ctx_swap(give, 1)
    return keep[:quarter], got[:quarter], jnp.concatenate([keep[quarter:], got[quarter:]])


def exchange_far(mine, near, onward):
    quarter = mine.shape[0]
    got = ctx_swap(onward, 2)
    return [mine, got[:quarter], near, got[quarter:]]


RING = (0, 2, 4, 6, 7, 5, 3, 1)
HALF = len(RING) // 2


def ring_hop(value, step):
    count = len(RING)
    pairs = [(RING[q], RING[(q + step) % count]) for q in range(count)]
    return row_major(lax.ppermute(row_major(value), "fsdp", pairs))


def ring_owners():
    place = jnp.asarray(np.argsort(np.array(RING)).astype(np.int32))
    mine = lax.dynamic_index_in_dim(place, lax.axis_index("fsdp"), 0, False)
    offsets = np.array([0, -1, 1, -2, 2, -3, 3, 4], np.int32)
    return jnp.take(jnp.asarray(np.array(RING, np.int32)), (mine + offsets) % len(RING))


def on_ring():
    return lax.axis_size("fsdp") == len(RING)


def upper_part(rows):
    return rows // 16 * 8


class Gather:
    def __init__(self, block):
        self.block = block
        self.cut = upper_part(block.shape[0])
        self.pieces = [block]
        self.forth = self.back = block

    def step(self):
        if not on_ring():
            return ()
        forth, back = self.forth, self.back
        if len(self.pieces) == 2 * HALF - 1:
            forth, back = forth[: self.cut], back[self.cut :]
        return ring_hop(forth, 1), ring_hop(back, -1)

    def take(self, moved):
        if moved:
            self.forth, self.back = moved
            self.pieces += list(moved)

    def hop(self):
        self.take(self.step())

    def arrived(self):
        return (self.forth, self.back) if on_ring() else ()

    def result(self, owners, columns, gates=()):
        if not on_ring():
            whole = lax.all_gather(self.block, "fsdp", axis=0, tiled=False)
            return [whole[:, top : top + n, c : c + w] for c, w, top, n in columns]
        return collect(self.pieces, owners, self.cut, columns, gates)


def spread_small(held, bit):
    got = lax.ppermute(held, "fsdp", [(i, i ^ bit) for i in range(lax.axis_size("fsdp"))])
    low = (lax.axis_index("fsdp") & bit) == 0
    return jnp.concatenate([jnp.where(low, held, got), jnp.where(low, got, held)])


def collect_kernel(cut, columns, owners, *refs):
    pieces = refs[: 2 * HALF + 1]
    outs = refs[2 * HALF + 1 : 2 * HALF + 1 + len(columns)]
    sems = refs[-1]
    copies = []
    for out, (start, width, top, rows) in zip(outs, columns):
        for j, piece in enumerate(pieces):
            first = cut if j == 2 * HALF else 0
            low = max(top, first)
            high = min(top + rows, first + piece.shape[0])
            if low < high:
                copies.append(
                    pltpu.make_async_copy(
                        piece.at[pl.ds(low - first, high - low), pl.ds(start, width)],
                        out.at[owners[min(j, 2 * HALF - 1)], pl.ds(low - top, high - low)],
                        sems.at[len(copies)],
                    )
                )
    for copy in copies:
        copy.start()
    for copy in copies:
        copy.wait()


def collect(pieces, owners, cut, columns, gates):
    shapes = [(len(RING), rows, width) for _, width, _, rows in columns]
    return call(
        functools.partial(collect_kernel, cut, columns),
        "collect",
        1,
        pieces,
        [pl.BlockSpec(memory_space=pl.ANY)] * len(pieces),
        [(shape, pieces[0].dtype) for shape in shapes],
        [whole(shape) for shape in shapes],
        [pltpu.SemaphoreType.DMA((len(pieces) * len(columns),))],
        owners,
        gates,
    )


PLACE = {0: 0, -1: 1, 1: 2, -2: 3, 2: 4, -3: 5, 3: 6, 4: 7}


def half_blocks(cut, rows, width, forth, back):
    return forth[forth.shape[0] - cut :, :width], back[back.shape[0] - (rows - cut) :, :width]


def ring_part_kernel(distance, cut, owners, *refs):
    if distance == HALF:
        far, ahead, behind = refs
        ahead[...] = far[:cut]
        behind[...] = far[cut:]
    elif distance == 0:
        own, forth, back, out = refs
        rows = own.shape[0]
        out[...] = added(own[...], forth[:rows], back[:rows]).astype(bf16)
    else:
        mine_ahead, mine_behind, forth, back, ahead, behind = refs
        if distance == HALF - 1:
            rows, width = mine_ahead.shape
            from_forth, from_back = half_blocks(cut, rows, width, forth, back)
            ahead[:cut] = added(mine_ahead[:cut], from_forth).astype(bf16)
            ahead[cut:] = mine_ahead[cut:]
            behind[:cut] = mine_behind[:cut]
            behind[cut:] = added(mine_behind[cut:], from_back).astype(bf16)
        else:
            ahead[...] = added(mine_ahead[...], forth[...]).astype(bf16)
            behind[...] = added(mine_behind[...], back[...]).astype(bf16)


def ring_part(blocks, owners, distance, cut, moved, gates=()):
    rows, columns = blocks.shape[1:]
    distances = (distance,) if distance in (0, HALF) else (distance, -distance)
    if distance == HALF:
        shapes = [(cut, columns), (rows - cut, columns)]
    else:
        shapes = [(rows, columns)] * len(distances)
    places = [PLACE[d] for d in distances]
    return call(
        functools.partial(ring_part_kernel, distance, cut),
        "ring_part",
        1,
        (*[blocks] * len(places), *moved),
        [
            pl.BlockSpec((None, rows, columns), lambda i, t, p=p: (t[p], 0, 0)) for p in places
        ]
        + [whole(value.shape) for value in moved],
        [(shape, bf16) for shape in shapes],
        [whole(shape) for shape in shapes],
        table=owners,
        gates=gates,
    )


def packed_kernel(cut, owners, mine_ahead, mine_behind, forth, back, far, ahead, behind):
    rows, width = mine_ahead.shape
    second = far.shape[1]
    ahead[:rows] = added(mine_ahead[...], forth[...]).astype(bf16)
    behind[:rows] = added(mine_behind[...], back[...]).astype(bf16)
    ahead[rows:, :second] = far[:cut]
    behind[rows:, :second] = far[cut:]
    if second < width:
        ahead[rows:, second:] = jnp.zeros((cut, width - second), bf16)
        behind[rows:, second:] = jnp.zeros((rows - cut, width - second), bf16)


def packed_step(blocks, others, owners, moved):
    if not on_ring():
        return ()
    rows, width = blocks.shape[1:]
    cut = upper_part(rows)
    shapes = [(rows + cut, width), (2 * rows - cut, width)]
    ahead, behind = call(
        functools.partial(packed_kernel, cut),
        "packed_part",
        1,
        (blocks, blocks, *moved, others),
        [
            pl.BlockSpec((None, rows, width), lambda i, t, p=PLACE[d]: (t[p], 0, 0))
            for d in (1, -1)
        ]
        + [whole(value.shape) for value in moved]
        + [pl.BlockSpec((None,) + others.shape[1:], lambda i, t: (t[PLACE[HALF]], 0, 0))],
        [(shape, bf16) for shape in shapes],
        [whole(shape) for shape in shapes],
        table=owners,
    )
    return ring_hop(ahead, 1), ring_hop(behind, -1)


def ring_step(blocks, owners, distance, moved=()):
    if not on_ring():
        return ()
    ahead, behind = ring_part(blocks, owners, distance, upper_part(blocks.shape[1]), moved)
    return ring_hop(ahead, 1), ring_hop(behind, -1)


def twin_block(owners, place, refs):
    kept, first, second = refs
    low = owners[place] < HALF
    return added(kept[...], jnp.where(low, first[...], second[...]))


def twin_kernel(distance, lag, cut, owners, *refs):
    width = refs[0].shape[-1]
    if distance == 0:
        own, forth, back, *twins = refs
        out, ahead, behind = twins[-3:]
        out[...] = added(own[...], forth[:, :width], back[:, :width]).astype(bf16)
        value_ahead = twin_block(owners, PLACE[lag], twins[0:3])
        value_behind = twin_block(owners, PLACE[-lag], twins[3:6])
        ahead[...] = added(value_ahead, forth[:, width:]).astype(bf16)
        behind[...] = added(value_behind, back[:, width:]).astype(bf16)
        return
    mine_ahead, mine_behind, forth, back, *twins = refs
    ahead, behind = twins[-2:]
    if distance == HALF - 1:
        from_forth, from_back = half_blocks(cut, mine_ahead.shape[0], width, forth, back)
        ahead[:cut, :width] = added(mine_ahead[:cut], from_forth).astype(bf16)
        ahead[cut:, :width] = mine_ahead[cut:]
        behind[:cut, :width] = mine_behind[:cut]
        behind[cut:, :width] = added(mine_behind[cut:], from_back).astype(bf16)
        value = twin_block(owners, PLACE[HALF], twins[0:3]).astype(bf16)
        ahead[:cut, width:] = value[:cut]
        ahead[cut:, width:] = jnp.zeros_like(value[cut:])
        behind[:cut, width:] = jnp.zeros_like(value[:cut])
        behind[cut:, width:] = value[cut:]
    else:
        ahead[:, :width] = added(mine_ahead[...], forth[:, :width]).astype(bf16)
        behind[:, :width] = added(mine_behind[...], back[:, :width]).astype(bf16)
        value_ahead = twin_block(owners, PLACE[lag], twins[0:3])
        value_behind = twin_block(owners, PLACE[-lag], twins[3:6])
        ahead[:, width:] = added(value_ahead, forth[:, width:]).astype(bf16)
        behind[:, width:] = added(value_behind, back[:, width:]).astype(bf16)


def twin_part(blocks, twin, owners, distance, moved):
    rows, width = blocks.shape[1:]
    span = twin[0].shape[2]
    lag = distance + 1
    mains = (distance, -distance) if distance else (0,)
    lags = (lag, -lag) if lag < HALF else (lag,)
    specs = [
        pl.BlockSpec((None, rows, width), lambda i, t, p=PLACE[d]: (t[p], 0, 0)) for d in mains
    ]
    specs += [whole(value.shape) for value in moved]
    for d in lags:
        p = PLACE[d]
        specs += [
            pl.BlockSpec((None, rows, span), lambda i, t, p=p: (t[p], 0, 0)),
            pl.BlockSpec(
                (None, rows, span), lambda i, t, p=p: (jnp.minimum(t[p], HALF - 1), 0, 0)
            ),
            pl.BlockSpec((None, rows, span), lambda i, t, p=p: (jnp.maximum(t[p] - HALF, 0), 0, 0)),
        ]
    if distance:
        shapes = [(rows, width + span)] * 2
    else:
        shapes = [(rows, width), (rows, span), (rows, span)]
    return call(
        functools.partial(twin_kernel, distance, lag, upper_part(rows)),
        "twin_part",
        1,
        (*[blocks] * len(mains), *moved, *twin * len(lags)),
        specs,
        [(shape, bf16) for shape in shapes],
        [whole(shape) for shape in shapes],
        table=owners,
    )


def twin_last_kernel(owners, forth, back, kept, first, second, out):
    value = twin_block(owners, PLACE[0], (kept, first, second))
    out[...] = added(value, forth[...], back[...]).astype(bf16)


def twin_last(twin, owners, moved):
    if not on_ring():
        blocks = added(twin[0], jnp.concatenate(twin[1:])).astype(bf16)
        return ring_end(blocks, owners, moved)
    rows, span = twin[0].shape[1:]
    block = (None, rows, span)
    return call(
        twin_last_kernel,
        "twin_last",
        1,
        (*moved, *twin),
        [whole((rows, span))] * 2
        + [
            pl.BlockSpec(block, lambda i, t: (t[0], 0, 0)),
            pl.BlockSpec(block, lambda i, t: (jnp.minimum(t[0], HALF - 1), 0, 0)),
            pl.BlockSpec(block, lambda i, t: (jnp.maximum(t[0] - HALF, 0), 0, 0)),
        ],
        [((rows, span), bf16)],
        [whole((rows, span))],
        table=owners,
    )[0]


def twin_step(blocks, twin, owners, distance, moved):
    if not on_ring():
        return ()
    ahead, behind = twin_part(blocks, twin, owners, distance, moved)
    return ring_hop(ahead, 1), ring_hop(behind, -1)


def twin_end(blocks, twin, owners, moved):
    if not on_ring():
        return ring_end(blocks, owners, moved), ()
    out, ahead, behind = twin_part(blocks, twin, owners, 0, moved)
    return out, (ring_hop(ahead, 1), ring_hop(behind, -1))


def ring_end(blocks, owners, moved):
    if not on_ring():
        return lax.psum_scatter(blocks, "fsdp", scatter_dimension=0, tiled=False)
    return ring_part(blocks, owners, 0, upper_part(blocks.shape[1]), moved)[0]


def halve_small(held, bit):
    me = lax.axis_index("fsdp")
    parts = held.reshape(2, bit, -1)
    high = (me & bit) != 0
    keep = jnp.where(high, parts[1], parts[0])
    give = jnp.where(high, parts[0], parts[1])
    pairs = [(i, i ^ bit) for i in range(lax.axis_size("fsdp"))]
    return keep + lax.ppermute(give, "fsdp", pairs)


def finish_small(held, bit):
    while bit:
        held = halve_small(held, bit)
        bit //= 2
    return held


def norm_stats(values):
    centre = values - jnp.mean(values, axis=-1, keepdims=True)
    scale = lax.rsqrt(jnp.mean(centre * centre, axis=-1, keepdims=True) + norm_eps)
    return centre * scale, scale


def norm_back(grad, unit, scale, gain):
    inner = grad * gain
    back = scale * (
        inner
        - jnp.mean(inner, axis=-1, keepdims=True)
        - unit * jnp.mean(inner * unit, axis=-1, keepdims=True)
    )
    return back, jnp.sum(grad * unit, axis=0), jnp.sum(grad, axis=0)


def across(left_op, right_op, left_dim, right_dim):
    return lax.dot_general(
        left_op, right_op, (((left_dim,), (right_dim,)), ((), ())), preferred_element_type=f32
    )


def diagonal_kept():
    shape = (QB, QB)
    return lax.broadcasted_iota(jnp.int32, shape, 0) <= lax.broadcasted_iota(jnp.int32, shape, 1)


def sorted_tile(table, ref, columns):
    groups = ref.shape[0] // GROUP
    return jnp.concatenate(
        [ref[pl.ds(pl.multiple_of(table[g], GROUP), GROUP), columns] for g in range(groups)],
        axis=0,
    )


def put_sorted(table, ref, columns, first, value):
    for j in range(value.shape[0] // GROUP):
        start = pl.multiple_of(table[first + j], GROUP)
        ref[pl.ds(start, GROUP), columns] = value[j * GROUP : (j + 1) * GROUP]


def split_heads(tiles, last):
    if last:
        return [(tiles[0][:, :HD], tiles[0][:, HD:], tiles[1][:, :HD])]
    return [tuple(t[:, w * HD : (w + 1) * HD] for t in tiles) for w in range(2)]


def pair_columns(pair, last):
    if last:
        start = SLOTS // 2 * 3 * PAIR
        return [slice(start, start + PAIR), slice(start + PAIR, start + 2 * PAIR)]
    return [pl.ds(pl.multiple_of(pair * 3 * PAIR + t * PAIR, PAIR), PAIR) for t in range(3)]


def attend_pair(pair, last, table, qkv_ref, out_ref, mass_ref):
    tiles = [sorted_tile(table, qkv_ref, c) for c in pair_columns(pair, last)]
    heads = split_heads(tiles, last)
    length = qkv_ref.shape[0]
    kept = diagonal_kept()
    ready = [(q * bf16(HD**-0.5), k, v.T) for q, k, v in heads]
    for i in range(length // QB):
        rows = slice(i * QB, (i + 1) * QB)
        outs = []
        for w, (queries, keys, values_t) in enumerate(ready):
            mine = queries[rows]
            diag = jnp.where(kept, across(keys[rows], mine, 1, 1), masked_low)
            peak = jnp.max(diag, axis=0, keepdims=True)
            if i:
                rest = across(keys[: i * QB], mine, 1, 1)
                peak = jnp.maximum(peak, jnp.max(rest, axis=0, keepdims=True))
            diag = jnp.exp(diag - peak)
            mass = jnp.sum(diag, axis=0, keepdims=True)
            out = across(values_t[:, rows], diag.astype(bf16), 1, 0)
            if i:
                rest = jnp.exp(rest - peak)
                mass = mass + jnp.sum(rest, axis=0, keepdims=True)
                out = out + across(values_t[:, : i * QB], rest.astype(bf16), 1, 0)
            outs.append(out / mass)
            mass_ref[0, w : w + 1, rows] = peak + jnp.log(mass)
        if last:
            outs.append(jnp.zeros_like(outs[0]))
        tile = jnp.concatenate(outs, axis=0).T.astype(bf16)
        put_sorted(table, out_ref, slice(None), 2 * i, tile)


def attend_kernel(table, qkv_ref, out_ref, mass_ref):
    pair = pl.program_id(0)
    final = pl.num_programs(0) - 1

    @pl.when(pair < final)
    def _():
        attend_pair(pair, False, table, qkv_ref, out_ref, mass_ref)

    @pl.when(pair == final)
    def _():
        mass_ref[...] = jnp.zeros_like(mass_ref)

        @pl.when(table[table.shape[0] - 1] == 0)
        def _():
            out_ref[...] = jnp.zeros_like(out_ref)

        @pl.when(table[table.shape[0] - 1] != 0)
        def _():
            attend_pair(pair, True, table, qkv_ref, out_ref, mass_ref)


def attend_back_pair(pair, last, table, qkv_ref, grad_ref, mass_ref, out_ref, acc):
    places = pair_columns(pair, last)
    heads = split_heads([sorted_tile(table, qkv_ref, c) for c in places], last)
    grads = sorted_tile(table, grad_ref, slice(None))
    length = qkv_ref.shape[0]
    kept = diagonal_kept()
    ready = [
        (q * bf16(HD**-0.5), k, k.T, v, grads[:, w * HD : (w + 1) * HD])
        for w, (q, k, v) in enumerate(heads)
    ]
    for i in range(length // QB):
        rows = slice(i * QB, (i + 1) * QB)
        query_tiles = []
        for w, (queries, keys, keys_t, values, grads_w) in enumerate(ready):
            mine = queries[rows]
            grad = grads_w[rows]
            mass = mass_ref[0, w : w + 1, rows]
            spans = [(rows, True)] + ([(slice(0, i * QB), False)] if i else [])
            probs, both, delta = [], [], None
            for span, diagonal in spans:
                scores = across(keys[span], mine, 1, 1)
                if diagonal:
                    scores = jnp.where(kept, scores, masked_low)
                prob = jnp.exp(scores - mass)
                prod = prob * across(values[span], grad, 1, 1)
                part = jnp.sum(prod, axis=0, keepdims=True)
                delta = part if delta is None else delta + part
                probs.append(prob)
                both.append(prod)
            query_t = None
            for (span, diagonal), prob, prod in zip(spans, probs, both):
                grad_scores = (prod - prob * delta).astype(bf16)
                part = across(keys_t[:, span], grad_scores, 1, 0)
                query_t = part if query_t is None else query_t + part
                key_part = across(grad_scores, mine, 1, 0)
                value_part = across(prob.astype(bf16), grad, 1, 0)
                if diagonal:
                    acc[2 * w, span, :] = key_part
                    acc[2 * w + 1, span, :] = value_part
                else:
                    acc[2 * w, span, :] += key_part
                    acc[2 * w + 1, span, :] += value_part
            query_tiles.append(query_t * HD**-0.5)
        if last:
            query_tiles.append(jnp.zeros_like(query_tiles[0]))
        tile = jnp.concatenate(query_tiles, axis=0).T
        if last:
            tile = jnp.concatenate([tile[:, :HD], jnp.zeros_like(tile[:, HD:])], axis=1)
        put_sorted(table, out_ref, places[0], 2 * i, tile.astype(bf16))
    if last:
        old = sorted_tile(table, out_ref, places[0])
        tile = jnp.concatenate([old[:, :HD], acc[0].astype(bf16)], axis=1)
        put_sorted(table, out_ref, places[0], 0, tile)
        tile = jnp.concatenate([acc[1].astype(bf16), jnp.zeros((length, HD), bf16)], axis=1)
        put_sorted(table, out_ref, places[1], 0, tile)
    else:
        for t in range(2):
            tile = jnp.concatenate([acc[t].astype(bf16), acc[2 + t].astype(bf16)], axis=1)
            put_sorted(table, out_ref, places[1 + t], 0, tile)


def attend_back_kernel(table, *refs):
    grad_refs, (qkv_ref, mass_ref, out_ref, acc, held) = refs[:4], refs[4:]
    pair = pl.program_id(0)
    final = pl.num_programs(0) - 1

    @pl.when(pair == 0)
    def _():
        span = SLOTS * HD
        rows = grad_refs[0].shape[0]
        for j, ref in enumerate(grad_refs):
            for p in range(span // PAIR):
                held[p, j * rows : (j + 1) * rows, :] = ref[:, p * PAIR : (p + 1) * PAIR]
            tail = jnp.concatenate([ref[:, span - HD :], jnp.zeros((rows, HD), bf16)], axis=1)
            held[span // PAIR, j * rows : (j + 1) * rows, :] = tail

    refs = (table, qkv_ref, held.at[pair], mass_ref, out_ref, acc)

    @pl.when(pair < final)
    def _():
        attend_back_pair(pair, False, *refs)

    @pl.when(pair == final)
    def _():
        @pl.when(table[table.shape[0] - 1] == 0)
        def _():
            for columns in pair_columns(pair, True):
                out_ref[:, columns] = jnp.zeros((out_ref.shape[0], PAIR), bf16)

        @pl.when(table[table.shape[0] - 1] != 0)
        def _():
            attend_back_pair(pair, True, *refs)


def attend(table, qkv, gates):
    length, columns = qkv.shape
    pairs = (SLOTS + 1) // 2
    return call(
        attend_kernel,
        "attend",
        pairs,
        (qkv,),
        [whole((length, columns))],
        [((length, pairs * PAIR), bf16), ((pairs, 8, length), f32)],
        [
            pl.BlockSpec((length, PAIR), lambda p, t: (0, p)),
            pl.BlockSpec((1, 8, length), lambda p, t: (p, 0, 0)),
        ],
        table=table,
        gates=gates,
    )


def attend_back(table, qkv, grads, mass, gates):
    length, columns = qkv.shape
    pairs = (SLOTS + 1) // 2
    return call(
        attend_back_kernel,
        "attend_back",
        pairs,
        (*grads, qkv, mass),
        [whole(grad.shape) for grad in grads]
        + [whole((length, columns)), pl.BlockSpec((1, 8, length), lambda p, t: (p, 0, 0))],
        [((length, columns), bf16)],
        [whole((length, columns))],
        [pltpu.VMEM((4, length, HD), f32), pltpu.VMEM((pairs, length, PAIR), bf16)],
        table,
        gates,
    )[0]


def whole(shape):
    return pl.BlockSpec(shape, lambda *_: (0,) * len(shape))


def rows_spec(rows, columns):
    return pl.BlockSpec((rows, columns), lambda i, *_: (i, 0))


def call(
    kernel,
    name,
    grid,
    operands,
    specs,
    outs,
    out_specs,
    scratch=(),
    table=None,
    gates=(),
    limit=VMEM_LIMIT,
):
    tables = () if table is None else (table,)
    first = len(tables) + len(operands)
    count = len(gates)

    def body(*refs):
        kernel(*refs[:first], *refs[first + count :])

    return pl.pallas_call(
        body,
        grid_spec=pltpu.PrefetchScalarGridSpec(
            num_scalar_prefetch=len(tables),
            grid=(grid,),
            in_specs=list(specs) + [pl.BlockSpec(memory_space=pl.ANY)] * count,
            out_specs=out_specs,
            scratch_shapes=list(scratch),
        ),
        out_shape=[jax.ShapeDtypeStruct(shape, kind) for shape, kind in outs],
        compiler_params=pltpu.CompilerParams(vmem_limit_bytes=limit),
        cost_estimate=LIGHT,
        name=name,
    )(*tables, *operands, *gates)


def pick_block(refs, held):
    for j, ref in enumerate(refs):

        @pl.when(pl.program_id(0) == j)
        def _(ref=ref):
            held[...] = ref[...]


def norm_mixed_kernel(*refs):
    blocks, (gain, shift, weights, bias, normed, mixed, held) = refs[:4], refs[4:]
    pick_block(blocks, held)
    unit, _ = norm_stats(held[...].astype(f32))
    low = (unit * gain[...] + shift[...]).astype(bf16)
    normed[...] = low
    mixed[...] = (product(low, weights[...]) + bias[...]).astype(bf16)


def norm_mixed(blocks, gain, shift, weights, bias):
    count, width = blocks[0].shape
    mixed_width = weights.shape[1]
    length = count * len(blocks)
    return call(
        norm_mixed_kernel,
        "norm_mixed",
        len(blocks),
        (*blocks, gain[None], shift[None], weights, bias),
        [whole((count, width))] * len(blocks)
        + [whole((1, width))] * 2
        + [whole(weights.shape), whole((1, mixed_width))],
        [((length, width), bf16), ((length, mixed_width), bf16)],
        [rows_spec(count, width), rows_spec(count, mixed_width)],
        [pltpu.VMEM((count, width), bf16)],
    )


def join_kernel(table, *refs):
    pieces, out, sems, last_sem = refs[:4], refs[4], refs[5], refs[6]
    step, span = BASE * HD, SLOTS * HD
    width = out.shape[1]
    rest = span - step
    last = len(pieces) - 1

    def copies(j):
        start = pl.multiple_of(table[j] * step, PAIR)
        main = pltpu.make_async_copy(
            pieces[j].at[:, pl.ds(0, step)], out.at[:, pl.ds(start, step)], sems.at[j]
        )
        tail = pltpu.make_async_copy(
            pieces[j].at[:, pl.ds(step, rest)], out.at[:, pl.ds(width - rest, rest)], last_sem.at[0]
        )
        return main, tail

    for j in range(len(pieces)):
        main, tail = copies(j)
        main.start()

        @pl.when(table[j] == last)
        def _(tail=tail):
            tail.start()

    for j in range(len(pieces)):
        main, tail = copies(j)
        main.wait()

        @pl.when(table[j] == last)
        def _(tail=tail):
            tail.wait()


def join_windows(table, pieces, width):
    rows = pieces[0].shape[0]
    return call(
        join_kernel,
        "join_windows",
        1,
        pieces,
        [pl.BlockSpec(memory_space=pl.ANY)] * len(pieces),
        [((rows, width), pieces[0].dtype)],
        [whole((rows, width))],
        [pltpu.SemaphoreType.DMA((len(pieces),)), pltpu.SemaphoreType.DMA((1,))],
        table,
    )[0]


def attn_out_kernel(table, *refs):
    pieces, rest = refs[:4], refs[4:]
    weights, tokens, bias, gain, shift, middle, normed, attended = rest
    step, span = BASE * HD, SLOTS * HD
    width = attended.shape[1]
    for j, piece in enumerate(pieces):
        start = pl.multiple_of(table[j] * step, PAIR)
        attended[:, pl.ds(start, step)] = piece[:, :step]

        @pl.when(table[j] == len(pieces) - 1)
        def _(piece=piece):
            attended[:, width - (span - step) :] = piece[:, step:]

    value = tokens[...].astype(f32) + product(attended[...], weights[...]) + bias[...]
    middle[...] = value
    unit, _ = norm_stats(value)
    normed[...] = (unit * gain[...] + shift[...]).astype(bf16)


def attn_out(table, pieces, weights, tokens, bias, gain, shift):
    count, width = tokens.shape
    return call(
        attn_out_kernel,
        "attn_out",
        1,
        (*pieces, weights, tokens, bias[None], gain[None], shift[None]),
        [whole(piece.shape) for piece in pieces]
        + [whole(weights.shape), whole((count, width))]
        + [whole((1, width))] * 3,
        [((count, width), f32), ((count, width), bf16), ((count, width), bf16)],
        [whole((count, width))] * 3,
        table=table,
    )


def up_kernel(*refs):
    blocks, (weights, bias, activated, slope, normed, held) = refs[:4], refs[4:]
    pick_block(blocks, held)
    normed[...] = held[...]
    before = product(held[...], weights[...]) + bias[...]
    square = before * before
    inner = jnp.tanh(before * (0.7978845608028654 + 0.7978845608028654 * 0.044715 * square))
    half = 0.5 * (1.0 + inner)
    activated[...] = (before * half).astype(bf16)
    slope[...] = (
        half
        + 0.5
        * before
        * (1.0 - inner * inner)
        * (0.7978845608028654 + 3 * 0.7978845608028654 * 0.044715 * square)
    ).astype(bf16)


def feed_up(blocks, weights, bias):
    count, width = blocks[0].shape
    units = weights.shape[1]
    length = count * len(blocks)
    return call(
        up_kernel,
        "feed_up",
        len(blocks),
        (*blocks, weights, bias[None]),
        [whole((count, width))] * len(blocks) + [whole(weights.shape), whole((1, units))],
        [((length, units), bf16), ((length, units), bf16), ((length, width), bf16)],
        [rows_spec(count, units), rows_spec(count, units), rows_spec(count, width)],
        [pltpu.VMEM((count, width), bf16)],
    )


def back_kernel(*refs):
    blocks, (down, slope, low, sums, held) = refs[:4], refs[4:]
    pick_block(blocks, held)
    value = (back_product(held[...], down[...]) * slope[...].astype(f32)).astype(bf16)
    low[...] = value

    @pl.when(pl.program_id(0) == 0)
    def _():
        sums[...] = jnp.zeros_like(sums)

    sums[...] += jnp.sum(value.astype(f32), axis=0, keepdims=True)


def feed_back(blocks, down, slope, gates):
    count, width = blocks[0].shape
    units = slope.shape[1]
    length = count * len(blocks)
    return call(
        back_kernel,
        "feed_back",
        len(blocks),
        (*blocks, down, slope),
        [whole((count, width))] * len(blocks) + [whole(down.shape), rows_spec(count, units)],
        [((length, units), bf16), ((1, units), f32)],
        [rows_spec(count, units), whole((1, units))],
        [pltpu.VMEM((count, width), bf16)],
        gates=gates,
    )


def plain_back_kernel(left, right, keep, give):
    value = back_product(left[...], right[...]).astype(bf16)
    first = pl.program_id(0) < pl.num_programs(0) // 2

    @pl.when(first)
    def _():
        keep[...] = value

    @pl.when(jnp.logical_not(first))
    def _():
        give[...] = value


def plain_back(left, right, name):
    length, inner = left.shape
    width = right.shape[0]
    steps = length // QB
    half = steps // 2
    return call(
        plain_back_kernel,
        name,
        steps,
        (left, right),
        [rows_spec(QB, inner), whole(right.shape)],
        [((length // 2, width), bf16)] * 2,
        [
            pl.BlockSpec((QB, width), lambda i: (jnp.minimum(i, half - 1), 0)),
            pl.BlockSpec((QB, width), lambda i: (jnp.maximum(i - half, 0), 0)),
        ],
    )


VECTOR_ROWS = 8
FC_START = 2 * PAIR
VECTOR_WIDTH = 9 * PAIR


def attn_block_kernel(place, qkv, out_weights, *refs):
    vectors, (bias_fc, block, lines_out) = refs[:VECTOR_ROWS], refs[VECTOR_ROWS:]
    step, span = BASE * HD, SLOTS * HD
    width = out_weights.shape[1]
    rows = qkv.shape[0]
    parts = []
    for t in range(3):
        skip = t * width % PAIR
        start = pl.multiple_of(place[0] * step + (t * width - skip), PAIR)
        parts.append(qkv[:, pl.ds(start, span + skip)][:, skip:])
    for p in range(SLOTS // 2):
        for t in range(3):
            first = (3 * p + t) * PAIR
            block[:, first : first + PAIR] = parts[t][:, p * PAIR : (p + 1) * PAIR]
    rest = [part[:, (SLOTS - 1) * HD :] for part in parts] + [jnp.zeros((rows, HD), bf16)]
    first = 3 * (SLOTS // 2) * PAIR
    for p in range(2):
        block[:, first + p * PAIR : first + (p + 1) * PAIR] = jnp.concatenate(
            rest[2 * p : 2 * p + 2], axis=1
        )
    start = pl.multiple_of(place[0] * step, PAIR)
    block[:, first + 2 * PAIR :] = out_weights[:, pl.ds(start, span)]
    lines = jnp.stack([vector[...].astype(f32) for vector in vectors])
    lines_out[...] = jnp.zeros_like(lines_out)
    lines_out[:, : lines.shape[1]] = lines.astype(bf16)
    units = bias_fc.shape[0]
    line = jnp.broadcast_to(bias_fc[...].astype(f32)[None], (VECTOR_ROWS, units))
    lines_out[:, FC_START : FC_START + units] = line.astype(bf16)


def form_attn_block(place, qkv, out_weights, vectors, bias_fc):
    rows = qkv.shape[0]
    columns = 3 * (SLOTS // 2) * PAIR + 2 * PAIR + SLOTS * HD
    vectors = [*vectors, bias_fc]
    return call(
        attn_block_kernel,
        "form_attn_block",
        1,
        (qkv, out_weights, *vectors),
        [whole(value.shape) for value in (qkv, out_weights, *vectors)],
        [((rows, columns), bf16), ((VECTOR_ROWS, VECTOR_WIDTH), bf16)],
        [whole((rows, columns)), whole((VECTOR_ROWS, VECTOR_WIDTH))],
        table=place,
        limit=56 << 20,
    )


def whole_rows_kernel(table, *refs):
    pieces, out, held = refs[:4], refs[4], refs[5]
    pick_block(pieces, held)
    out[...] = held[...].astype(f32)


def whole_rows(table, pieces, gates):
    rows, width = pieces[0].shape
    return call(
        whole_rows_kernel,
        "whole_rows",
        len(pieces),
        pieces,
        [whole((rows, width))] * len(pieces),
        [((len(pieces), rows, width), f32)],
        [pl.BlockSpec((None, rows, width), lambda i, t: (t[i], 0, 0))],
        [pltpu.VMEM((rows, width), bf16)],
        table,
        gates,
    )[0].reshape(-1, width)


def put_windows(table, held, outs):
    for j in range(2 * len(outs)):
        start = pl.multiple_of(table[j] * BASE * HD, PAIR)
        outs[j // 2][j % 2] = held[:, pl.ds(start, SLOTS * HD)]


def norm_two_kernel(table, *refs):
    kept, far, middle, grad_out, gain, weights, grad_middle, low, keep, give, sums, held = refs
    grad = kept[...] + far[...].astype(f32)
    unit, scale = norm_stats(middle[...])
    back, grad_gain, grad_shift = norm_back(grad, unit, scale, gain[...])
    out = grad_out[...].astype(f32)
    value = out + back
    grad_middle[...] = value
    value_low = value.astype(bf16)
    low[...] = value_low
    held[...] = back_product(value_low, weights[...]).astype(bf16)
    put_windows(table, held, (keep, give))
    sums[0:1, :] = grad_gain[None]
    sums[1:2, :] = grad_shift[None]
    sums[2:3, :] = jnp.sum(value_low.astype(f32), axis=0, keepdims=True)
    sums[3:4, :] = jnp.sum(out, axis=0, keepdims=True)


def norm_two_back(table, kept, far, middle, grad_out, gain, weights, gates):
    count, width = middle.shape
    half = (2, count, SLOTS * HD)
    return call(
        norm_two_kernel,
        "norm_two_back",
        1,
        (kept, far, middle, grad_out, gain[None], weights),
        [whole((count, width))] * 4 + [whole((1, width)), whole(weights.shape)],
        [
            ((count, width), f32),
            ((count, width), bf16),
            (half, bf16),
            (half, bf16),
            ((4, width), f32),
        ],
        [
            whole((count, width)),
            whole((count, width)),
            whole(half),
            whole(half),
            whole((4, width)),
        ],
        [pltpu.VMEM((count, width), bf16)],
        table,
        gates=gates,
    )


def norm_one_kernel(kept, far, tokens, grad_middle, gain, grad_tokens, sums):
    grad = kept[...] + far[...].astype(f32)
    unit, scale = norm_stats(tokens[...].astype(f32))
    back, grad_gain, grad_shift = norm_back(grad, unit, scale, gain[...])
    grad_tokens[...] = grad_middle[...] + back
    sums[0:1, :] = grad_gain[None]
    sums[1:2, :] = grad_shift[None]


def norm_one_back(kept, far, tokens, grad_middle, gain, gates):
    shape = kept.shape
    return call(
        norm_one_kernel,
        "norm_one_back",
        1,
        (kept, far, tokens, grad_middle, gain[None]),
        [whole(shape)] * 4 + [whole((1, shape[1]))],
        [(shape, f32), ((2, shape[1]), f32)],
        [whole(shape), whole((2, shape[1]))],
        gates=gates,
    )


def out_grad_kernel(table, attended, low, keep, give, held):
    held[...] = outer_sum(attended[...], low[...]).astype(bf16)
    put_windows(table, held, (keep, give))


def out_weight_grad(table, attended, low, gates):
    count, width = attended.shape
    half = (2, width, SLOTS * HD)
    return call(
        out_grad_kernel,
        "out_weight_grad",
        1,
        (attended, low),
        [whole((count, width))] * 2,
        [(half, bf16)] * 2,
        [whole(half)] * 2,
        [pltpu.VMEM((width, width), bf16)],
        table,
        gates=gates,
    )


def whole_out_kernel(table, *refs):
    pieces, out = refs[:4], refs[4]
    step, span = BASE * HD, SLOTS * HD
    width = out.shape[1]
    for j, piece in enumerate(pieces):
        start = pl.multiple_of(table[j] * step, PAIR)
        out[:, pl.ds(start, step)] = piece[:, :step].astype(f32)

        @pl.when(table[j] == len(pieces) - 1)
        def _(piece=piece):
            out[:, width - (span - step) :] = piece[:, step:].astype(f32)


def whole_out(table, pieces, width):
    rows = pieces[0].shape[0]
    return call(
        whole_out_kernel,
        "whole_out",
        1,
        pieces,
        [whole(piece.shape) for piece in pieces],
        [((rows, width), f32)],
        [whole((rows, width))],
        table=table,
    )[0]


def whole_fc_kernel(table, *refs):
    pieces, out, held, sems = refs[:4], refs[4], refs[5], refs[6]
    copies = [
        pltpu.make_async_copy(piece, held.at[table[j]], sems.at[j])
        for j, piece in enumerate(pieces)
    ]
    for copy in copies:
        copy.start()
    for copy in copies:
        copy.wait()
    ranks = len(pieces)
    units = pieces[0].shape[0]
    for r in range(ranks):
        for i in range(pieces[0].shape[1] // units):
            first = (i * ranks + r) * units
            out[:, first : first + units] = held[r, :, i * units : (i + 1) * units].astype(f32)


def whole_fc(table, pieces, gates):
    rows, width = pieces[0].shape
    ranks = len(pieces)
    return call(
        whole_fc_kernel,
        "whole_fc",
        1,
        pieces,
        [pl.BlockSpec(memory_space=pl.ANY)] * ranks,
        [((rows, ranks * width), f32)],
        [whole((rows, ranks * width))],
        [pltpu.VMEM((ranks, rows, width), bf16), pltpu.SemaphoreType.DMA((ranks,))],
        table,
        gates,
    )[0]


def whole_qkv_kernel(table, *refs):
    pieces, out, held, sems = refs[:4], refs[4], refs[5], refs[6]
    copies = [
        pltpu.make_async_copy(piece, held.at[table[j]], sems.at[j])
        for j, piece in enumerate(pieces)
    ]
    for copy in copies:
        copy.start()
    for copy in copies:
        copy.wait()
    width = out.shape[1] // 3
    for rank in range(len(pieces)):
        for part in range(3):
            start = part * width + rank * BASE * HD
            for p in range(SLOTS // 2):
                tile = held[rank, :, (3 * p + part) * PAIR : (3 * p + part + 1) * PAIR]
                out[:, start + p * PAIR : start + (p + 1) * PAIR] = tile.astype(f32)
            if rank == len(pieces) - 1:
                first = 3 * (SLOTS // 2) * PAIR + part * HD
                tile = held[rank, :, first : first + HD]
                out[:, start + BASE * HD : start + SLOTS * HD] = tile.astype(f32)


def whole_qkv(table, pieces, width):
    rows = pieces[0].shape[0]
    return call(
        whole_qkv_kernel,
        "whole_qkv",
        1,
        pieces,
        [pl.BlockSpec(memory_space=pl.ANY)] * len(pieces),
        [((rows, 3 * width), f32)],
        [whole((rows, 3 * width))],
        [
            pltpu.VMEM((len(pieces),) + pieces[0].shape, bf16),
            pltpu.SemaphoreType.DMA((len(pieces),)),
        ],
        table,
    )[0]


def to_pairs(parts):
    pieces = []
    for p in range(SLOTS // 2):
        pieces += [part[:, p * PAIR : (p + 1) * PAIR] for part in parts]
    pieces += [part[:, (SLOTS - 1) * HD :] for part in parts]
    pieces.append(jnp.zeros((parts[0].shape[0], HD), parts[0].dtype))
    return jnp.concatenate(pieces, axis=1)


def from_pairs(matrix, part, last):
    pieces = [
        matrix[:, (3 * p + part) * PAIR : (3 * p + part + 1) * PAIR] for p in range(SLOTS // 2)
    ]
    if last:
        start = 3 * (SLOTS // 2) * PAIR + part * HD
        pieces.append(matrix[:, start : start + HD])
    return pieces


def per_device(
    tokens_in,
    group_order,
    out_grad,
    w_qkv,
    w_attn_out,
    b_query,
    b_value,
    b_attn_out,
    w_fc,
    w_proj,
    b_fc,
    b_proj,
    ln1_gain,
    ln1_bias,
    ln2_gain,
    ln2_bias,
):
    ctx = lax.axis_size("ctx")
    shards = lax.axis_size("fsdp")
    rank = lax.axis_index("ctx")
    tokens = tokens_in[0].astype(f32)
    count, width = tokens.shape
    span = SLOTS * HD
    step = BASE * HD
    mixed_width = (3 * span + PAIR - 1) // PAIR * PAIR
    attn_width = mixed_width + span
    shard_rows = w_qkv.shape[0]
    unit_rows = w_proj.shape[0] // ctx
    peers = [rank ^ bit for bit in PEERS]
    owners = ring_owners() if on_ring() else None

    always = group_order[0] >= 0
    peer_table = jnp.stack(peers).astype(jnp.int32)

    slots = jnp.argsort(group_order).astype(jnp.int32)
    place = jnp.take(jnp.asarray(np.argsort(np.array(PEERS)).astype(np.int32)), (slots // 2) ^ rank)
    slot_rows = (place * 2 + slots % 2) * GROUP
    table = jnp.concatenate([slot_rows, (rank == ctx - 1).astype(jnp.int32)[None]])

    attn_block, vectors = form_attn_block(
        rank[None].astype(jnp.int32),
        w_qkv,
        w_attn_out,
        (b_query, b_value, b_attn_out, b_proj, ln1_gain, ln1_bias, ln2_gain, ln2_bias),
        b_fc,
    )
    own_tokens = tokens_in[0]
    own_grad = out_grad[0]
    attn_gather = Gather(attn_block)
    attn_gather.hop()
    small, bit = vectors[None], 1
    while bit < shards:
        small = spread_small(small, bit)
        bit *= 2
    w_fc = after(w_fc, attn_block)
    fc_block = jnp.concatenate(
        [
            lax.dynamic_slice(
                w_fc, (0, (i * ctx + rank) * unit_rows), (shard_rows, unit_rows)
            )
            for i in range(shards)
        ],
        axis=1,
    )
    proj_block = lax.dynamic_slice(w_proj, (rank * unit_rows, 0), (unit_rows, width))
    feed_block = jnp.concatenate([fc_block, proj_block])
    token_blocks = gather_ctx(own_tokens)
    grad_blocks = gather_ctx(after(own_grad, token_blocks[1]))
    attn_gather.hop()
    attn_gather.hop()
    feed_gather = Gather(feed_block)

    def my_bias(vector):
        return lax.dynamic_slice(vector, (rank * step,), (span,))[None]

    def slot_zero():
        moved = attn_gather.step(), feed_gather.step()

        def beside():
            lines = small.astype(f32)
            values = [lines[:, t, :shard_rows].reshape(-1) for t in range(VECTOR_ROWS)]
            units = lax.dynamic_index_in_dim(
                lines[:, 0, FC_START : FC_START + ctx * unit_rows].reshape(
                    shards, ctx, unit_rows
                ),
                rank,
                1,
                False,
            ).reshape(-1)
            mixed_bias = to_pairs(
                [my_bias(values[0]), jnp.zeros((1, span), f32), my_bias(values[1])]
            )
            return mixed_bias, values[2:], units

        return moved, slot(always, beside)

    (attn_moved, feed_moved), (bias_mixed, values, bias_fc) = slot(always, slot_zero)
    attn_gather.take(attn_moved)
    feed_gather.take(feed_moved)
    bias_o, bias_p, gain_one, shift_one, gain_two, shift_two = values
    qkv_weights, out_columns = attn_gather.result(
        owners, ((0, mixed_width, 0, shard_rows), (mixed_width, span, 0, shard_rows))
    )
    qkv_weights = qkv_weights.reshape(width, mixed_width)

    normed_all, mixed = norm_mixed(
        [after(token_blocks[0], grad_blocks[3])] + token_blocks[1:],
        gain_one,
        shift_one,
        qkv_weights,
        bias_mixed,
    )
    attended_mine, mass = attend(table, mixed, feed_gather.arrived())
    feed_gather.hop()
    out_blocks = gather_ctx(out_columns.reshape(width, span))
    out_weights = join_windows(peer_table, out_blocks, width)
    pieces = exchange_far(
        *exchange_near(*halves(after(row_major(attended_mine[:, :span]), out_blocks[1])))
    )
    middle, normed_two, attended = attn_out(
        peer_table,
        pieces,
        out_weights,
        after(own_tokens, *feed_gather.arrived()),
        bias_o,
        gain_two,
        shift_two,
    )
    feed_gather.hop()

    normed_far = ctx_swap(normed_two, 2)
    normed_blocks = [
        normed_two,
        normed_far,
        ctx_swap(normed_two, 1),
    ]
    feed_gather.hop()
    normed_blocks.append(ctx_swap(after(normed_far, *feed_gather.arrived()), 1))
    grad_all = row_major(jnp.concatenate([after(grad_blocks[0], normed_two)] + grad_blocks[1:]))
    fc_weights, proj_weights = feed_gather.result(
        owners, ((0, width, 0, shard_rows), (0, width, shard_rows, unit_rows))
    )
    fc_weights = fc_weights.reshape(width, -1)
    proj_weights = proj_weights.reshape(-1, width)
    activated, slope, normed_two_all = feed_up(
        [after(normed_blocks[0], grad_all)] + normed_blocks[1:], fc_weights, bias_fc
    )

    grad_proj = row_major(outer_sum(activated, grad_all).astype(bf16))
    proj_blocks = grad_proj.reshape(shards, unit_rows, width)

    def slot_one():
        moved = ring_step(proj_blocks, owners, 4)
        return moved, feed_back(grad_blocks, proj_weights, slope, ())

    proj_moved, (before_low, grad_bias_fc) = slot(always, slot_one)

    def slot_two():
        moved = ring_step(proj_blocks, owners, 3, proj_moved)

        def beside():
            keep, give = plain_back(before_low, fc_weights, "feed_back_two")
            return keep, ctx_swap(give, 1)

        return moved, slot(always, beside)

    proj_moved, (keep_two, got_two) = slot(always, slot_two)

    def slot_three():
        moved = ring_step(proj_blocks, owners, 2, proj_moved)

        def beside():
            kept, onward = pair_add(keep_two, got_two)
            grad_fc = row_major(outer_sum(normed_two_all, before_low).astype(bf16))
            branch = row_major(product(activated, proj_weights).astype(bf16))
            return kept, ctx_swap(onward, 2), grad_fc, halves(branch)

        return moved, slot(always, beside)

    proj_moved, (kept_two, far_two, grad_fc, branch_halves) = slot(always, slot_three)
    fc_blocks = grad_fc.reshape(shards, shard_rows, shards * unit_rows)

    def slot_four():
        moved = packed_step(proj_blocks, fc_blocks, owners, proj_moved)

        def beside():
            grad_middle, low, keep, give, sums = norm_two_back(
                peer_table, kept_two, far_two, middle, own_grad, gain_two, out_weights, ()
            )
            near = exchange_near(keep.reshape(-1, span), give.reshape(-1, span))
            out_pair = out_weight_grad(peer_table, attended, low, ())
            return grad_middle, low, sums, exchange_far(*near), out_pair

        return moved, slot(always, beside)

    proj_moved, (grad_middle, middle_low, sums_two, heads, out_pair) = slot(
        always, slot_four
    )
    out_keep, out_give = [value.reshape(-1, span) for value in out_pair]

    def slot_five():
        moved = ring_step(fc_blocks, owners, 3, proj_moved)

        def beside():
            shard = ring_end(proj_blocks, owners, proj_moved)
            far, near, got = ctx_swap(shard, 2), ctx_swap(shard, 1), ctx_swap(out_give, 1)
            return [shard, far, near], got, attend_back(table, mixed, heads, mass, ())

        return moved, slot(always, beside)

    fc_moved, (proj_pieces, got_out, grad_mixed) = slot(always, slot_five)

    def slot_six():
        moved = ring_step(fc_blocks, owners, 2, fc_moved)

        def beside():
            last = ctx_swap(proj_pieces[1], 1)
            kept, first, second = pair_split(out_keep, got_out)
            far = ctx_swap(first, 2)
            grad_qkv = row_major(outer_sum(normed_all, grad_mixed).astype(bf16))
            return last, kept, second, far, grad_qkv

        return moved, slot(always, beside)

    fc_moved, (proj_last, kept_out, onward_out, far_first, grad_qkv) = slot(always, slot_six)
    proj_pieces = proj_pieces + [proj_last]
    qkv_blocks = grad_qkv.reshape(shards, shard_rows, mixed_width)

    def partial_table():
        bias_sums = jnp.sum(grad_mixed.astype(f32), axis=0, keepdims=True)

        def all_heads(part):
            mine = jnp.concatenate(from_pairs(bias_sums, part, True), axis=1)
            return lax.dynamic_update_slice(jnp.zeros((1, width), f32), mine, (0, rank * step))

        whole_bias_fc = lax.dynamic_update_slice(
            jnp.zeros((shards, ctx, unit_rows), f32),
            grad_bias_fc.reshape(shards, 1, unit_rows),
            (0, rank, 0),
        )
        return [
            value.reshape(shards, -1)
            for value in (all_heads(0), all_heads(2), *sums_two, whole_bias_fc)
        ]

    def whole_table(part, sums):
        one = [value.reshape(shards, -1) for value in sums]
        query, value, gain_two_sum, shift_two_sum, out, down, units = part
        return jnp.concatenate(
            [query, value, out, down, *one, gain_two_sum, shift_two_sum, units], axis=1
        )

    def slot_seven():
        moved = packed_step(fc_blocks, qkv_blocks, owners, fc_moved)

        def beside():
            far = ctx_swap(onward_out, 2)

            def inmost():
                keep, give = plain_back(grad_mixed, qkv_weights, "mixed_back")
                return pair_add(keep, ctx_swap(give, 1))

            return far, slot(always, inmost)

        return moved, slot(always, beside)

    fc_moved, (far_second, (kept_one, onward_one)) = slot(always, slot_seven)

    twin = [
        value.reshape(-1, shard_rows, span) for value in (kept_out, far_first, far_second)
    ]

    def slot_eight():
        qkv_next = twin_step(qkv_blocks, twin, owners, 3, fc_moved)

        def beside():
            far = ctx_swap(onward_one, 2)
            got = ctx_swap(branch_halves[1], 1)

            def inmost():
                shard = ring_end(fc_blocks, owners, fc_moved)
                return shard, partial_table(), whole_rows(peer_table, proj_pieces, ())

            return far, got, slot(always, inmost)

        return qkv_next, slot(always, beside)

    qkv_moved, (far_one, got_branch, (shard_fc, table_part, grad_w_proj)) = slot(
        always, slot_eight
    )

    def slot_nine():
        qkv_next = twin_step(qkv_blocks, twin, owners, 2, qkv_moved)

        def beside():
            far, near = ctx_swap(shard_fc, 2), ctx_swap(shard_fc, 1)

            def inmost():
                kept, onward = pair_add(branch_halves[0], got_branch)
                back, sums = norm_one_back(
                    kept_one, far_one, own_tokens, grad_middle, gain_one, ()
                )
                return kept, onward, back, whole_table(table_part, sums)

            return [shard_fc, far, near], slot(always, inmost)

        return qkv_next, slot(always, beside)

    qkv_moved, (fc_pieces, beside_nine) = slot(always, slot_nine)
    kept_branch, onward_branch, grad_tokens, small = beside_nine

    def slot_ten():
        held = halve_small(small, shards // 2)
        qkv_next = twin_step(qkv_blocks, twin, owners, 1, qkv_moved)
        far, last = ctx_swap(onward_branch, 2), ctx_swap(fc_pieces[1], 1)
        return qkv_next, held, far, last

    qkv_moved, held, far_branch, fc_last = slot(always, slot_ten)

    def slot_eleven():
        shard_qkv, out_next = twin_end(qkv_blocks, twin, owners, qkv_moved)
        far, near = ctx_swap(shard_qkv, 2), ctx_swap(shard_qkv, 1)
        next_held = halve_small(held, shards // 4)

        def beside():
            out = (middle + added(kept_branch, far_branch) + bias_p).astype(bf16)[None]
            return whole_fc(peer_table, fc_pieces + [fc_last], ()), out

        return [shard_qkv, far, near], out_next, next_held, slot(always, beside)

    qkv_pieces, out_moved, held, (grad_w_fc, tokens_out) = slot(always, slot_eleven)
    def slot_twelve():
        last = ctx_swap(qkv_pieces[1], 1)
        return last, slot(always, lambda: twin_last(twin, owners, out_moved))

    qkv_last, shard_out = slot(always, slot_twelve)

    def slot_thirteen():
        far, near = ctx_swap(shard_out, 2), ctx_swap(shard_out, 1)
        next_held = halve_small(held, shards // 8)

        def beside():
            return whole_qkv(peer_table, qkv_pieces + [qkv_last], width)

        return [shard_out, far, near], next_held, slot(always, beside)

    out_pieces, held, grad_w_qkv = slot(always, slot_thirteen)
    held = finish_small(held, shards // 16)
    out_last = ctx_swap(out_pieces[1], 1)
    summed = held[0] + ctx_swap(held[0], 1)
    summed = summed + ctx_swap(summed, 2)
    whole_attn_out = whole_out(peer_table, out_pieces + [out_last], width)
    shares = [summed[t * shard_rows : (t + 1) * shard_rows] for t in range(8)]
    share_fc = summed[8 * shard_rows :]
    grad_tokens = grad_tokens[None]

    return (
        tokens_out,
        grad_tokens,
        grad_w_qkv,
        whole_attn_out,
        shares[0],
        shares[1],
        shares[2],
        grad_w_fc,
        grad_w_proj,
        share_fc,
        shares[3],
        shares[4],
        shares[5],
        shares[6],
        shares[7],
    )


def solution(mesh):
    placed = (
        P("fsdp", "ctx", None),
        P(),
        P("fsdp", "ctx", None),
        P("fsdp", None),
        P("fsdp", None),
        P("fsdp"),
        P("fsdp"),
        P("fsdp"),
        P("fsdp", None),
        P("fsdp", None),
        P("fsdp"),
        P("fsdp"),
        P("fsdp"),
        P("fsdp"),
        P("fsdp"),
        P("fsdp"),
    )
    return jax.shard_map(
        per_device,
        mesh=mesh,
        in_specs=placed,
        out_specs=(
            P("fsdp", "ctx", None),
            P("fsdp", "ctx", None),
            P("fsdp", None),
            P("fsdp", None),
            P("fsdp"),
            P("fsdp"),
            P("fsdp"),
            P("fsdp", None),
            P("fsdp", None),
            P("fsdp"),
            P("fsdp"),
            P("fsdp"),
            P("fsdp"),
            P("fsdp"),
            P("fsdp"),
        ),
        check_vma=False,
    )
```
